32 devices in a mesh: groups: 2 (over y), seq: 8 (over z, x), section: 2 (over core).
Axes of the slice: x: 2, y: 2, z: 4, core: 2. Of those that a mesh axis runs over, the one named last changes fastest.
Arguments:
- skip_in: bfloat16 [2, 1024, 1536], P('groups', 'seq'), parts along dimension 0, may hold values from -6 to 6
- attn_gain: float32 [1536], replicated, may hold values from 0.25 to 1.75
- query_weight: bfloat16 [1536, 1024], P(None, 'section'), may hold values from -0.625 to 0.625
- kv_weight: bfloat16 [1536, 256], replicated, may hold values from -0.15625 to 0.15625
- pair_bias: float32 [2, 8, 32, 32], P('groups', 'section', 'seq'), parts along dimension 0, may hold values from -12 to 400
- out_weight: bfloat16 [1024, 1536], P('section'), may hold values from -0.1875 to 0.1875
- dec_gain: float32 [1536], replicated, may hold values from 0.25 to 1.75
- dec_weight: bfloat16 [5, 1536, 768], P(None, 'seq', 'section'), may hold values from -0.0625 to 0.0625
- dec_bias: float32 [768], P('section'), may hold values from -3 to 3
Outputs:
- decoded: bfloat16 [2, 1024, 768], P('groups', 'seq', 'section'), parts along dimension 0
The draws below stay inside these ranges and needn't reach their ends.
There are 2 independent parts, one for each index of `groups`. The reference program is written for one: setup_inputs(seed, part) draws one part's arguments, and reference() takes and returns one part's arrays. A program takes and returns all parts, laid end to end along the dimension named above; an argument that names none is the same for every part. Nothing has to cross between parts.
All inputs are finite; a program needn't handle non-finite values.
Results may differ from the reference program's by a relative error of at most 0.0095.
Values may be sent and summed in bfloat16 or wider, within the bound.
No kernel may reach another device: no remote copies, remote signals or barrier semaphores. Data moves between devices by JAX's collectives and lax.ppermute only.
A program may use at most 64 MiB of HBM per device.

```python
import jax
import jax.numpy as jnp
from jax import lax

D = 1536
OUT = 768
HEADS = 8
HEAD = 128
KW = 5
PAIR = 16
SEQS = 1
SEQ_LEN = 1024
COARSE_LEN = 512


def draw_pair_bias(key, part):
    base_key = jax.random.fold_in(key, 11)
    sub_keys = jax.random.split(base_key, 1)
    cells = COARSE_LEN // PAIR
    shape = (SEQS, HEADS, cells, cells)
    return jnp.clip(2.0 * jax.random.normal(sub_keys[0], shape, jnp.float32), -12.0, 12.0)


def shard_levels(rng, shape, cuts, low, top_value):
    level, own = 1.0, jax.random.fold_in(rng, 6)
    for position, parts in cuts:
        heights = jnp.exp(jax.random.uniform(jax.random.fold_in(own, position), (parts,), jnp.float32, low / len(cuts), top_value / len(cuts)))
        level = level * jnp.repeat(heights, shape[position] // parts).reshape([-1 if axis == position else 1 for axis in range(len(shape))])
    return level


def noise(key, shape, deviation, limit, cuts=(), kind=jnp.bfloat16):
    array = jax.random.normal(key, shape, jnp.float32) * deviation
    if len(cuts) > 0:
        array = shard_levels(key, shape, cuts, -0.22, 0.18) * array
    return jnp.clip(array, min=-limit, max=limit).astype(kind)


def setup_inputs(seed: int = 0, part: int = 0) -> dict:
    key_of = jax.random.split(jax.random.key(seed), 10)
    part_keys = jax.random.split(jax.random.fold_in(key_of[9], part), 10)
    skip_in = noise(part_keys[0], (SEQS, SEQ_LEN, D), 1.0, 6.0, ((1, 8),))
    attn_gain = jnp.clip(1.0 + 0.15 * jax.random.normal(key_of[1], (D,), jnp.float32), 0.25, 1.75)
    query_weight = noise(key_of[2], (D, HEADS * HEAD), (D // 16) ** -0.5, 0.625, ((1, 2),))
    kv_weight = noise(key_of[3], (D, 2 * HEAD), D ** -0.5, 0.15625)
    pair_bias = draw_pair_bias(jax.random.fold_in(jax.random.fold_in(key_of[9], part), 71), part)
    out_weight = noise(key_of[5], (HEADS * HEAD, D), (HEADS * HEAD) ** -0.5, 0.1875, ((0, 2),))
    dec_gain = jnp.clip(1.0 + 0.15 * jax.random.normal(key_of[6], (D,), jnp.float32), 0.25, 1.75)
    dec_weight = noise(key_of[7], (KW, D, OUT), (KW * D) ** -0.5, 0.0625, ((1, 8), (2, 2)))
    dec_bias = noise(key_of[8], (OUT,), 0.5, 3.0, ((0, 2),), jnp.float32)
    return dict(skip_in=skip_in, attn_gain=attn_gain, query_weight=query_weight, kv_weight=kv_weight, pair_bias=pair_bias, out_weight=out_weight, dec_gain=dec_gain, dec_weight=dec_weight, dec_bias=dec_bias)


def norm_scale(values_in, gain):
    wide = values_in.astype(jnp.float32)
    return wide * lax.rsqrt(lax.optimization_barrier(jnp.mean(wide * wide, axis=-1, keepdims=True)) + 1e-06) * gain

def reference(skip_in, attn_gain, query_weight, kv_weight, pair_bias, out_weight, dec_gain, dec_weight, dec_bias):
    seq_count, seq_length, channels = skip_in.shape
    half_length = seq_length // 2
    pooled = lax.optimization_barrier(jnp.max(skip_in.reshape(seq_count, half_length, 2, channels), axis=2))
    normed = norm_scale(pooled, attn_gain).astype(jnp.bfloat16)
    flattened = normed.reshape(seq_count * half_length, channels)
    query_rows = jnp.dot(flattened, query_weight, preferred_element_type=jnp.float32).astype(jnp.bfloat16)
    query_rows = query_rows.reshape(seq_count, half_length, HEADS, HEAD)
    key_values = jnp.dot(flattened, kv_weight, preferred_element_type=jnp.float32).astype(jnp.bfloat16)
    key_values = key_values.reshape(seq_count, half_length, 2 * HEAD)
    query_block = min(512, half_length)
    block_count = half_length // query_block
    logit_scale = 1.0 / jnp.sqrt(jnp.float32(HEAD))

    def attend_block(flat_index):
        seq_index = flat_index // block_count
        block_index = flat_index % block_count
        seq_queries = lax.dynamic_index_in_dim(query_rows, seq_index, 0, keepdims=False)
        block_queries = lax.dynamic_slice_in_dim(seq_queries, (block_index * query_block).astype(jnp.int32), query_block, 0)
        seq_kv = lax.dynamic_index_in_dim(key_values, seq_index, 0, keepdims=False)
        key_rows = seq_kv[:, :HEAD].astype(jnp.float32)
        value_matrix = seq_kv[:, HEAD:].astype(jnp.float32)
        seq_bias = lax.dynamic_index_in_dim(pair_bias, seq_index, 0, keepdims=False)
        bias_rows = lax.dynamic_slice_in_dim(seq_bias, (block_index * (query_block // PAIR)).astype(jnp.int32), query_block // PAIR, 1)
        full_bias = jnp.repeat(jnp.repeat(bias_rows, PAIR, axis=1), PAIR, axis=2)
        scores = jnp.einsum('qhd,kd->hqk', block_queries.astype(jnp.float32), key_rows) * logit_scale + full_bias
        row_max = lax.optimization_barrier(jnp.max(scores, axis=-1, keepdims=True))
        exponent_scores = jnp.exp(scores - row_max)
        totals = lax.optimization_barrier(jnp.sum(exponent_scores, axis=-1))
        rounded = lax.optimization_barrier(exponent_scores.astype(jnp.bfloat16)).astype(jnp.float32)
        context = jnp.einsum('hqk,kd->qhd', rounded, value_matrix) / jnp.transpose(totals)[:, :, None]
        return context.astype(jnp.bfloat16).reshape(query_block, HEADS * HEAD)
    contexts = lax.map(attend_block, jnp.arange(seq_count * block_count, dtype=jnp.int32))
    contexts = contexts.reshape(seq_count * half_length, HEADS * HEAD)
    projected = jnp.dot(contexts, out_weight, preferred_element_type=jnp.float32).reshape(seq_count, half_length, channels)
    attended = (pooled.astype(jnp.float32) + projected).astype(jnp.bfloat16)
    joined = (jnp.repeat(attended, 2, axis=1).astype(jnp.float32) + skip_in.astype(jnp.float32)).astype(jnp.bfloat16)
    activated = jax.nn.gelu(norm_scale(joined, dec_gain)).astype(jnp.bfloat16)
    margin = KW // 2
    padded = jnp.pad(activated, ((0, 0), (margin, margin), (0, 0)))
    convolved = jnp.zeros((seq_count * seq_length, OUT), jnp.float32)
    for tap_index in range(KW):
        window = padded[:, tap_index:tap_index + seq_length].reshape(seq_count * seq_length, channels)
        convolved = convolved + jnp.dot(window, dec_weight[tap_index], preferred_element_type=jnp.float32)
    convolved = convolved.reshape(seq_count, seq_length, OUT)
    decoded = convolved + dec_bias + joined[:, :, :OUT].astype(jnp.float32)
    return decoded.astype(jnp.bfloat16)
```

```python
import math

import jax
import jax.numpy as jnp
from jax import lax
from jax.experimental import pallas as pl
from jax.experimental.pallas import tpu as pltpu
from jax.sharding import PartitionSpec as P

HEAD = 128
KW = 5
PAIR = 16


def extended(block, sides, width):
    for axis, dim in sides:
        count = lax.axis_size(axis)
        forward = [(i, i + 1) for i in range(count - 1)]
        backward = [(target, source) for source, target in forward]
        low = lax.ppermute(
            lax.slice_in_dim(block, block.shape[dim] - width, None, axis=dim), axis, forward
        )
        high = lax.ppermute(lax.slice_in_dim(block, 0, width, axis=dim), axis, backward)
        block = jnp.concatenate([low, block, high], axis=dim)
    return block


def norm_scale(values_in, gain):
    wide = values_in.astype(jnp.float32)
    return wide * lax.rsqrt(jnp.mean(wide * wide, axis=-1, keepdims=True) + 1e-06) * gain


def body(
    skip_in,
    attn_gain,
    query_weight,
    kv_weight,
    pair_bias,
    out_weight,
    dec_gain,
    dec_weight,
    dec_bias,
):
    seq_count, local_rows, channels = skip_in.shape
    half_rows = local_rows // 2
    local_heads = query_weight.shape[1] // HEAD
    logit_scale = 1.0 / math.sqrt(HEAD)
    pooled = jnp.max(skip_in.reshape(seq_count, half_rows, 2, channels), axis=2)
    normed = norm_scale(pooled, attn_gain).astype(jnp.bfloat16)
    flattened = normed.reshape(seq_count * half_rows, channels)
    query_rows = jnp.dot(flattened, query_weight, preferred_element_type=jnp.float32).astype(
        jnp.bfloat16
    )
    query_rows = query_rows.reshape(seq_count, half_rows, local_heads, HEAD)
    row_bias = jnp.repeat(pair_bias, PAIR, axis=2)
    row_bias = jnp.pad(row_bias, ((0, 0), (0, 0), (0, 0), (0, 2)))
    quarter = half_rows // 2
    own_rows = lax.dynamic_slice_in_dim(normed, lax.axis_index("section") * quarter, quarter, 1)
    key_values = jnp.dot(
        own_rows.reshape(seq_count * quarter, channels),
        kv_weight,
        preferred_element_type=jnp.float32,
    )
    key_values = key_values.astype(jnp.bfloat16).reshape(seq_count, quarter, 2 * HEAD)
    piece = lax.all_gather(key_values, ("seq", "section"), axis=1, tiled=True)
    start = jnp.int32(0)
    running_max = jnp.full((seq_count, local_heads, half_rows), -1e30, jnp.float32)
    running_sum = jnp.zeros((seq_count, local_heads, half_rows), jnp.float32)
    weighted = jnp.zeros((seq_count, local_heads, half_rows, HEAD), jnp.float32)
    piece_rows = piece.shape[1]
    block_size = min(piece_rows, 2048)
    for offset in range(0, piece_rows, block_size):
        piece_len = min(block_size, piece_rows - offset)
        sub_piece = piece[:, offset : offset + piece_len]
        key_portion = sub_piece[:, :, :HEAD]
        value_part = sub_piece[:, :, HEAD:]
        first_row = start + offset
        blocks = lax.dynamic_slice_in_dim(row_bias, first_row // PAIR, piece_len // PAIR + 2, 3)
        spread = jnp.repeat(blocks, PAIR, axis=3)
        key_bias = lax.dynamic_slice_in_dim(spread, first_row % PAIR, piece_len, 3)
        scores = (
            jnp.einsum(
                "wtzj,wgj->wztg", query_rows, key_portion, preferred_element_type=jnp.float32
            )
            * logit_scale
            + key_bias
        )
        new_max = jnp.maximum(running_max, jnp.max(scores, axis=-1))
        rescale = jnp.exp(running_max - new_max)
        exponent_scores = jnp.exp(scores - new_max[..., None])
        running_sum = running_sum * rescale + jnp.sum(exponent_scores, axis=-1)
        weighted = weighted * rescale[..., None] + jnp.einsum(
            "umrl,ult->umrt",
            exponent_scores.astype(jnp.bfloat16),
            value_part,
            preferred_element_type=jnp.float32,
        )
        running_max = new_max
    folded = (running_max, running_sum, weighted)
    running_max, running_sum, weighted = folded
    context = (weighted / running_sum[..., None]).astype(jnp.bfloat16)
    context = jnp.transpose(context, (0, 2, 1, 3)).reshape(
        seq_count * half_rows, local_heads * HEAD
    )
    partial_value = jnp.dot(context, out_weight, preferred_element_type=jnp.float32).reshape(
        seq_count, half_rows, channels
    )
    summed = lax.psum(partial_value.astype(jnp.bfloat16), "section").astype(jnp.float32)
    attended = (pooled.astype(jnp.float32) + summed).astype(jnp.bfloat16)
    joined = (
        jnp.repeat(attended, 2, axis=1).astype(jnp.float32) + skip_in.astype(jnp.float32)
    ).astype(jnp.bfloat16)
    activated = jax.nn.gelu(norm_scale(joined, dec_gain)).astype(jnp.bfloat16)
    padded = extended(activated, (("seq", 1),), KW // 2)
    out_half = dec_weight.shape[2]
    piece = lax.all_gather(dec_weight, "seq", axis=1, tiled=True)
    piece_rows = piece.shape[1]
    stacked = jnp.concatenate(
        [padded[:, tap_index : tap_index + local_rows] for tap_index in range(KW)], axis=2
    )
    stacked = stacked.reshape(seq_count * local_rows, KW * piece_rows)
    convolved = jnp.dot(
        stacked, piece.reshape(KW * piece_rows, out_half), preferred_element_type=jnp.float32
    )
    residual = lax.dynamic_slice_in_dim(joined, lax.axis_index("section") * out_half, out_half, 2)
    decoded = (
        convolved.reshape(seq_count, local_rows, out_half) + dec_bias + residual.astype(jnp.float32)
    )
    return decoded.astype(jnp.bfloat16)


ROWS = 80
MSG = 112
LIMIT = 56 * 1024 * 1024


def exchange(values_in, axis, mask):
    count = lax.axis_size(axis)
    return lax.ppermute(values_in, axis, [(i, i ^ mask) for i in range(count)])


def call(kernel, outs, args, scratch=(), spaces=None):
    vmem = pl.BlockSpec(memory_space=pltpu.VMEM)
    specs = [vmem] * len(args) if spaces is None else spaces
    return pl.pallas_call(
        kernel,
        out_shape=[jax.ShapeDtypeStruct(shape, kind) for shape, kind in outs],
        in_specs=specs,
        out_specs=[vmem] * len(outs),
        scratch_shapes=list(scratch),
        compiler_params=pltpu.CompilerParams(vmem_limit_bytes=LIMIT),
    )(*args)


def split_three(wide):
    high = wide.astype(jnp.bfloat16)
    rest = wide - high.astype(jnp.float32)
    middle = rest.astype(jnp.bfloat16)
    low = (rest - middle.astype(jnp.float32)).astype(jnp.bfloat16)
    return high, middle, low


def normalize(wide, gain):
    return wide * lax.rsqrt(jnp.mean(wide * wide, axis=-1, keepdims=True) + 1e-06) * gain


def gelu(wide):
    inner = math.sqrt(2.0 / math.pi) * (wide + 0.044715 * (wide * wide * wide))
    return 0.5 * wide * (1.0 + jnp.tanh(inner))


def spread_columns(wide, values_in):
    for k in range(wide.shape[0]):
        wide[k] = values_in[:, 128 * k : 128 * k + 128].astype(jnp.float32)


def take_rows(wide, start, size):
    return jnp.concatenate(
        [wide[k, pl.ds(start, size, stride=2), :] for k in range(wide.shape[0])], axis=1
    )


def put_rows(wide, start, values_in):
    for k in range(wide.shape[0]):
        wide[k, pl.ds(start, values_in.shape[0], stride=2), :] = values_in[:, 128 * k : 128 * k + 128]


def pool_kernel(skip_ref, gain_ref, weight_ref, bias_ref, message_ref, normed_ref, wide, lines):
    half = skip_ref.shape[0] // 2
    spread_columns(wide, skip_ref)
    pooled = jnp.maximum(take_rows(wide, 0, half), take_rows(wide, 1, half))
    normed = normalize(pooled, gain_ref[...]).astype(jnp.bfloat16)
    normed_ref[...] = normed
    lines[0:half, :] = jnp.dot(normed, weight_ref[...], preferred_element_type=jnp.float32)
    last = skip_ref.shape[0]
    for n, row in enumerate((0, 1, last - 2, last - 1)):
        for k in range(12):
            at = half + 6 * n + k // 2
            lines[at : at + 1, 128 * (k % 2) : 128 * (k % 2) + 128] = wide[k, row : row + 1, :]
    lines[88:MSG, :] = jnp.zeros((MSG - 88, 256), jnp.float32)
    for n, term in enumerate(split_three(bias_ref[...])):
        for h in range(4):
            for k, cell in enumerate((0, 3)):
                at = 88 + 8 * n + 2 * h + k
                lines[at : at + 1, 0:32] = term[4 * h + cell : 4 * h + cell + 1, :].astype(
                    jnp.float32
                )
    message_ref[...] = lines[...].astype(jnp.bfloat16)


def reverse_bits(value):
    return (value & 1) * 4 + (value & 2) + (value >> 2)


def attention_kernel(
    query_ref, message_ref, query_weight_ref, gain_ref, bias_ref, out_weight_ref, terms_ref, edge_ref
):
    me = lax.axis_index("seq")
    count = lax.axis_size("seq")
    low_slot = reverse_bits(me ^ jnp.maximum(me - 1, 0))
    high_slot = reverse_bits(me ^ jnp.minimum(me + 1, count - 1))
    low = message_ref[low_slot].astype(jnp.float32)
    high = message_ref[high_slot].astype(jnp.float32)

    def line(block, row):
        start = 64 + 6 * row
        return jnp.concatenate([block[start + k : start + k + 1, :] for k in range(6)], axis=1)

    edges = jnp.concatenate(
        [line(low, 2), line(low, 3), line(high, 0), line(high, 1)], axis=0
    )
    edge_ref[0:4, :] = edges
    edge_ref[4:8, :] = jnp.zeros_like(edges)
    pooled = jnp.concatenate(
        [
            jnp.maximum(edges[0:1], edges[1:2]),
            jnp.maximum(edges[2:3], edges[3:4]),
            jnp.zeros((14, edges.shape[1]), jnp.float32),
        ],
        axis=0,
    )
    normed = normalize(pooled, gain_ref[...]).astype(jnp.bfloat16)
    halo_query = jnp.dot(normed, query_weight_ref[...], preferred_element_type=jnp.float32)
    queries = jnp.concatenate([query_ref[...], halo_query.astype(jnp.bfloat16)], axis=0)
    keys = jnp.concatenate([message_ref[k, 0:64, 0:HEAD] for k in range(8)], axis=0)
    values = jnp.concatenate([message_ref[k, 0:64, HEAD : 2 * HEAD] for k in range(8)], axis=0)
    cell = lax.broadcasted_iota(jnp.int32, (32, 512), 0)
    column = lax.broadcasted_iota(jnp.int32, (32, 512), 1)
    wanted = 4 * (reverse_bits(column >> 6) ^ me) + ((column & 63) >> 4)
    spread = jnp.where(cell == wanted, 1.0, 0.0).astype(jnp.bfloat16)
    bias = jnp.zeros((32, 512), jnp.float32)
    for n, term in enumerate(split_three(bias_ref[...])):
        at = 88 + 8 * n
        table = jnp.concatenate(
            [term, low[at : at + 8, 0:32].astype(jnp.bfloat16), high[at : at + 8, 0:32].astype(jnp.bfloat16)],
            axis=0,
        )
        bias = bias + jnp.dot(table, spread, preferred_element_type=jnp.float32)
    first = lax.broadcasted_iota(jnp.int32, (16, 512), 0) == 0
    parts = []
    for h in range(4):
        scores = lax.dot_general(
            queries[:, h * HEAD : (h + 1) * HEAD],
            keys,
            (((1,), (1,)), ((), ())),
            preferred_element_type=jnp.float32,
        )
        rows = [jnp.broadcast_to(bias[4 * h + r : 4 * h + r + 1, :], (16, 512)) for r in range(4)]
        rows.append(
            jnp.where(first, bias[17 + 2 * h : 18 + 2 * h, :], bias[24 + 2 * h : 25 + 2 * h, :])
        )
        scores = scores * (1.0 / math.sqrt(HEAD)) + jnp.concatenate(rows, axis=0)
        exps = jnp.exp(scores - jnp.max(scores, axis=-1, keepdims=True))
        totals = jnp.sum(exps, axis=-1, keepdims=True)
        mixed = jnp.dot(exps.astype(jnp.bfloat16), values, preferred_element_type=jnp.float32)
        parts.append((mixed / totals).astype(jnp.bfloat16))
    context = jnp.concatenate(parts, axis=1)
    terms_ref[...] = jnp.dot(
        context, out_weight_ref[...], preferred_element_type=jnp.float32
    ).astype(jnp.bfloat16)


def activate_kernel(
    skip_ref, edge_ref, own_ref, other_ref, gain_ref, dec_bias_ref, keep_ref, send_ref, base_ref, wide, active
):
    me = lax.axis_index("seq")
    section = lax.axis_index("section")
    upper = me >> 2
    gain = gain_ref[...]
    spread_columns(wide, skip_ref)
    even = take_rows(wide, 0, 64)
    odd = take_rows(wide, 1, 64)
    projected = own_ref[...].astype(jnp.float32) + other_ref[...].astype(jnp.float32)

    def rounded(values_in):
        return values_in.astype(jnp.bfloat16).astype(jnp.float32)

    attended = rounded(jnp.maximum(even, odd) + projected[0:64])
    even = rounded(attended + even)
    odd = rounded(attended + odd)
    put_rows(wide, 0, even)
    put_rows(wide, 1, odd)
    put_rows(active, 8, gelu(normalize(even, gain)))
    put_rows(active, 9, gelu(normalize(odd, gain)))
    edges = edge_ref[0:4, :]
    low = rounded(jnp.maximum(edges[0:1], edges[1:2]) + projected[64:65])
    high = rounded(jnp.maximum(edges[2:3], edges[3:4]) + projected[65:66])
    joined = rounded(edges + jnp.concatenate([low, low, high, high], axis=0))
    halo = gelu(normalize(joined, gain))
    above = jnp.where(me > 0, halo[0:2], 0.0)
    below = jnp.where(me < lax.axis_size("seq") - 1, halo[2:4], 0.0)
    zeros = jnp.zeros((6, 128), jnp.float32)
    for k in range(12):
        columns = slice(128 * k, 128 * k + 128)
        active[k, 0:8, :] = jnp.concatenate([zeros, above[:, columns]], axis=0)
        active[k, 136:144, :] = jnp.concatenate([below[:, columns], zeros], axis=0)
    for k in range(6):
        keep_ref[:, 128 * k : 128 * k + 128] = active[upper * 6 + k].astype(jnp.bfloat16)
    for k in range(3):
        columns = slice(128 * k, 128 * k + 128)
        send_ref[:, columns] = active[(1 - upper) * 6 + section * 3 + k].astype(jnp.bfloat16)
        base_ref[:, columns] = wide[section * 3 + k] + dec_bias_ref[:, columns]


def load_weight(own_ref, side_ref, next_ref, far_top_ref, far_bottom_ref, weight, semaphores):
    slot = lax.axis_index("seq") & 3
    pieces = (
        (own_ref, slot * 192, 192),
        (side_ref, (slot ^ 1) * 192, 192),
        (next_ref, (slot ^ 2) * 192, 192),
        (far_top_ref, (slot ^ 3) * 192, 96),
        (far_bottom_ref, (slot ^ 3) * 192 + 96, 96),
    )
    copies = [
        pltpu.make_async_copy(
            ref, weight.at[:, pl.ds(pl.multiple_of(start, 32), size), :], semaphores.at[n]
        )
        for n, (ref, start, size) in enumerate(pieces)
    ]
    for copy in copies:
        copy.start()
    for copy in copies:
        copy.wait()


def shifted_sum(products):
    total = products[0][6:134]
    for tap in range(1, KW):
        total = total + products[tap][6 + tap : 134 + tap]
    return total


def own_kernel(active_ref, base_ref, w0, w1, w2, w3, w4, out_ref, weight, semaphores):
    load_weight(w0, w1, w2, w3, w4, weight, semaphores)
    active = active_ref[...]
    out_ref[...] = base_ref[...] + shifted_sum(
        [jnp.dot(active, weight[t], preferred_element_type=jnp.float32) for t in range(KW)]
    )


def partner_kernel(first_ref, second_ref, w0, w1, w2, w3, w4, out_ref, weight, semaphores):
    load_weight(w0, w1, w2, w3, w4, weight, semaphores)
    section = lax.axis_index("section")
    first, second = first_ref[...], second_ref[...]
    near = pl.ds(pl.multiple_of(section * 384, 128), 384)
    far = pl.ds(pl.multiple_of((1 - section) * 384, 128), 384)
    out_ref[...] = shifted_sum(
        [
            jnp.dot(first, weight[t, near, :], preferred_element_type=jnp.float32)
            + jnp.dot(second, weight[t, far, :], preferred_element_type=jnp.float32)
            for t in range(KW)
        ]
    ).astype(jnp.bfloat16)


def split_body(
    skip_in, attn_gain, query_weight, kv_weight, pair_bias, out_weight, dec_gain, dec_weight, dec_bias
):
    bf16, f32 = jnp.bfloat16, jnp.float32
    skip = skip_in[0]
    rows, channels = skip.shape
    gain = attn_gain.reshape(1, channels)
    bias = pair_bias.reshape(16, 32)
    taps, depth, width = dec_weight.shape
    side = exchange(dec_weight, "seq", 1)
    after = exchange(dec_weight, "seq", 2)
    far_top = exchange(after[:, : depth // 2], "seq", 1)
    far_bottom = exchange(side[:, depth // 2 :], "seq", 2)
    message, normed = call(
        pool_kernel,
        [((MSG, 256), bf16), ((rows // 2, channels), bf16)],
        [skip, gain, kv_weight, bias],
        [pltpu.VMEM((channels // 128, rows, 128), f32), pltpu.VMEM((MSG, 256), f32)],
    )
    messages = message[None]
    for mask in (4, 2, 1):
        messages = jnp.concatenate([messages, exchange(messages, "seq", mask)], axis=0)
    queries = jnp.dot(normed, query_weight, preferred_element_type=f32).astype(bf16)
    terms, edges = call(
        attention_kernel,
        [((ROWS, channels), bf16), ((8, channels), f32)],
        [queries, messages, query_weight, gain, bias, out_weight],
    )
    other = exchange(terms, "section", 1)
    keep, send, base = call(
        activate_kernel,
        [((rows + 16, channels // 2), bf16), ((rows + 16, channels // 4), bf16), ((rows, width), f32)],
        [skip, edges, terms, other, dec_gain.reshape(1, channels), dec_bias.reshape(1, width)],
        [pltpu.VMEM((channels // 128, rows + extra, 128), f32) for extra in (0, 16)],
    )
    first = exchange(send, "seq", 4)
    second = exchange(first, "section", 1)
    weights = [dec_weight, side, after, far_top, far_bottom]
    vmem = pl.BlockSpec(memory_space=pltpu.VMEM)
    spaces = [vmem, vmem] + [pl.BlockSpec(memory_space=pl.ANY)] * 5
    scratch = [pltpu.VMEM((taps, 4 * depth, width), bf16), pltpu.SemaphoreType.DMA((5,))]
    (own,) = call(own_kernel, [((rows, width), f32)], [keep, base] + weights, scratch, spaces)
    (partial,) = call(
        partner_kernel, [((rows, width), bf16)], [first, second] + weights, scratch, spaces
    )
    decoded = own + exchange(partial, "seq", 4).astype(f32)
    return decoded.astype(bf16)[None]


def solution(mesh):
    return jax.shard_map(
        split_body if mesh.shape["seq"] == 8 else body,
        mesh=mesh,
        in_specs=(
            P("groups", "seq", None),
            P(),
            P(None, "section"),
            P(),
            P("groups", "section", "seq", None),
            P("section", None),
            P(),
            P(None, "seq", "section"),
            P("section"),
        ),
        out_specs=P("groups", "seq", "section"),
        check_vma=False,
    )
```

```python
import math

import jax
import jax.numpy as jnp
from jax import lax
from jax.experimental import pallas as pl
from jax.experimental.pallas import tpu as pltpu
from jax.sharding import PartitionSpec as P

HEAD = 128
KW = 5
PAIR = 16


def extended(block, sides, width):
    for axis, dim in sides:
        count = lax.axis_size(axis)
        forward = [(i, i + 1) for i in range(count - 1)]
        backward = [(target, source) for source, target in forward]
        low = lax.ppermute(
            lax.slice_in_dim(block, block.shape[dim] - width, None, axis=dim), axis, forward
        )
        high = lax.ppermute(lax.slice_in_dim(block, 0, width, axis=dim), axis, backward)
        block = jnp.concatenate([low, block, high], axis=dim)
    return block


def norm_scale(values_in, gain):
    wide = values_in.astype(jnp.float32)
    return wide * lax.rsqrt(jnp.mean(wide * wide, axis=-1, keepdims=True) + 1e-06) * gain


def body(
    skip_in,
    attn_gain,
    query_weight,
    kv_weight,
    pair_bias,
    out_weight,
    dec_gain,
    dec_weight,
    dec_bias,
):
    seq_count, local_rows, channels = skip_in.shape
    half_rows = local_rows // 2
    local_heads = query_weight.shape[1] // HEAD
    logit_scale = 1.0 / math.sqrt(HEAD)
    pooled = jnp.max(skip_in.reshape(seq_count, half_rows, 2, channels), axis=2)
    normed = norm_scale(pooled, attn_gain).astype(jnp.bfloat16)
    flattened = normed.reshape(seq_count * half_rows, channels)
    query_rows = jnp.dot(flattened, query_weight, preferred_element_type=jnp.float32).astype(
        jnp.bfloat16
    )
    query_rows = query_rows.reshape(seq_count, half_rows, local_heads, HEAD)
    row_bias = jnp.repeat(pair_bias, PAIR, axis=2)
    row_bias = jnp.pad(row_bias, ((0, 0), (0, 0), (0, 0), (0, 2)))
    quarter = half_rows // 2
    own_rows = lax.dynamic_slice_in_dim(normed, lax.axis_index("section") * quarter, quarter, 1)
    key_values = jnp.dot(
        own_rows.reshape(seq_count * quarter, channels),
        kv_weight,
        preferred_element_type=jnp.float32,
    )
    key_values = key_values.astype(jnp.bfloat16).reshape(seq_count, quarter, 2 * HEAD)
    piece = lax.all_gather(key_values, ("seq", "section"), axis=1, tiled=True)
    start = jnp.int32(0)
    running_max = jnp.full((seq_count, local_heads, half_rows), -1e30, jnp.float32)
    running_sum = jnp.zeros((seq_count, local_heads, half_rows), jnp.float32)
    weighted = jnp.zeros((seq_count, local_heads, half_rows, HEAD), jnp.float32)
    piece_rows = piece.shape[1]
    block_size = min(piece_rows, 2048)
    for offset in range(0, piece_rows, block_size):
        piece_len = min(block_size, piece_rows - offset)
        sub_piece = piece[:, offset : offset + piece_len]
        key_portion = sub_piece[:, :, :HEAD]
        value_part = sub_piece[:, :, HEAD:]
        first_row = start + offset
        blocks = lax.dynamic_slice_in_dim(row_bias, first_row // PAIR, piece_len // PAIR + 2, 3)
        spread = jnp.repeat(blocks, PAIR, axis=3)
        key_bias = lax.dynamic_slice_in_dim(spread, first_row % PAIR, piece_len, 3)
        scores = (
            jnp.einsum(
                "wtzj,wgj->wztg", query_rows, key_portion, preferred_element_type=jnp.float32
            )
            * logit_scale
            + key_bias
        )
        new_max = jnp.maximum(running_max, jnp.max(scores, axis=-1))
        rescale = jnp.exp(running_max - new_max)
        exponent_scores = jnp.exp(scores - new_max[..., None])
        running_sum = running_sum * rescale + jnp.sum(exponent_scores, axis=-1)
        weighted = weighted * rescale[..., None] + jnp.einsum(
            "umrl,ult->umrt",
            exponent_scores.astype(jnp.bfloat16),
            value_part,
            preferred_element_type=jnp.float32,
        )
        running_max = new_max
    folded = (running_max, running_sum, weighted)
    running_max, running_sum, weighted = folded
    context = (weighted / running_sum[..., None]).astype(jnp.bfloat16)
    context = jnp.transpose(context, (0, 2, 1, 3)).reshape(
        seq_count * half_rows, local_heads * HEAD
    )
    partial_value = jnp.dot(context, out_weight, preferred_element_type=jnp.float32).reshape(
        seq_count, half_rows, channels
    )
    summed = lax.psum(partial_value.astype(jnp.bfloat16), "section").astype(jnp.float32)
    attended = (pooled.astype(jnp.float32) + summed).astype(jnp.bfloat16)
    joined = (
        jnp.repeat(attended, 2, axis=1).astype(jnp.float32) + skip_in.astype(jnp.float32)
    ).astype(jnp.bfloat16)
    activated = jax.nn.gelu(norm_scale(joined, dec_gain)).astype(jnp.bfloat16)
    padded = extended(activated, (("seq", 1),), KW // 2)
    out_half = dec_weight.shape[2]
    piece = lax.all_gather(dec_weight, "seq", axis=1, tiled=True)
    piece_rows = piece.shape[1]
    stacked = jnp.concatenate(
        [padded[:, tap_index : tap_index + local_rows] for tap_index in range(KW)], axis=2
    )
    stacked = stacked.reshape(seq_count * local_rows, KW * piece_rows)
    convolved = jnp.dot(
        stacked, piece.reshape(KW * piece_rows, out_half), preferred_element_type=jnp.float32
    )
    residual = lax.dynamic_slice_in_dim(joined, lax.axis_index("section") * out_half, out_half, 2)
    decoded = (
        convolved.reshape(seq_count, local_rows, out_half) + dec_bias + residual.astype(jnp.float32)
    )
    return decoded.astype(jnp.bfloat16)


ROWS = 80
MSG = 112
LIMIT = 24 * 1024 * 1024


def exchange(values_in, axis, mask):
    count = lax.axis_size(axis)
    return lax.ppermute(values_in, axis, [(i, i ^ mask) for i in range(count)])


def call(kernel, outs, args, scratch=()):
    vmem = pl.BlockSpec(memory_space=pltpu.VMEM)
    return pl.pallas_call(
        kernel,
        out_shape=[jax.ShapeDtypeStruct(shape, kind) for shape, kind in outs],
        in_specs=[vmem] * len(args),
        out_specs=[vmem] * len(outs),
        scratch_shapes=list(scratch),
        compiler_params=pltpu.CompilerParams(vmem_limit_bytes=LIMIT),
    )(*args)


def split_three(wide):
    high = wide.astype(jnp.bfloat16)
    rest = wide - high.astype(jnp.float32)
    middle = rest.astype(jnp.bfloat16)
    low = (rest - middle.astype(jnp.float32)).astype(jnp.bfloat16)
    return high, middle, low


def own_bias(bias_ref):
    return jnp.concatenate([bias_ref[0, h] for h in range(4)], axis=0)


def normalize(wide, gain):
    return wide * lax.rsqrt(jnp.mean(wide * wide, axis=-1, keepdims=True) + 1e-06) * gain


def gelu(wide):
    inner = math.sqrt(2.0 / math.pi) * (wide + 0.044715 * (wide * wide * wide))
    return 0.5 * wide * (1.0 + jnp.tanh(inner))


def spread_columns(wide, values_in):
    for k in range(wide.shape[0]):
        wide[k] = values_in[:, 128 * k : 128 * k + 128].astype(jnp.float32)


def take_rows(wide, start, size):
    return jnp.concatenate(
        [wide[k, pl.ds(start, size, stride=2), :] for k in range(wide.shape[0])], axis=1
    )


def put_rows(wide, start, values_in):
    for k in range(wide.shape[0]):
        wide[k, pl.ds(start, values_in.shape[0], stride=2), :] = values_in[:, 128 * k : 128 * k + 128]


def pool_kernel(skip_ref, gain_ref, weight_ref, bias_ref, message_ref, normed_ref, wide, lines):
    half = skip_ref.shape[0] // 2
    spread_columns(wide, skip_ref)
    pooled = jnp.maximum(take_rows(wide, 0, half), take_rows(wide, 1, half))
    normed = normalize(pooled, gain_ref[...][None, :]).astype(jnp.bfloat16)
    normed_ref[...] = normed
    lines[0:half, :] = jnp.dot(normed, weight_ref[...], preferred_element_type=jnp.float32)
    last = skip_ref.shape[0]
    for n, row in enumerate((0, 1, last - 2, last - 1)):
        for k in range(12):
            at = half + 6 * n + k // 2
            lines[at : at + 1, 128 * (k % 2) : 128 * (k % 2) + 128] = wide[k, row : row + 1, :]
    lines[88:MSG, :] = jnp.zeros((MSG - 88, 256), jnp.float32)
    for n, term in enumerate(split_three(own_bias(bias_ref))):
        for h in range(4):
            for k, cell in enumerate((0, 3)):
                at = 88 + 8 * n + 2 * h + k
                lines[at : at + 1, 0:32] = term[4 * h + cell : 4 * h + cell + 1, :].astype(
                    jnp.float32
                )
    message_ref[...] = lines[...].astype(jnp.bfloat16)


def reverse_bits(value):
    return (value & 1) * 4 + (value & 2) + (value >> 2)


def attention_kernel(
    query_ref, near_ref, side_ref, query_weight_ref, gain_ref, bias_ref, out_weight_ref, terms_ref, edge_ref
):
    me = lax.axis_index("seq")
    count = lax.axis_size("seq")
    low_slot = reverse_bits(me ^ jnp.maximum(me - 1, 0))
    high_slot = reverse_bits(me ^ jnp.minimum(me + 1, count - 1))

    def block_of(slot):
        near = near_ref[slot & 3].astype(jnp.float32)
        return jnp.where(slot < 4, near, side_ref[slot & 3].astype(jnp.float32))

    low, high = block_of(low_slot), block_of(high_slot)

    def line(block, row):
        start = 64 + 6 * row
        return jnp.concatenate([block[start + k : start + k + 1, :] for k in range(6)], axis=1)

    edges = jnp.concatenate(
        [line(low, 2), line(low, 3), line(high, 0), line(high, 1)], axis=0
    )
    edge_ref[0:4, :] = edges
    edge_ref[4:8, :] = jnp.zeros_like(edges)
    pooled = jnp.concatenate(
        [
            jnp.maximum(edges[0:1], edges[1:2]),
            jnp.maximum(edges[2:3], edges[3:4]),
            jnp.zeros((14, edges.shape[1]), jnp.float32),
        ],
        axis=0,
    )
    normed = normalize(pooled, gain_ref[...][None, :]).astype(jnp.bfloat16)
    halo_query = jnp.dot(normed, query_weight_ref[...], preferred_element_type=jnp.float32)
    queries = jnp.concatenate([query_ref[...], halo_query.astype(jnp.bfloat16)], axis=0)
    pieces = [ref[k, 0:64, :] for ref in (near_ref, side_ref) for k in range(4)]
    keys = jnp.concatenate([piece[:, 0:HEAD] for piece in pieces], axis=0)
    values = jnp.concatenate([piece[:, HEAD : 2 * HEAD] for piece in pieces], axis=0)
    cell = lax.broadcasted_iota(jnp.int32, (32, 512), 0)
    column = lax.broadcasted_iota(jnp.int32, (32, 512), 1)
    wanted = 4 * (reverse_bits(column >> 6) ^ me) + ((column & 63) >> 4)
    spread = jnp.where(cell == wanted, 1.0, 0.0).astype(jnp.bfloat16)
    bias = jnp.zeros((32, 512), jnp.float32)
    for n, term in enumerate(split_three(own_bias(bias_ref))):
        at = 88 + 8 * n
        table = jnp.concatenate(
            [term, low[at : at + 8, 0:32].astype(jnp.bfloat16), high[at : at + 8, 0:32].astype(jnp.bfloat16)],
            axis=0,
        )
        bias = bias + jnp.dot(table, spread, preferred_element_type=jnp.float32)
    first = lax.broadcasted_iota(jnp.int32, (16, 512), 0) == 0
    parts = []
    for h in range(4):
        scores = lax.dot_general(
            queries[:, h * HEAD : (h + 1) * HEAD],
            keys,
            (((1,), (1,)), ((), ())),
            preferred_element_type=jnp.float32,
        )
        rows = [jnp.broadcast_to(bias[4 * h + r : 4 * h + r + 1, :], (16, 512)) for r in range(4)]
        rows.append(
            jnp.where(first, bias[17 + 2 * h : 18 + 2 * h, :], bias[24 + 2 * h : 25 + 2 * h, :])
        )
        scores = scores * (1.0 / math.sqrt(HEAD)) + jnp.concatenate(rows, axis=0)
        exps = jnp.exp(scores - jnp.max(scores, axis=-1, keepdims=True))
        totals = jnp.sum(exps, axis=-1, keepdims=True)
        mixed = jnp.dot(exps.astype(jnp.bfloat16), values, preferred_element_type=jnp.float32)
        parts.append((mixed / totals).astype(jnp.bfloat16))
    context = jnp.concatenate(parts, axis=1)
    terms_ref[...] = jnp.dot(
        context, out_weight_ref[...], preferred_element_type=jnp.float32
    ).astype(jnp.bfloat16)


def activate_kernel(
    skip_ref, edge_ref, own_ref, other_ref, gain_ref, dec_bias_ref, keep_ref, send_ref, base_ref, wide, active
):
    me = lax.axis_index("seq")
    section = lax.axis_index("section")
    upper = me >> 2
    gain = gain_ref[...][None, :]
    spread_columns(wide, skip_ref)
    even = take_rows(wide, 0, 64)
    odd = take_rows(wide, 1, 64)
    projected = own_ref[...].astype(jnp.float32) + other_ref[...].astype(jnp.float32)

    def rounded(values_in):
        return values_in.astype(jnp.bfloat16).astype(jnp.float32)

    attended = rounded(jnp.maximum(even, odd) + projected[0:64])
    even = rounded(attended + even)
    odd = rounded(attended + odd)
    put_rows(wide, 0, even)
    put_rows(wide, 1, odd)
    put_rows(active, 8, gelu(normalize(even, gain)))
    put_rows(active, 9, gelu(normalize(odd, gain)))
    edges = edge_ref[0:4, :]
    low = rounded(jnp.maximum(edges[0:1], edges[1:2]) + projected[64:65])
    high = rounded(jnp.maximum(edges[2:3], edges[3:4]) + projected[65:66])
    joined = rounded(edges + jnp.concatenate([low, low, high, high], axis=0))
    halo = gelu(normalize(joined, gain))
    above = jnp.where(me > 0, halo[0:2], 0.0)
    below = jnp.where(me < lax.axis_size("seq") - 1, halo[2:4], 0.0)
    zeros = jnp.zeros((6, 128), jnp.float32)
    for k in range(12):
        columns = slice(128 * k, 128 * k + 128)
        active[k, 0:8, :] = jnp.concatenate([zeros, above[:, columns]], axis=0)
        active[k, 136:144, :] = jnp.concatenate([below[:, columns], zeros], axis=0)
    for k in range(6):
        keep_ref[:, 128 * k : 128 * k + 128] = active[upper * 6 + k].astype(jnp.bfloat16)
    for k in range(3):
        columns = slice(128 * k, 128 * k + 128)
        send_ref[:, columns] = active[(1 - upper) * 6 + section * 3 + k].astype(jnp.bfloat16)
        base_ref[:, columns] = wide[section * 3 + k] + dec_bias_ref[columns][None, :]


def load_weight(own_ref, side_ref, next_ref, far_first_ref, far_last_ref, weight):
    slot = lax.axis_index("seq") & 3
    split = far_first_ref.shape[0]
    for relation, ref in enumerate((own_ref, side_ref, next_ref)):
        start = pl.multiple_of((slot ^ relation) * 192, 64)
        for tap in range(KW):
            weight[tap, pl.ds(start, 192), :] = ref[tap]
    start = pl.multiple_of((slot ^ 3) * 192, 64)
    for tap in range(KW):
        piece = far_first_ref[tap] if tap < split else far_last_ref[tap - split]
        weight[tap, pl.ds(start, 192), :] = piece


def shifted_sum(products):
    total = products[0][6:134]
    for tap in range(1, KW):
        total = total + products[tap][6 + tap : 134 + tap]
    return total


def own_kernel(active_ref, base_ref, w0, w1, w2, w3, w4, out_ref, weight):
    load_weight(w0, w1, w2, w3, w4, weight)
    active = active_ref[...]
    out_ref[...] = base_ref[...] + shifted_sum(
        [jnp.dot(active, weight[t], preferred_element_type=jnp.float32) for t in range(KW)]
    )


def partner_kernel(first_ref, second_ref, w0, w1, w2, w3, w4, out_ref, weight):
    load_weight(w0, w1, w2, w3, w4, weight)
    section = lax.axis_index("section")
    first, second = first_ref[...], second_ref[...]
    near = pl.ds(pl.multiple_of(section * 384, 128), 384)
    far = pl.ds(pl.multiple_of((1 - section) * 384, 128), 384)
    out_ref[...] = shifted_sum(
        [
            jnp.dot(first, weight[t, near, :], preferred_element_type=jnp.float32)
            + jnp.dot(second, weight[t, far, :], preferred_element_type=jnp.float32)
            for t in range(KW)
        ]
    ).astype(jnp.bfloat16)


def split_body(
    skip_in, attn_gain, query_weight, kv_weight, pair_bias, out_weight, dec_gain, dec_weight, dec_bias
):
    bf16, f32 = jnp.bfloat16, jnp.float32
    skip = skip_in[0]
    rows, channels = skip.shape
    taps, depth, width = dec_weight.shape
    message, normed = call(
        pool_kernel,
        [((MSG, 256), bf16), ((rows // 2, channels), bf16)],
        [skip, attn_gain, kv_weight, pair_bias],
        [pltpu.VMEM((channels // 128, rows, 128), f32), pltpu.VMEM((MSG, 256), f32)],
    )
    messages = message[None]
    messages = jnp.concatenate([messages, exchange(messages, "seq", 4)], axis=0)
    messages = jnp.concatenate([messages, exchange(messages, "seq", 2)], axis=0)
    held, messages = lax.optimization_barrier((dec_weight, messages))
    after = exchange(held, "seq", 2)
    messages_side = exchange(messages, "seq", 1)
    held, messages_side = lax.optimization_barrier((held, messages_side))
    side = exchange(held, "seq", 1)
    split = (taps + 1) // 2
    far_first = exchange(after[:split], "seq", 1)
    far_last = exchange(side[split:], "seq", 2)
    queries = jnp.dot(normed, query_weight, preferred_element_type=f32).astype(bf16)
    terms, edges = call(
        attention_kernel,
        [((ROWS, channels), bf16), ((8, channels), f32)],
        [queries, messages, messages_side, query_weight, attn_gain, pair_bias, out_weight],
    )
    other = exchange(terms, "section", 1)
    keep, send, base = call(
        activate_kernel,
        [((rows + 16, channels // 2), bf16), ((rows + 16, channels // 4), bf16), ((rows, width), f32)],
        [skip, edges, terms, other, dec_gain, dec_bias],
        [pltpu.VMEM((channels // 128, rows + extra, 128), f32) for extra in (0, 16)],
    )
    first = exchange(send, "seq", 4)
    second = exchange(first, "section", 1)
    weights = [dec_weight, side, after, far_first, far_last]
    scratch = [pltpu.VMEM((taps, 4 * depth, width), bf16)]
    (own,) = call(own_kernel, [((rows, width), f32)], [keep, base] + weights, scratch)
    (partial,) = call(
        partner_kernel, [((rows, width), bf16)], [first, second] + weights, scratch
    )
    decoded = own + exchange(partial, "seq", 4).astype(f32)
    return decoded.astype(bf16)[None]


def solution(mesh):
    return jax.shard_map(
        split_body if mesh.shape["seq"] == 8 else body,
        mesh=mesh,
        in_specs=(
            P("groups", "seq", None),
            P(),
            P(None, "section"),
            P(),
            P("groups", "section", "seq", None),
            P("section", None),
            P(),
            P(None, "seq", "section"),
            P("section"),
        ),
        out_specs=P("groups", "seq", "section"),
        check_vma=False,
    )
```

```python
import math

import jax
import jax.numpy as jnp
from jax import lax
from jax.experimental import pallas as pl
from jax.experimental.pallas import tpu as pltpu
from jax.sharding import PartitionSpec as P

HEAD = 128
KW = 5
PAIR = 16


def extended(block, sides, width):
    for axis, dim in sides:
        count = lax.axis_size(axis)
        forward = [(i, i + 1) for i in range(count - 1)]
        backward = [(target, source) for source, target in forward]
        low = lax.ppermute(
            lax.slice_in_dim(block, block.shape[dim] - width, None, axis=dim), axis, forward
        )
        high = lax.ppermute(lax.slice_in_dim(block, 0, width, axis=dim), axis, backward)
        block = jnp.concatenate([low, block, high], axis=dim)
    return block


def norm_scale(values_in, gain):
    wide = values_in.astype(jnp.float32)
    return wide * lax.rsqrt(jnp.mean(wide * wide, axis=-1, keepdims=True) + 1e-06) * gain


def body(
    skip_in,
    attn_gain,
    query_weight,
    kv_weight,
    pair_bias,
    out_weight,
    dec_gain,
    dec_weight,
    dec_bias,
):
    seq_count, local_rows, channels = skip_in.shape
    half_rows = local_rows // 2
    local_heads = query_weight.shape[1] // HEAD
    logit_scale = 1.0 / math.sqrt(HEAD)
    pooled = jnp.max(skip_in.reshape(seq_count, half_rows, 2, channels), axis=2)
    normed = norm_scale(pooled, attn_gain).astype(jnp.bfloat16)
    flattened = normed.reshape(seq_count * half_rows, channels)
    query_rows = jnp.dot(flattened, query_weight, preferred_element_type=jnp.float32).astype(
        jnp.bfloat16
    )
    query_rows = query_rows.reshape(seq_count, half_rows, local_heads, HEAD)
    row_bias = jnp.repeat(pair_bias, PAIR, axis=2)
    row_bias = jnp.pad(row_bias, ((0, 0), (0, 0), (0, 0), (0, 2)))
    quarter = half_rows // 2
    own_rows = lax.dynamic_slice_in_dim(normed, lax.axis_index("section") * quarter, quarter, 1)
    key_values = jnp.dot(
        own_rows.reshape(seq_count * quarter, channels),
        kv_weight,
        preferred_element_type=jnp.float32,
    )
    key_values = key_values.astype(jnp.bfloat16).reshape(seq_count, quarter, 2 * HEAD)
    piece = lax.all_gather(key_values, ("seq", "section"), axis=1, tiled=True)
    start = jnp.int32(0)
    running_max = jnp.full((seq_count, local_heads, half_rows), -1e30, jnp.float32)
    running_sum = jnp.zeros((seq_count, local_heads, half_rows), jnp.float32)
    weighted = jnp.zeros((seq_count, local_heads, half_rows, HEAD), jnp.float32)
    piece_rows = piece.shape[1]
    block_size = min(piece_rows, 2048)
    for offset in range(0, piece_rows, block_size):
        piece_len = min(block_size, piece_rows - offset)
        sub_piece = piece[:, offset : offset + piece_len]
        key_portion = sub_piece[:, :, :HEAD]
        value_part = sub_piece[:, :, HEAD:]
        first_row = start + offset
        blocks = lax.dynamic_slice_in_dim(row_bias, first_row // PAIR, piece_len // PAIR + 2, 3)
        spread = jnp.repeat(blocks, PAIR, axis=3)
        key_bias = lax.dynamic_slice_in_dim(spread, first_row % PAIR, piece_len, 3)
        scores = (
            jnp.einsum(
                "wtzj,wgj->wztg", query_rows, key_portion, preferred_element_type=jnp.float32
            )
            * logit_scale
            + key_bias
        )
        new_max = jnp.maximum(running_max, jnp.max(scores, axis=-1))
        rescale = jnp.exp(running_max - new_max)
        exponent_scores = jnp.exp(scores - new_max[..., None])
        running_sum = running_sum * rescale + jnp.sum(exponent_scores, axis=-1)
        weighted = weighted * rescale[..., None] + jnp.einsum(
            "umrl,ult->umrt",
            exponent_scores.astype(jnp.bfloat16),
            value_part,
            preferred_element_type=jnp.float32,
        )
        running_max = new_max
    folded = (running_max, running_sum, weighted)
    running_max, running_sum, weighted = folded
    context = (weighted / running_sum[..., None]).astype(jnp.bfloat16)
    context = jnp.transpose(context, (0, 2, 1, 3)).reshape(
        seq_count * half_rows, local_heads * HEAD
    )
    partial_value = jnp.dot(context, out_weight, preferred_element_type=jnp.float32).reshape(
        seq_count, half_rows, channels
    )
    summed = lax.psum(partial_value.astype(jnp.bfloat16), "section").astype(jnp.float32)
    attended = (pooled.astype(jnp.float32) + summed).astype(jnp.bfloat16)
    joined = (
        jnp.repeat(attended, 2, axis=1).astype(jnp.float32) + skip_in.astype(jnp.float32)
    ).astype(jnp.bfloat16)
    activated = jax.nn.gelu(norm_scale(joined, dec_gain)).astype(jnp.bfloat16)
    padded = extended(activated, (("seq", 1),), KW // 2)
    out_half = dec_weight.shape[2]
    piece = lax.all_gather(dec_weight, "seq", axis=1, tiled=True)
    piece_rows = piece.shape[1]
    stacked = jnp.concatenate(
        [padded[:, tap_index : tap_index + local_rows] for tap_index in range(KW)], axis=2
    )
    stacked = stacked.reshape(seq_count * local_rows, KW * piece_rows)
    convolved = jnp.dot(
        stacked, piece.reshape(KW * piece_rows, out_half), preferred_element_type=jnp.float32
    )
    residual = lax.dynamic_slice_in_dim(joined, lax.axis_index("section") * out_half, out_half, 2)
    decoded = (
        convolved.reshape(seq_count, local_rows, out_half) + dec_bias + residual.astype(jnp.float32)
    )
    return decoded.astype(jnp.bfloat16)


ROWS = 80
MSG = 112
LIMIT = 24 * 1024 * 1024


def exchange(values_in, axis, mask):
    count = lax.axis_size(axis)
    return lax.ppermute(values_in, axis, [(i, i ^ mask) for i in range(count)])


def call(kernel, outs, args, scratch=(), spaces=None, limit=LIMIT):
    vmem = pl.BlockSpec(memory_space=pltpu.VMEM)
    return pl.pallas_call(
        kernel,
        out_shape=[jax.ShapeDtypeStruct(shape, kind) for shape, kind in outs],
        in_specs=[vmem] * len(args) if spaces is None else spaces,
        out_specs=[vmem] * len(outs),
        scratch_shapes=list(scratch),
        compiler_params=pltpu.CompilerParams(vmem_limit_bytes=limit),
    )(*args)


def split_three(wide):
    high = wide.astype(jnp.bfloat16)
    rest = wide - high.astype(jnp.float32)
    middle = rest.astype(jnp.bfloat16)
    low = (rest - middle.astype(jnp.float32)).astype(jnp.bfloat16)
    return high, middle, low


def own_bias(bias_ref):
    return jnp.concatenate([bias_ref[0, h] for h in range(4)], axis=0)


def normalize(wide, gain):
    return wide * lax.rsqrt(jnp.mean(wide * wide, axis=-1, keepdims=True) + 1e-06) * gain


def gelu(wide):
    inner = math.sqrt(2.0 / math.pi) * (wide + 0.044715 * (wide * wide * wide))
    return 0.5 * wide * (1.0 + jnp.tanh(inner))


def spread_columns(wide, values_in):
    for k in range(wide.shape[0]):
        wide[k] = values_in[:, 128 * k : 128 * k + 128].astype(jnp.float32)


def take_rows(wide, start, size):
    return jnp.concatenate(
        [wide[k, pl.ds(start, size, stride=2), :] for k in range(wide.shape[0])], axis=1
    )


def put_rows(wide, start, values_in):
    for k in range(wide.shape[0]):
        wide[k, pl.ds(start, values_in.shape[0], stride=2), :] = values_in[:, 128 * k : 128 * k + 128]


def pool_kernel(
    skip_hbm,
    gain_hbm,
    weight_hbm,
    bias_hbm,
    dec_hbm,
    message_ref,
    normed_ref,
    piece_ref,
    skip_ref,
    gain_ref,
    weight_ref,
    bias_ref,
    wide,
    lines,
    semaphores,
):
    group = lax.axis_index("groups")
    pieces = dec_hbm.shape[0] // 2
    pairs = (
        (skip_hbm, skip_ref),
        (gain_hbm, gain_ref),
        (bias_hbm, bias_ref),
        (weight_hbm, weight_ref),
        (dec_hbm.at[pl.ds(group * pieces, pieces)], piece_ref),
    )
    copies = [
        pltpu.make_async_copy(source, target, semaphores.at[n])
        for n, (source, target) in enumerate(pairs)
    ]
    for copy in copies:
        copy.start()
    for copy in copies[:3]:
        copy.wait()
    half = skip_ref.shape[0] // 2
    spread_columns(wide, skip_ref)
    pooled = jnp.maximum(take_rows(wide, 0, half), take_rows(wide, 1, half))
    normed = normalize(pooled, gain_ref[...][None, :]).astype(jnp.bfloat16)
    normed_ref[...] = normed
    copies[3].wait()
    lines[0:half, :] = jnp.dot(normed, weight_ref[...], preferred_element_type=jnp.float32)
    last = skip_ref.shape[0]
    for n, row in enumerate((0, 1, last - 2, last - 1)):
        for k in range(12):
            at = half + 6 * n + k // 2
            lines[at : at + 1, 128 * (k % 2) : 128 * (k % 2) + 128] = wide[k, row : row + 1, :]
    lines[88:MSG, :] = jnp.zeros((MSG - 88, 256), jnp.float32)
    for n, term in enumerate(split_three(own_bias(bias_ref))):
        for h in range(4):
            for k, cell in enumerate((0, 3)):
                at = 88 + 8 * n + 2 * h + k
                lines[at : at + 1, 0:32] = term[4 * h + cell : 4 * h + cell + 1, :].astype(
                    jnp.float32
                )
    message_ref[...] = lines[...].astype(jnp.bfloat16)
    copies[4].wait()


def reverse_bits(value):
    return (value & 1) * 4 + (value & 2) + (value >> 2)


def attention_kernel(
    query_ref, near_ref, side_ref, query_weight_ref, gain_ref, bias_ref, out_weight_ref, terms_ref, edge_ref
):
    me = lax.axis_index("seq")
    count = lax.axis_size("seq")
    low_slot = reverse_bits(me ^ jnp.maximum(me - 1, 0))
    high_slot = reverse_bits(me ^ jnp.minimum(me + 1, count - 1))

    def block_of(slot):
        near = near_ref[slot & 3].astype(jnp.float32)
        return jnp.where(slot < 4, near, side_ref[slot & 3].astype(jnp.float32))

    low, high = block_of(low_slot), block_of(high_slot)

    def line(block, row):
        start = 64 + 6 * row
        return jnp.concatenate([block[start + k : start + k + 1, :] for k in range(6)], axis=1)

    edges = jnp.concatenate(
        [line(low, 2), line(low, 3), line(high, 0), line(high, 1)], axis=0
    )
    edge_ref[0:4, :] = edges
    edge_ref[4:8, :] = jnp.zeros_like(edges)
    pooled = jnp.concatenate(
        [
            jnp.maximum(edges[0:1], edges[1:2]),
            jnp.maximum(edges[2:3], edges[3:4]),
            jnp.zeros((14, edges.shape[1]), jnp.float32),
        ],
        axis=0,
    )
    normed = normalize(pooled, gain_ref[...][None, :]).astype(jnp.bfloat16)
    halo_query = jnp.dot(normed, query_weight_ref[...], preferred_element_type=jnp.float32)
    queries = jnp.concatenate([query_ref[...], halo_query.astype(jnp.bfloat16)], axis=0)
    pieces = [ref[k, 0:64, :] for ref in (near_ref, side_ref) for k in range(4)]
    keys = jnp.concatenate([piece[:, 0:HEAD] for piece in pieces], axis=0)
    values = jnp.concatenate([piece[:, HEAD : 2 * HEAD] for piece in pieces], axis=0)
    cell = lax.broadcasted_iota(jnp.int32, (32, 512), 0)
    column = lax.broadcasted_iota(jnp.int32, (32, 512), 1)
    wanted = 4 * (reverse_bits(column >> 6) ^ me) + ((column & 63) >> 4)
    spread = jnp.where(cell == wanted, 1.0, 0.0).astype(jnp.bfloat16)
    bias = jnp.zeros((32, 512), jnp.float32)
    for n, term in enumerate(split_three(own_bias(bias_ref))):
        at = 88 + 8 * n
        table = jnp.concatenate(
            [term, low[at : at + 8, 0:32].astype(jnp.bfloat16), high[at : at + 8, 0:32].astype(jnp.bfloat16)],
            axis=0,
        )
        bias = bias + jnp.dot(table, spread, preferred_element_type=jnp.float32)
    first = lax.broadcasted_iota(jnp.int32, (16, 512), 0) == 0
    parts = []
    for h in range(4):
        scores = lax.dot_general(
            queries[:, h * HEAD : (h + 1) * HEAD],
            keys,
            (((1,), (1,)), ((), ())),
            preferred_element_type=jnp.float32,
        )
        rows = [jnp.broadcast_to(bias[4 * h + r : 4 * h + r + 1, :], (16, 512)) for r in range(4)]
        rows.append(
            jnp.where(first, bias[17 + 2 * h : 18 + 2 * h, :], bias[24 + 2 * h : 25 + 2 * h, :])
        )
        scores = scores * (1.0 / math.sqrt(HEAD)) + jnp.concatenate(rows, axis=0)
        exps = jnp.exp(scores - jnp.max(scores, axis=-1, keepdims=True))
        totals = jnp.sum(exps, axis=-1, keepdims=True)
        mixed = jnp.dot(exps.astype(jnp.bfloat16), values, preferred_element_type=jnp.float32)
        parts.append((mixed / totals).astype(jnp.bfloat16))
    context = jnp.concatenate(parts, axis=1)
    terms_ref[...] = jnp.dot(
        context, out_weight_ref[...], preferred_element_type=jnp.float32
    ).astype(jnp.bfloat16)


def activate_kernel(
    skip_ref, edge_ref, own_ref, other_ref, gain_ref, dec_bias_ref, keep_ref, send_ref, base_ref, wide, active
):
    me = lax.axis_index("seq")
    section = lax.axis_index("section")
    upper = me >> 2
    gain = gain_ref[...][None, :]
    spread_columns(wide, skip_ref)
    even = take_rows(wide, 0, 64)
    odd = take_rows(wide, 1, 64)
    projected = own_ref[...].astype(jnp.float32) + other_ref[...].astype(jnp.float32)

    def rounded(values_in):
        return values_in.astype(jnp.bfloat16).astype(jnp.float32)

    attended = rounded(jnp.maximum(even, odd) + projected[0:64])
    even = rounded(attended + even)
    odd = rounded(attended + odd)
    put_rows(wide, 0, even)
    put_rows(wide, 1, odd)
    put_rows(active, 8, gelu(normalize(even, gain)))
    put_rows(active, 9, gelu(normalize(odd, gain)))
    edges = edge_ref[0:4, :]
    low = rounded(jnp.maximum(edges[0:1], edges[1:2]) + projected[64:65])
    high = rounded(jnp.maximum(edges[2:3], edges[3:4]) + projected[65:66])
    joined = rounded(edges + jnp.concatenate([low, low, high, high], axis=0))
    halo = gelu(normalize(joined, gain))
    above = jnp.where(me > 0, halo[0:2], 0.0)
    below = jnp.where(me < lax.axis_size("seq") - 1, halo[2:4], 0.0)
    zeros = jnp.zeros((6, 128), jnp.float32)
    for k in range(12):
        columns = slice(128 * k, 128 * k + 128)
        active[k, 0:8, :] = jnp.concatenate([zeros, above[:, columns]], axis=0)
        active[k, 136:144, :] = jnp.concatenate([below[:, columns], zeros], axis=0)
    for k in range(6):
        keep_ref[:, 128 * k : 128 * k + 128] = active[upper * 6 + k].astype(jnp.bfloat16)
    for k in range(3):
        columns = slice(128 * k, 128 * k + 128)
        send_ref[:, columns] = active[(1 - upper) * 6 + section * 3 + k].astype(jnp.bfloat16)
        base_ref[:, columns] = wide[section * 3 + k] + dec_bias_ref[columns][None, :]


def load_weight(own_ref, remote_refs, weight):
    slot = lax.axis_index("seq") & 3
    group = lax.axis_index("groups")
    for n in range(2 * KW):
        weight[(n // 2) * 8 + 2 * slot + n % 2] = own_ref[n]
    for n, ref in enumerate(remote_refs):
        block = slot ^ (n // 2 + 1)
        first = KW * (group if n % 2 == 0 else 1 - group)
        for k in range(KW):
            chunk = first + k
            weight[(chunk // 2) * 8 + 2 * block + chunk % 2] = ref[k]


def tap_weight(weight, tap, start, size):
    return weight[pl.ds(8 * tap + start, size)].reshape(size * weight.shape[1], weight.shape[2])


def shifted_sum(products):
    total = products[0][6:134]
    for tap in range(1, KW):
        total = total + products[tap][6 + tap : 134 + tap]
    return total


def own_kernel(active_ref, base_ref, w0, w1, w2, w3, w4, w5, w6, out_ref, weight):
    load_weight(w0, (w1, w2, w3, w4, w5, w6), weight)
    active = active_ref[...]
    out_ref[...] = base_ref[...] + shifted_sum(
        [
            jnp.dot(active, tap_weight(weight, t, 0, 8), preferred_element_type=jnp.float32)
            for t in range(KW)
        ]
    )


def partner_kernel(first_ref, second_ref, w0, w1, w2, w3, w4, w5, w6, out_ref, weight):
    load_weight(w0, (w1, w2, w3, w4, w5, w6), weight)
    section = lax.axis_index("section")
    first, second = first_ref[...], second_ref[...]
    near, far = 4 * section, 4 * (1 - section)
    out_ref[...] = shifted_sum(
        [
            jnp.dot(first, tap_weight(weight, t, near, 4), preferred_element_type=jnp.float32)
            + jnp.dot(second, tap_weight(weight, t, far, 4), preferred_element_type=jnp.float32)
            for t in range(KW)
        ]
    ).astype(jnp.bfloat16)


def split_body(
    skip_in, attn_gain, query_weight, kv_weight, pair_bias, out_weight, dec_gain, dec_weight, dec_bias
):
    bf16, f32 = jnp.bfloat16, jnp.float32
    skip = skip_in[0]
    rows, channels = skip.shape
    taps, depth, width = dec_weight.shape
    chunks = dec_weight.reshape(2 * taps, depth // 2, width)
    message, normed, piece = call(
        pool_kernel,
        [((MSG, 256), bf16), ((rows // 2, channels), bf16), ((taps, depth // 2, width), bf16)],
        [skip, attn_gain, kv_weight, pair_bias, chunks],
        [
            pltpu.VMEM((rows, channels), bf16),
            pltpu.VMEM((channels,), f32),
            pltpu.VMEM(kv_weight.shape, bf16),
            pltpu.VMEM(pair_bias.shape, f32),
            pltpu.VMEM((channels // 128, rows, 128), f32),
            pltpu.VMEM((MSG, 256), f32),
            pltpu.SemaphoreType.DMA((5,)),
        ],
        [pl.BlockSpec(memory_space=pl.ANY)] * 5,
        60 * 1024 * 1024,
    )
    messages = message[None]
    messages = jnp.concatenate([messages, exchange(messages, "seq", 4)], axis=0)
    side = exchange(piece, "seq", 1)
    messages = jnp.concatenate([messages, exchange(messages, "seq", 2)], axis=0)
    after = exchange(lax.optimization_barrier((piece, messages))[0], "seq", 2)
    messages_side = exchange(messages, "seq", 1)
    side_rest = exchange(lax.optimization_barrier((side, messages))[0], "groups", 1)
    queries = jnp.dot(normed, query_weight, preferred_element_type=f32).astype(bf16)
    terms, edges = call(
        attention_kernel,
        [((ROWS, channels), bf16), ((8, channels), f32)],
        [queries, messages, messages_side, query_weight, attn_gain, pair_bias, out_weight],
    )
    other = exchange(terms, "section", 1)
    keep, send, base = call(
        activate_kernel,
        [((rows + 16, channels // 2), bf16), ((rows + 16, channels // 4), bf16), ((rows, width), f32)],
        [skip, edges, terms, other, dec_gain, dec_bias],
        [pltpu.VMEM((channels // 128, rows + extra, 128), f32) for extra in (0, 16)],
    )
    first = exchange(send, "seq", 4)
    held = lax.optimization_barrier((after, send))[0]
    after_rest = exchange(held, "groups", 1)
    far = exchange(held, "seq", 1)
    far_rest = exchange(lax.optimization_barrier((side_rest, send))[0], "seq", 2)
    second = exchange(first, "section", 1)
    weights = [chunks, side, side_rest, after, after_rest, far, far_rest]
    scratch = [pltpu.VMEM((8 * taps, depth // 2, width), bf16)]
    (own,) = call(own_kernel, [((rows, width), f32)], [keep, base] + weights, scratch)
    (partial,) = call(
        partner_kernel, [((rows, width), bf16)], [first, second] + weights, scratch
    )
    decoded = own + exchange(partial, "seq", 4).astype(f32)
    return decoded.astype(bf16)[None]


def solution(mesh):
    return jax.shard_map(
        split_body if mesh.shape["seq"] == 8 else body,
        mesh=mesh,
        in_specs=(
            P("groups", "seq", None),
            P(),
            P(None, "section"),
            P(),
            P("groups", "section", "seq", None),
            P("section", None),
            P(),
            P(None, "seq", "section"),
            P("section"),
        ),
        out_specs=P("groups", "seq", "section"),
        check_vma=False,
    )
```

```python
import math

import jax
import jax.numpy as jnp
from jax import lax
from jax.experimental import pallas as pl
from jax.experimental.pallas import tpu as pltpu
from jax.sharding import PartitionSpec as P

HEAD = 128
KW = 5
PAIR = 16


def extended(block, sides, width):
    for axis, dim in sides:
        count = lax.axis_size(axis)
        forward = [(i, i + 1) for i in range(count - 1)]
        backward = [(target, source) for source, target in forward]
        low = lax.ppermute(
            lax.slice_in_dim(block, block.shape[dim] - width, None, axis=dim), axis, forward
        )
        high = lax.ppermute(lax.slice_in_dim(block, 0, width, axis=dim), axis, backward)
        block = jnp.concatenate([low, block, high], axis=dim)
    return block


def norm_scale(values_in, gain):
    wide = values_in.astype(jnp.float32)
    return wide * lax.rsqrt(jnp.mean(wide * wide, axis=-1, keepdims=True) + 1e-06) * gain


def body(
    skip_in,
    attn_gain,
    query_weight,
    kv_weight,
    pair_bias,
    out_weight,
    dec_gain,
    dec_weight,
    dec_bias,
):
    seq_count, local_rows, channels = skip_in.shape
    half_rows = local_rows // 2
    local_heads = query_weight.shape[1] // HEAD
    logit_scale = 1.0 / math.sqrt(HEAD)
    pooled = jnp.max(skip_in.reshape(seq_count, half_rows, 2, channels), axis=2)
    normed = norm_scale(pooled, attn_gain).astype(jnp.bfloat16)
    flattened = normed.reshape(seq_count * half_rows, channels)
    query_rows = jnp.dot(flattened, query_weight, preferred_element_type=jnp.float32).astype(
        jnp.bfloat16
    )
    query_rows = query_rows.reshape(seq_count, half_rows, local_heads, HEAD)
    row_bias = jnp.repeat(pair_bias, PAIR, axis=2)
    row_bias = jnp.pad(row_bias, ((0, 0), (0, 0), (0, 0), (0, 2)))
    quarter = half_rows // 2
    own_rows = lax.dynamic_slice_in_dim(normed, lax.axis_index("section") * quarter, quarter, 1)
    key_values = jnp.dot(
        own_rows.reshape(seq_count * quarter, channels),
        kv_weight,
        preferred_element_type=jnp.float32,
    )
    key_values = key_values.astype(jnp.bfloat16).reshape(seq_count, quarter, 2 * HEAD)
    piece = lax.all_gather(key_values, ("seq", "section"), axis=1, tiled=True)
    start = jnp.int32(0)
    running_max = jnp.full((seq_count, local_heads, half_rows), -1e30, jnp.float32)
    running_sum = jnp.zeros((seq_count, local_heads, half_rows), jnp.float32)
    weighted = jnp.zeros((seq_count, local_heads, half_rows, HEAD), jnp.float32)
    piece_rows = piece.shape[1]
    block_size = min(piece_rows, 2048)
    for offset in range(0, piece_rows, block_size):
        piece_len = min(block_size, piece_rows - offset)
        sub_piece = piece[:, offset : offset + piece_len]
        key_portion = sub_piece[:, :, :HEAD]
        value_part = sub_piece[:, :, HEAD:]
        first_row = start + offset
        blocks = lax.dynamic_slice_in_dim(row_bias, first_row // PAIR, piece_len // PAIR + 2, 3)
        spread = jnp.repeat(blocks, PAIR, axis=3)
        key_bias = lax.dynamic_slice_in_dim(spread, first_row % PAIR, piece_len, 3)
        scores = (
            jnp.einsum(
                "wtzj,wgj->wztg", query_rows, key_portion, preferred_element_type=jnp.float32
            )
            * logit_scale
            + key_bias
        )
        new_max = jnp.maximum(running_max, jnp.max(scores, axis=-1))
        rescale = jnp.exp(running_max - new_max)
        exponent_scores = jnp.exp(scores - new_max[..., None])
        running_sum = running_sum * rescale + jnp.sum(exponent_scores, axis=-1)
        weighted = weighted * rescale[..., None] + jnp.einsum(
            "umrl,ult->umrt",
            exponent_scores.astype(jnp.bfloat16),
            value_part,
            preferred_element_type=jnp.float32,
        )
        running_max = new_max
    folded = (running_max, running_sum, weighted)
    running_max, running_sum, weighted = folded
    context = (weighted / running_sum[..., None]).astype(jnp.bfloat16)
    context = jnp.transpose(context, (0, 2, 1, 3)).reshape(
        seq_count * half_rows, local_heads * HEAD
    )
    partial_value = jnp.dot(context, out_weight, preferred_element_type=jnp.float32).reshape(
        seq_count, half_rows, channels
    )
    summed = lax.psum(partial_value.astype(jnp.bfloat16), "section").astype(jnp.float32)
    attended = (pooled.astype(jnp.float32) + summed).astype(jnp.bfloat16)
    joined = (
        jnp.repeat(attended, 2, axis=1).astype(jnp.float32) + skip_in.astype(jnp.float32)
    ).astype(jnp.bfloat16)
    activated = jax.nn.gelu(norm_scale(joined, dec_gain)).astype(jnp.bfloat16)
    padded = extended(activated, (("seq", 1),), KW // 2)
    out_half = dec_weight.shape[2]
    piece = lax.all_gather(dec_weight, "seq", axis=1, tiled=True)
    piece_rows = piece.shape[1]
    stacked = jnp.concatenate(
        [padded[:, tap_index : tap_index + local_rows] for tap_index in range(KW)], axis=2
    )
    stacked = stacked.reshape(seq_count * local_rows, KW * piece_rows)
    convolved = jnp.dot(
        stacked, piece.reshape(KW * piece_rows, out_half), preferred_element_type=jnp.float32
    )
    residual = lax.dynamic_slice_in_dim(joined, lax.axis_index("section") * out_half, out_half, 2)
    decoded = (
        convolved.reshape(seq_count, local_rows, out_half) + dec_bias + residual.astype(jnp.float32)
    )
    return decoded.astype(jnp.bfloat16)


ROWS = 80
MSG = 48
LIMIT = 24 * 1024 * 1024


def exchange(values_in, axis, mask):
    count = lax.axis_size(axis)
    return lax.ppermute(values_in, axis, [(i, i ^ mask) for i in range(count)])


def call(kernel, outs, args, scratch=(), spaces=None, limit=LIMIT):
    vmem = pl.BlockSpec(memory_space=pltpu.VMEM)
    return pl.pallas_call(
        kernel,
        out_shape=[jax.ShapeDtypeStruct(shape, kind) for shape, kind in outs],
        in_specs=[vmem] * len(args) if spaces is None else spaces,
        out_specs=[vmem] * len(outs),
        scratch_shapes=list(scratch),
        compiler_params=pltpu.CompilerParams(vmem_limit_bytes=limit),
    )(*args)


def split_three(wide):
    high = wide.astype(jnp.bfloat16)
    rest = wide - high.astype(jnp.float32)
    middle = rest.astype(jnp.bfloat16)
    low = (rest - middle.astype(jnp.float32)).astype(jnp.bfloat16)
    return high, middle, low


def own_bias(bias_ref):
    return jnp.concatenate([bias_ref[0, h] for h in range(4)], axis=0)


def normalize(wide, gain):
    return wide * lax.rsqrt(jnp.mean(wide * wide, axis=-1, keepdims=True) + 1e-06) * gain


def gelu(wide):
    inner = math.sqrt(2.0 / math.pi) * (wide + 0.044715 * (wide * wide * wide))
    return 0.5 * wide * (1.0 + jnp.tanh(inner))


def spread_columns(wide, values_in):
    for k in range(wide.shape[0]):
        wide[k] = values_in[:, 128 * k : 128 * k + 128].astype(jnp.float32)


def take_rows(wide, start, size):
    return jnp.concatenate(
        [wide[k, pl.ds(start, size, stride=2), :] for k in range(wide.shape[0])], axis=1
    )


def put_rows(wide, start, values_in):
    for k in range(wide.shape[0]):
        wide[k, pl.ds(start, values_in.shape[0], stride=2), :] = values_in[:, 128 * k : 128 * k + 128]


def pool_kernel(
    skip_hbm,
    gain_hbm,
    weight_hbm,
    bias_hbm,
    dec_hbm,
    message_ref,
    normed_ref,
    piece_ref,
    skip_ref,
    gain_ref,
    weight_ref,
    bias_ref,
    wide,
    lines,
    semaphores,
):
    group = lax.axis_index("groups")
    pieces = dec_hbm.shape[0] // 2
    pairs = (
        (skip_hbm, skip_ref),
        (gain_hbm, gain_ref),
        (bias_hbm, bias_ref),
        (weight_hbm, weight_ref),
        (dec_hbm.at[pl.ds(group * pieces, pieces)], piece_ref),
    )
    copies = [
        pltpu.make_async_copy(source, target, semaphores.at[n])
        for n, (source, target) in enumerate(pairs)
    ]
    for copy in copies:
        copy.start()
    for copy in copies[:3]:
        copy.wait()
    section = lax.axis_index("section")
    half = skip_ref.shape[0] // 2
    quarter = half // 2
    spread_columns(wide, skip_ref)
    pooled = jnp.maximum(take_rows(wide, 0, half), take_rows(wide, 1, half))
    normed_ref[...] = normalize(pooled, gain_ref[...][None, :]).astype(jnp.bfloat16)
    copies[3].wait()
    own = normed_ref[pl.ds(pl.multiple_of(section * quarter, 16), quarter), :]
    lines[0:quarter, :] = jnp.dot(own, weight_ref[...], preferred_element_type=jnp.float32)
    for n in range(2):
        row = section * (skip_ref.shape[0] - 2) + n
        for k in range(12):
            at = quarter + 6 * n + k // 2
            lines[at : at + 1, 128 * (k % 2) : 128 * (k % 2) + 128] = wide[k, pl.ds(row, 1), :]
    terms = [term.astype(jnp.float32) for term in split_three(own_bias(bias_ref))]
    packed = [
        jnp.concatenate(
            [term[4 * h + cell : 4 * h + cell + 1, :] for cell in (0, 3) for h in range(4)], axis=1
        )
        for term in terms
    ]
    lines[MSG - 4 : MSG, :] = jnp.concatenate(packed + [jnp.zeros((1, 256), jnp.float32)], axis=0)
    message_ref[...] = lines[...].astype(jnp.bfloat16)
    copies[4].wait()


def join_kernel(first_ref, second_ref, out_ref):
    count = first_ref.shape[0]
    out_ref[0:count] = first_ref[...]
    out_ref[count:] = second_ref[...]


def swap_bits(value):
    return 4 * (value & 1) + (value & 2) + (value & 4) // 4


def attention_kernel(
    query_ref,
    near_ref,
    near_other_ref,
    side_ref,
    side_other_ref,
    query_weight_ref,
    gain_ref,
    bias_ref,
    out_weight_ref,
    terms_ref,
    edge_ref,
):
    me = lax.axis_index("seq")
    section = lax.axis_index("section")
    count = lax.axis_size("seq")
    low_slot = swap_bits(me ^ jnp.maximum(me - 1, 0))
    high_slot = swap_bits(me ^ jnp.minimum(me + 1, count - 1))

    def block_of(slot, near, side):
        return jnp.where(
            slot < 4, near[slot & 3].astype(jnp.float32), side[slot & 3].astype(jnp.float32)
        )

    low, high = (block_of(slot, near_ref, side_ref) for slot in (low_slot, high_slot))
    low_edge = jnp.where(section == 1, low, block_of(low_slot, near_other_ref, side_other_ref))
    high_edge = jnp.where(section == 0, high, block_of(high_slot, near_other_ref, side_other_ref))

    def line(block, row):
        start = 32 + 6 * row
        return jnp.concatenate([block[start + k : start + k + 1, :] for k in range(6)], axis=1)

    edges = jnp.concatenate(
        [line(low_edge, 0), line(low_edge, 1), line(high_edge, 0), line(high_edge, 1)], axis=0
    )
    edge_ref[0:4, :] = edges
    edge_ref[4:8, :] = jnp.zeros_like(edges)
    pooled = jnp.concatenate(
        [
            jnp.maximum(edges[0:1], edges[1:2]),
            jnp.maximum(edges[2:3], edges[3:4]),
            jnp.zeros((14, edges.shape[1]), jnp.float32),
        ],
        axis=0,
    )
    normed = normalize(pooled, gain_ref[...][None, :]).astype(jnp.bfloat16)
    halo_query = jnp.dot(normed, query_weight_ref[...], preferred_element_type=jnp.float32)
    queries = jnp.concatenate([query_ref[...], halo_query.astype(jnp.bfloat16)], axis=0)
    pieces = []
    for mine, others in ((near_ref, near_other_ref), (side_ref, side_other_ref)):
        for k in range(4):
            pieces += [mine[k, 0:32, :], others[k, 0:32, :]]
    keys = jnp.concatenate([piece[:, 0:HEAD] for piece in pieces], axis=0)
    values = jnp.concatenate([piece[:, HEAD : 2 * HEAD] for piece in pieces], axis=0)
    cell = lax.broadcasted_iota(jnp.int32, (32, 512), 0)
    column = lax.broadcasted_iota(jnp.int32, (32, 512), 1)
    inner = 2 * (((column >> 5) & 1) ^ section) + ((column & 31) >> 4)
    wanted = 4 * (swap_bits(column >> 6) ^ me) + inner
    spread = jnp.where(cell == wanted, 1.0, 0.0).astype(jnp.bfloat16)
    bias = jnp.zeros((24, 512), jnp.float32)
    for n, term in enumerate(split_three(own_bias(bias_ref))):
        at = MSG - 4 + n
        rows = [low[at : at + 1, 128 + 32 * h : 160 + 32 * h] for h in range(4)]
        rows += [high[at : at + 1, 32 * h : 32 * h + 32] for h in range(4)]
        table = jnp.concatenate([term.astype(jnp.float32)] + rows, axis=0).astype(jnp.bfloat16)
        bias = bias + jnp.dot(table, spread, preferred_element_type=jnp.float32)
    first = lax.broadcasted_iota(jnp.int32, (16, 512), 0) == 0
    parts = []
    for h in range(4):
        scores = lax.dot_general(
            queries[:, h * HEAD : (h + 1) * HEAD],
            keys,
            (((1,), (1,)), ((), ())),
            preferred_element_type=jnp.float32,
        )
        rows = [jnp.broadcast_to(bias[4 * h + r : 4 * h + r + 1, :], (16, 512)) for r in range(4)]
        rows.append(
            jnp.where(first, bias[16 + h : 17 + h, :], bias[20 + h : 21 + h, :])
        )
        scores = scores * (1.0 / math.sqrt(HEAD)) + jnp.concatenate(rows, axis=0)
        exps = jnp.exp(scores - jnp.max(scores, axis=-1, keepdims=True))
        totals = jnp.sum(exps, axis=-1, keepdims=True)
        mixed = jnp.dot(exps.astype(jnp.bfloat16), values, preferred_element_type=jnp.float32)
        parts.append((mixed / totals).astype(jnp.bfloat16))
    context = jnp.concatenate(parts, axis=1)
    terms_ref[...] = jnp.dot(
        context, out_weight_ref[...], preferred_element_type=jnp.float32
    ).astype(jnp.bfloat16)


def activate_kernel(
    skip_ref, edge_ref, own_ref, other_ref, gain_ref, dec_bias_ref, keep_ref, send_ref, base_ref, wide, active
):
    me = lax.axis_index("seq")
    section = lax.axis_index("section")
    upper = me >> 2
    gain = gain_ref[...][None, :]
    spread_columns(wide, skip_ref)
    even = take_rows(wide, 0, 64)
    odd = take_rows(wide, 1, 64)
    projected = own_ref[...].astype(jnp.float32) + other_ref[...].astype(jnp.float32)

    def rounded(values_in):
        return values_in.astype(jnp.bfloat16).astype(jnp.float32)

    attended = rounded(jnp.maximum(even, odd) + projected[0:64])
    even = rounded(attended + even)
    odd = rounded(attended + odd)
    put_rows(wide, 0, even)
    put_rows(wide, 1, odd)
    put_rows(active, 8, gelu(normalize(even, gain)))
    put_rows(active, 9, gelu(normalize(odd, gain)))
    edges = edge_ref[0:4, :]
    low = rounded(jnp.maximum(edges[0:1], edges[1:2]) + projected[64:65])
    high = rounded(jnp.maximum(edges[2:3], edges[3:4]) + projected[65:66])
    joined = rounded(edges + jnp.concatenate([low, low, high, high], axis=0))
    halo = gelu(normalize(joined, gain))
    above = jnp.where(me > 0, halo[0:2], 0.0)
    below = jnp.where(me < lax.axis_size("seq") - 1, halo[2:4], 0.0)
    zeros = jnp.zeros((6, 128), jnp.float32)
    for k in range(12):
        columns = slice(128 * k, 128 * k + 128)
        active[k, 0:8, :] = jnp.concatenate([zeros, above[:, columns]], axis=0)
        active[k, 136:144, :] = jnp.concatenate([below[:, columns], zeros], axis=0)
    for k in range(6):
        keep_ref[:, 128 * k : 128 * k + 128] = active[upper * 6 + k].astype(jnp.bfloat16)
    for k in range(3):
        columns = slice(128 * k, 128 * k + 128)
        send_ref[:, columns] = active[(1 - upper) * 6 + section * 3 + k].astype(jnp.bfloat16)
        base_ref[:, columns] = wide[section * 3 + k] + dec_bias_ref[columns][None, :]


def load_weight(own_ref, remote_refs, weight):
    slot = lax.axis_index("seq") & 3
    group = lax.axis_index("groups")
    for n in range(2 * KW):
        weight[(n // 2) * 8 + 2 * slot + n % 2] = own_ref[n]
    for n, ref in enumerate(remote_refs):
        block = slot ^ (n // 2 + 1)
        first = KW * (group if n % 2 == 0 else 1 - group)
        for k in range(KW):
            chunk = first + k
            weight[(chunk // 2) * 8 + 2 * block + chunk % 2] = ref[k]


def tap_weight(weight, tap, start, size):
    return weight[pl.ds(8 * tap + start, size)].reshape(size * weight.shape[1], weight.shape[2])


def shifted_sum(products):
    total = products[0][6:134]
    for tap in range(1, KW):
        total = total + products[tap][6 + tap : 134 + tap]
    return total


def own_kernel(active_ref, base_ref, w0, w1, w2, w3, w4, w5, w6, out_ref, weight):
    load_weight(w0, (w1, w2, w3, w4, w5, w6), weight)
    active = active_ref[...]
    out_ref[...] = base_ref[...] + shifted_sum(
        [
            jnp.dot(active, tap_weight(weight, t, 0, 8), preferred_element_type=jnp.float32)
            for t in range(KW)
        ]
    )


def partner_kernel(first_ref, second_ref, w0, w1, w2, w3, w4, w5, w6, out_ref, weight):
    load_weight(w0, (w1, w2, w3, w4, w5, w6), weight)
    section = lax.axis_index("section")
    first, second = first_ref[...], second_ref[...]
    near, far = 4 * section, 4 * (1 - section)
    out_ref[...] = shifted_sum(
        [
            jnp.dot(first, tap_weight(weight, t, near, 4), preferred_element_type=jnp.float32)
            + jnp.dot(second, tap_weight(weight, t, far, 4), preferred_element_type=jnp.float32)
            for t in range(KW)
        ]
    ).astype(jnp.bfloat16)


def split_body(
    skip_in, attn_gain, query_weight, kv_weight, pair_bias, out_weight, dec_gain, dec_weight, dec_bias
):
    bf16, f32 = jnp.bfloat16, jnp.float32
    skip = skip_in[0]
    rows, channels = skip.shape
    taps, depth, width = dec_weight.shape
    chunks = dec_weight.reshape(2 * taps, depth // 2, width)
    message, normed, piece = call(
        pool_kernel,
        [((MSG, 256), bf16), ((rows // 2, channels), bf16), ((taps, depth // 2, width), bf16)],
        [
            pltpu.with_memory_space_constraint(values_in, pltpu.HBM)
            for values_in in (skip, attn_gain, kv_weight, pair_bias, chunks)
        ],
        [
            pltpu.VMEM((rows, channels), bf16),
            pltpu.VMEM((channels,), f32),
            pltpu.VMEM(kv_weight.shape, bf16),
            pltpu.VMEM(pair_bias.shape, f32),
            pltpu.VMEM((channels // 128, rows, 128), f32),
            pltpu.VMEM((MSG, 256), f32),
            pltpu.SemaphoreType.DMA((5,)),
        ],
        [pl.BlockSpec(memory_space=pl.ANY)] * 5,
    )
    def joined(values_in, mask):
        count = values_in.shape[0]
        return call(
            join_kernel,
            [((2 * count,) + values_in.shape[1:], bf16)],
            [values_in, exchange(values_in, "seq", mask)],
        )[0]

    def behind(values_in, gate):
        return lax.optimization_barrier((values_in, gate))[0]

    near = joined(message[None], 4)
    side = exchange(piece, "seq", 1)
    near = joined(near, 2)
    after = exchange(behind(piece, near), "seq", 2)
    across = exchange(near, "seq", 1)
    near_other = exchange(near, "section", 1)
    side_rest = exchange(behind(side, near), "groups", 1)
    across_other = exchange(across, "section", 1)
    queries = jnp.dot(normed, query_weight, preferred_element_type=f32).astype(bf16)
    terms, edges = call(
        attention_kernel,
        [((ROWS, channels), bf16), ((8, channels), f32)],
        [queries, near, near_other, across, across_other, query_weight, attn_gain, pair_bias, out_weight],
    )
    other = exchange(terms, "section", 1)
    keep, send, base = call(
        activate_kernel,
        [((rows + 16, channels // 2), bf16), ((rows + 16, channels // 4), bf16), ((rows, width), f32)],
        [skip, edges, terms, other, dec_gain, dec_bias],
        [pltpu.VMEM((channels // 128, rows + extra, 128), f32) for extra in (0, 16)],
    )
    first = exchange(send, "seq", 4)
    held = behind(after, send)
    after_rest = exchange(held, "groups", 1)
    far = exchange(held, "seq", 1)
    far_rest = exchange(behind(side_rest, send), "seq", 2)
    second = exchange(first, "section", 1)
    weights = [chunks, side, side_rest, after, after_rest, far, far_rest]
    scratch = [pltpu.VMEM((8 * taps, depth // 2, width), bf16)]
    (own,) = call(own_kernel, [((rows, width), f32)], [keep, base] + weights, scratch)
    (partial,) = call(
        partner_kernel, [((rows, width), bf16)], [first, second] + weights, scratch
    )
    decoded = own + exchange(partial, "seq", 4).astype(f32)
    return decoded.astype(bf16)[None]


def solution(mesh):
    return jax.shard_map(
        split_body if mesh.shape["seq"] == 8 else body,
        mesh=mesh,
        in_specs=(
            P("groups", "seq", None),
            P(),
            P(None, "section"),
            P(),
            P("groups", "section", "seq", None),
            P("section", None),
            P(),
            P(None, "seq", "section"),
            P("section"),
        ),
        out_specs=P("groups", "seq", "section"),
        check_vma=False,
    )
```

```python
import math

import jax
import jax.numpy as jnp
from jax import lax
from jax.experimental import pallas as pl
from jax.experimental.pallas import tpu as pltpu
from jax.sharding import PartitionSpec as P

HEAD = 128
KW = 5
PAIR = 16


def extended(block, sides, width):
    for axis, dim in sides:
        count = lax.axis_size(axis)
        forward = [(i, i + 1) for i in range(count - 1)]
        backward = [(target, source) for source, target in forward]
        low = lax.ppermute(
            lax.slice_in_dim(block, block.shape[dim] - width, None, axis=dim), axis, forward
        )
        high = lax.ppermute(lax.slice_in_dim(block, 0, width, axis=dim), axis, backward)
        block = jnp.concatenate([low, block, high], axis=dim)
    return block


def norm_scale(values_in, gain):
    wide = values_in.astype(jnp.float32)
    return wide * lax.rsqrt(jnp.mean(wide * wide, axis=-1, keepdims=True) + 1e-06) * gain


def body(
    skip_in,
    attn_gain,
    query_weight,
    kv_weight,
    pair_bias,
    out_weight,
    dec_gain,
    dec_weight,
    dec_bias,
):
    seq_count, local_rows, channels = skip_in.shape
    half_rows = local_rows // 2
    local_heads = query_weight.shape[1] // HEAD
    logit_scale = 1.0 / math.sqrt(HEAD)
    pooled = jnp.max(skip_in.reshape(seq_count, half_rows, 2, channels), axis=2)
    normed = norm_scale(pooled, attn_gain).astype(jnp.bfloat16)
    flattened = normed.reshape(seq_count * half_rows, channels)
    query_rows = jnp.dot(flattened, query_weight, preferred_element_type=jnp.float32).astype(
        jnp.bfloat16
    )
    query_rows = query_rows.reshape(seq_count, half_rows, local_heads, HEAD)
    row_bias = jnp.repeat(pair_bias, PAIR, axis=2)
    row_bias = jnp.pad(row_bias, ((0, 0), (0, 0), (0, 0), (0, 2)))
    quarter = half_rows // 2
    own_rows = lax.dynamic_slice_in_dim(normed, lax.axis_index("section") * quarter, quarter, 1)
    key_values = jnp.dot(
        own_rows.reshape(seq_count * quarter, channels),
        kv_weight,
        preferred_element_type=jnp.float32,
    )
    key_values = key_values.astype(jnp.bfloat16).reshape(seq_count, quarter, 2 * HEAD)
    piece = lax.all_gather(key_values, ("seq", "section"), axis=1, tiled=True)
    start = jnp.int32(0)
    running_max = jnp.full((seq_count, local_heads, half_rows), -1e30, jnp.float32)
    running_sum = jnp.zeros((seq_count, local_heads, half_rows), jnp.float32)
    weighted = jnp.zeros((seq_count, local_heads, half_rows, HEAD), jnp.float32)
    piece_rows = piece.shape[1]
    block_size = min(piece_rows, 2048)
    for offset in range(0, piece_rows, block_size):
        piece_len = min(block_size, piece_rows - offset)
        sub_piece = piece[:, offset : offset + piece_len]
        key_portion = sub_piece[:, :, :HEAD]
        value_part = sub_piece[:, :, HEAD:]
        first_row = start + offset
        blocks = lax.dynamic_slice_in_dim(row_bias, first_row // PAIR, piece_len // PAIR + 2, 3)
        spread = jnp.repeat(blocks, PAIR, axis=3)
        key_bias = lax.dynamic_slice_in_dim(spread, first_row % PAIR, piece_len, 3)
        scores = (
            jnp.einsum(
                "wtzj,wgj->wztg", query_rows, key_portion, preferred_element_type=jnp.float32
            )
            * logit_scale
            + key_bias
        )
        new_max = jnp.maximum(running_max, jnp.max(scores, axis=-1))
        rescale = jnp.exp(running_max - new_max)
        exponent_scores = jnp.exp(scores - new_max[..., None])
        running_sum = running_sum * rescale + jnp.sum(exponent_scores, axis=-1)
        weighted = weighted * rescale[..., None] + jnp.einsum(
            "umrl,ult->umrt",
            exponent_scores.astype(jnp.bfloat16),
            value_part,
            preferred_element_type=jnp.float32,
        )
        running_max = new_max
    folded = (running_max, running_sum, weighted)
    running_max, running_sum, weighted = folded
    context = (weighted / running_sum[..., None]).astype(jnp.bfloat16)
    context = jnp.transpose(context, (0, 2, 1, 3)).reshape(
        seq_count * half_rows, local_heads * HEAD
    )
    partial_value = jnp.dot(context, out_weight, preferred_element_type=jnp.float32).reshape(
        seq_count, half_rows, channels
    )
    summed = lax.psum(partial_value.astype(jnp.bfloat16), "section").astype(jnp.float32)
    attended = (pooled.astype(jnp.float32) + summed).astype(jnp.bfloat16)
    joined = (
        jnp.repeat(attended, 2, axis=1).astype(jnp.float32) + skip_in.astype(jnp.float32)
    ).astype(jnp.bfloat16)
    activated = jax.nn.gelu(norm_scale(joined, dec_gain)).astype(jnp.bfloat16)
    padded = extended(activated, (("seq", 1),), KW // 2)
    out_half = dec_weight.shape[2]
    piece = lax.all_gather(dec_weight, "seq", axis=1, tiled=True)
    piece_rows = piece.shape[1]
    stacked = jnp.concatenate(
        [padded[:, tap_index : tap_index + local_rows] for tap_index in range(KW)], axis=2
    )
    stacked = stacked.reshape(seq_count * local_rows, KW * piece_rows)
    convolved = jnp.dot(
        stacked, piece.reshape(KW * piece_rows, out_half), preferred_element_type=jnp.float32
    )
    residual = lax.dynamic_slice_in_dim(joined, lax.axis_index("section") * out_half, out_half, 2)
    decoded = (
        convolved.reshape(seq_count, local_rows, out_half) + dec_bias + residual.astype(jnp.float32)
    )
    return decoded.astype(jnp.bfloat16)


ROWS = 80
MSG = 48
LIMIT = 24 * 1024 * 1024


def exchange(values_in, axis, mask):
    count = lax.axis_size(axis)
    return lax.ppermute(values_in, axis, [(i, i ^ mask) for i in range(count)])


def call(kernel, outs, args, scratch=(), spaces=None, limit=LIMIT):
    vmem = pl.BlockSpec(memory_space=pltpu.VMEM)
    return pl.pallas_call(
        kernel,
        out_shape=[jax.ShapeDtypeStruct(shape, kind) for shape, kind in outs],
        in_specs=[vmem] * len(args) if spaces is None else spaces,
        out_specs=[vmem] * len(outs),
        scratch_shapes=list(scratch),
        compiler_params=pltpu.CompilerParams(vmem_limit_bytes=limit),
    )(*args)


def split_three(wide):
    high = wide.astype(jnp.bfloat16)
    rest = wide - high.astype(jnp.float32)
    middle = rest.astype(jnp.bfloat16)
    low = (rest - middle.astype(jnp.float32)).astype(jnp.bfloat16)
    return high, middle, low


def own_bias(bias_ref):
    return jnp.concatenate([bias_ref[0, h] for h in range(4)], axis=0)


def normalize(wide, gain):
    return wide * lax.rsqrt(jnp.mean(wide * wide, axis=-1, keepdims=True) + 1e-06) * gain


def gelu(wide):
    inner = math.sqrt(2.0 / math.pi) * (wide + 0.044715 * (wide * wide * wide))
    return 0.5 * wide * (1.0 + jnp.tanh(inner))


def spread_columns(wide, values_in):
    for k in range(wide.shape[0]):
        wide[k] = values_in[:, 128 * k : 128 * k + 128].astype(jnp.float32)


def take_rows(wide, start, size):
    return jnp.concatenate(
        [wide[k, pl.ds(start, size, stride=2), :] for k in range(wide.shape[0])], axis=1
    )


def put_rows(wide, start, values_in):
    for k in range(wide.shape[0]):
        wide[k, pl.ds(start, values_in.shape[0], stride=2), :] = values_in[:, 128 * k : 128 * k + 128]


def pool_kernel(
    skip_hbm,
    gain_hbm,
    weight_hbm,
    bias_hbm,
    dec_hbm,
    message_ref,
    normed_ref,
    piece_ref,
    skip_ref,
    gain_ref,
    weight_ref,
    bias_ref,
    wide,
    lines,
    semaphores,
):
    group = lax.axis_index("groups")
    pieces = dec_hbm.shape[0] // 2
    pairs = (
        (skip_hbm, skip_ref),
        (gain_hbm, gain_ref),
        (bias_hbm, bias_ref),
        (weight_hbm, weight_ref),
        (dec_hbm.at[pl.ds(group * pieces, pieces)], piece_ref),
    )
    copies = [
        pltpu.make_async_copy(source, target, semaphores.at[n])
        for n, (source, target) in enumerate(pairs)
    ]
    for copy in copies:
        copy.start()
    for copy in copies[:3]:
        copy.wait()
    section = lax.axis_index("section")
    half = skip_ref.shape[0] // 2
    quarter = half // 2
    spread_columns(wide, skip_ref)
    pooled = jnp.maximum(take_rows(wide, 0, half), take_rows(wide, 1, half))
    normed_ref[...] = normalize(pooled, gain_ref[...][None, :]).astype(jnp.bfloat16)
    copies[3].wait()
    own = normed_ref[pl.ds(pl.multiple_of(section * quarter, 16), quarter), :]
    lines[0:quarter, :] = jnp.dot(own, weight_ref[...], preferred_element_type=jnp.float32)
    for n in range(2):
        row = section * (skip_ref.shape[0] - 2) + n
        for k in range(12):
            at = quarter + 6 * n + k // 2
            lines[at : at + 1, 128 * (k % 2) : 128 * (k % 2) + 128] = wide[k, pl.ds(row, 1), :]
    terms = [term.astype(jnp.float32) for term in split_three(own_bias(bias_ref))]
    packed = [
        jnp.concatenate(
            [term[4 * h + cell : 4 * h + cell + 1, :] for cell in (0, 3) for h in range(4)], axis=1
        )
        for term in terms
    ]
    lines[MSG - 4 : MSG, :] = jnp.concatenate(packed + [jnp.zeros((1, 256), jnp.float32)], axis=0)
    message_ref[...] = lines[...].astype(jnp.bfloat16)
    copies[4].wait()


def join_kernel(first_ref, second_ref, out_ref):
    count = first_ref.shape[0]
    out_ref[0:count] = first_ref[...]
    out_ref[count:] = second_ref[...]


def swap_bits(value):
    return (value & 1) + 2 * (value & 2) + (value & 4) // 2


def attention_kernel(
    query_ref,
    near_ref,
    near_other_ref,
    side_ref,
    side_other_ref,
    query_weight_ref,
    gain_ref,
    bias_ref,
    out_weight_ref,
    terms_ref,
    edge_ref,
):
    me = lax.axis_index("seq")
    section = lax.axis_index("section")
    count = lax.axis_size("seq")
    low_slot = swap_bits(me ^ jnp.maximum(me - 1, 0))
    high_slot = swap_bits(me ^ jnp.minimum(me + 1, count - 1))

    def block_of(slot, near, side):
        return jnp.where(
            slot < 4, near[slot & 3].astype(jnp.float32), side[slot & 3].astype(jnp.float32)
        )

    low, high = (block_of(slot, near_ref, side_ref) for slot in (low_slot, high_slot))
    low_edge = jnp.where(section == 1, low, block_of(low_slot, near_other_ref, side_other_ref))
    high_edge = jnp.where(section == 0, high, block_of(high_slot, near_other_ref, side_other_ref))

    def line(block, row):
        start = 32 + 6 * row
        return jnp.concatenate([block[start + k : start + k + 1, :] for k in range(6)], axis=1)

    edges = jnp.concatenate(
        [line(low_edge, 0), line(low_edge, 1), line(high_edge, 0), line(high_edge, 1)], axis=0
    )
    edge_ref[0:4, :] = edges
    edge_ref[4:8, :] = jnp.zeros_like(edges)
    pooled = jnp.concatenate(
        [
            jnp.maximum(edges[0:1], edges[1:2]),
            jnp.maximum(edges[2:3], edges[3:4]),
            jnp.zeros((14, edges.shape[1]), jnp.float32),
        ],
        axis=0,
    )
    normed = normalize(pooled, gain_ref[...][None, :]).astype(jnp.bfloat16)
    halo_query = jnp.dot(normed, query_weight_ref[...], preferred_element_type=jnp.float32)
    queries = jnp.concatenate([query_ref[...], halo_query.astype(jnp.bfloat16)], axis=0)
    pieces = []
    for mine, others in ((near_ref, near_other_ref), (side_ref, side_other_ref)):
        for k in range(4):
            pieces += [mine[k, 0:32, :], others[k, 0:32, :]]
    keys = jnp.concatenate([piece[:, 0:HEAD] for piece in pieces], axis=0)
    values = jnp.concatenate([piece[:, HEAD : 2 * HEAD] for piece in pieces], axis=0)
    cell = lax.broadcasted_iota(jnp.int32, (32, 512), 0)
    column = lax.broadcasted_iota(jnp.int32, (32, 512), 1)
    inner = 2 * (((column >> 5) & 1) ^ section) + ((column & 31) >> 4)
    wanted = 4 * (swap_bits(column >> 6) ^ me) + inner
    spread = jnp.where(cell == wanted, 1.0, 0.0).astype(jnp.bfloat16)
    bias = jnp.zeros((24, 512), jnp.float32)
    for n, term in enumerate(split_three(own_bias(bias_ref))):
        at = MSG - 4 + n
        rows = [low[at : at + 1, 128 + 32 * h : 160 + 32 * h] for h in range(4)]
        rows += [high[at : at + 1, 32 * h : 32 * h + 32] for h in range(4)]
        table = jnp.concatenate([term.astype(jnp.float32)] + rows, axis=0).astype(jnp.bfloat16)
        bias = bias + jnp.dot(table, spread, preferred_element_type=jnp.float32)
    first = lax.broadcasted_iota(jnp.int32, (16, 512), 0) == 0
    parts = []
    for h in range(4):
        scores = lax.dot_general(
            queries[:, h * HEAD : (h + 1) * HEAD],
            keys,
            (((1,), (1,)), ((), ())),
            preferred_element_type=jnp.float32,
        )
        rows = [jnp.broadcast_to(bias[4 * h + r : 4 * h + r + 1, :], (16, 512)) for r in range(4)]
        rows.append(
            jnp.where(first, bias[16 + h : 17 + h, :], bias[20 + h : 21 + h, :])
        )
        scores = scores * (1.0 / math.sqrt(HEAD)) + jnp.concatenate(rows, axis=0)
        exps = jnp.exp(scores - jnp.max(scores, axis=-1, keepdims=True))
        totals = jnp.sum(exps, axis=-1, keepdims=True)
        mixed = jnp.dot(exps.astype(jnp.bfloat16), values, preferred_element_type=jnp.float32)
        parts.append((mixed / totals).astype(jnp.bfloat16))
    context = jnp.concatenate(parts, axis=1)
    terms_ref[...] = jnp.dot(
        context, out_weight_ref[...], preferred_element_type=jnp.float32
    ).astype(jnp.bfloat16)


def activate_kernel(
    skip_ref, edge_ref, own_ref, other_ref, gain_ref, dec_bias_ref, keep_ref, send_ref, base_ref, wide, active
):
    me = lax.axis_index("seq")
    section = lax.axis_index("section")
    upper = me >> 2
    gain = gain_ref[...][None, :]
    spread_columns(wide, skip_ref)
    even = take_rows(wide, 0, 64)
    odd = take_rows(wide, 1, 64)
    projected = own_ref[...].astype(jnp.float32) + other_ref[...].astype(jnp.float32)

    def rounded(values_in):
        return values_in.astype(jnp.bfloat16).astype(jnp.float32)

    attended = rounded(jnp.maximum(even, odd) + projected[0:64])
    even = rounded(attended + even)
    odd = rounded(attended + odd)
    put_rows(wide, 0, even)
    put_rows(wide, 1, odd)
    put_rows(active, 8, gelu(normalize(even, gain)))
    put_rows(active, 9, gelu(normalize(odd, gain)))
    edges = edge_ref[0:4, :]
    low = rounded(jnp.maximum(edges[0:1], edges[1:2]) + projected[64:65])
    high = rounded(jnp.maximum(edges[2:3], edges[3:4]) + projected[65:66])
    joined = rounded(edges + jnp.concatenate([low, low, high, high], axis=0))
    halo = gelu(normalize(joined, gain))
    above = jnp.where(me > 0, halo[0:2], 0.0)
    below = jnp.where(me < lax.axis_size("seq") - 1, halo[2:4], 0.0)
    zeros = jnp.zeros((6, 128), jnp.float32)
    for k in range(12):
        columns = slice(128 * k, 128 * k + 128)
        active[k, 0:8, :] = jnp.concatenate([zeros, above[:, columns]], axis=0)
        active[k, 136:144, :] = jnp.concatenate([below[:, columns], zeros], axis=0)
    for k in range(6):
        keep_ref[:, 128 * k : 128 * k + 128] = active[upper * 6 + k].astype(jnp.bfloat16)
    for k in range(3):
        columns = slice(128 * k, 128 * k + 128)
        send_ref[:, columns] = active[(1 - upper) * 6 + section * 3 + k].astype(jnp.bfloat16)
        base_ref[:, columns] = wide[section * 3 + k] + dec_bias_ref[columns][None, :]


def load_weight(own_ref, remote_refs, weight):
    slot = lax.axis_index("seq") & 3
    group = lax.axis_index("groups")
    for n in range(2 * KW):
        weight[(n // 2) * 8 + 2 * slot + n % 2] = own_ref[n]
    for n, ref in enumerate(remote_refs):
        block = slot ^ (n // 2 + 1)
        first = KW * (group if n % 2 == 0 else 1 - group)
        for k in range(KW):
            chunk = first + k
            weight[(chunk // 2) * 8 + 2 * block + chunk % 2] = ref[k]


def tap_weight(weight, tap, start, size):
    return weight[pl.ds(8 * tap + start, size)].reshape(size * weight.shape[1], weight.shape[2])


def shifted_sum(products):
    total = products[0][6:134]
    for tap in range(1, KW):
        total = total + products[tap][6 + tap : 134 + tap]
    return total


def own_kernel(active_ref, base_ref, w0, w1, w2, w3, w4, w5, w6, out_ref, weight):
    load_weight(w0, (w1, w2, w3, w4, w5, w6), weight)
    active = active_ref[...]
    out_ref[...] = base_ref[...] + shifted_sum(
        [
            jnp.dot(active, tap_weight(weight, t, 0, 8), preferred_element_type=jnp.float32)
            for t in range(KW)
        ]
    )


def partner_kernel(first_ref, second_ref, w0, w1, w2, w3, w4, w5, w6, out_ref, weight):
    load_weight(w0, (w1, w2, w3, w4, w5, w6), weight)
    section = lax.axis_index("section")
    first, second = first_ref[...], second_ref[...]
    near, far = 4 * section, 4 * (1 - section)
    out_ref[...] = shifted_sum(
        [
            jnp.dot(first, tap_weight(weight, t, near, 4), preferred_element_type=jnp.float32)
            + jnp.dot(second, tap_weight(weight, t, far, 4), preferred_element_type=jnp.float32)
            for t in range(KW)
        ]
    ).astype(jnp.bfloat16)


def split_body(
    skip_in, attn_gain, query_weight, kv_weight, pair_bias, out_weight, dec_gain, dec_weight, dec_bias
):
    bf16, f32 = jnp.bfloat16, jnp.float32
    skip = skip_in[0]
    rows, channels = skip.shape
    taps, depth, width = dec_weight.shape
    chunks = dec_weight.reshape(2 * taps, depth // 2, width)
    message, normed, piece = call(
        pool_kernel,
        [((MSG, 256), bf16), ((rows // 2, channels), bf16), ((taps, depth // 2, width), bf16)],
        [
            pltpu.with_memory_space_constraint(values_in, pltpu.HBM)
            for values_in in (skip, attn_gain, kv_weight, pair_bias, chunks)
        ],
        [
            pltpu.VMEM((rows, channels), bf16),
            pltpu.VMEM((channels,), f32),
            pltpu.VMEM(kv_weight.shape, bf16),
            pltpu.VMEM(pair_bias.shape, f32),
            pltpu.VMEM((channels // 128, rows, 128), f32),
            pltpu.VMEM((MSG, 256), f32),
            pltpu.SemaphoreType.DMA((5,)),
        ],
        [pl.BlockSpec(memory_space=pl.ANY)] * 5,
    )
    def joined(values_in, mask):
        count = values_in.shape[0]
        return call(
            join_kernel,
            [((2 * count,) + values_in.shape[1:], bf16)],
            [values_in, exchange(values_in, "seq", mask)],
        )[0]

    def behind(values_in, gate):
        return lax.optimization_barrier((values_in, gate))[0]

    after = exchange(piece, "seq", 2)
    near = joined(message[None], 1)
    side = exchange(behind(piece, near), "seq", 1)
    near = joined(near, 4)
    across = exchange(near, "seq", 2)
    near_other = exchange(near, "section", 1)
    after_rest = exchange(behind(after, near), "groups", 1)
    side_rest = exchange(behind(side, near), "groups", 1)
    across, side = lax.optimization_barrier((across, side))
    across_other = exchange(across, "section", 1)
    queries = jnp.dot(normed, query_weight, preferred_element_type=f32).astype(bf16)
    terms, edges = call(
        attention_kernel,
        [((ROWS, channels), bf16), ((8, channels), f32)],
        [queries, near, near_other, across, across_other, query_weight, attn_gain, pair_bias, out_weight],
    )
    other = exchange(terms, "section", 1)
    far = exchange(behind(after, terms), "seq", 1)
    keep, send, base = call(
        activate_kernel,
        [((rows + 16, channels // 2), bf16), ((rows + 16, channels // 4), bf16), ((rows, width), f32)],
        [skip, edges, terms, other, dec_gain, dec_bias],
        [pltpu.VMEM((channels // 128, rows + extra, 128), f32) for extra in (0, 16)],
    )
    first = exchange(send, "seq", 4)
    far_rest = exchange(behind(after_rest, send), "seq", 1)
    second = exchange(first, "section", 1)
    weights = [chunks, side, side_rest, after, after_rest, far, far_rest]
    scratch = [pltpu.VMEM((8 * taps, depth // 2, width), bf16)]
    (own,) = call(own_kernel, [((rows, width), f32)], [keep, base] + weights, scratch)
    (partial,) = call(
        partner_kernel, [((rows, width), bf16)], [first, second] + weights, scratch
    )
    decoded = own + exchange(partial, "seq", 4).astype(f32)
    return decoded.astype(bf16)[None]


def solution(mesh):
    return jax.shard_map(
        split_body if mesh.shape["seq"] == 8 else body,
        mesh=mesh,
        in_specs=(
            P("groups", "seq", None),
            P(),
            P(None, "section"),
            P(),
            P("groups", "section", "seq", None),
            P("section", None),
            P(),
            P(None, "seq", "section"),
            P("section"),
        ),
        out_specs=P("groups", "seq", "section"),
        check_vma=False,
    )
```

```python
import math

import jax
import jax.numpy as jnp
from jax import lax
from jax.experimental import pallas as pl
from jax.experimental.pallas import tpu as pltpu
from jax.sharding import PartitionSpec as P

HEAD = 128
KW = 5
PAIR = 16


def extended(block, sides, width):
    for axis, dim in sides:
        count = lax.axis_size(axis)
        forward = [(i, i + 1) for i in range(count - 1)]
        backward = [(target, source) for source, target in forward]
        low = lax.ppermute(
            lax.slice_in_dim(block, block.shape[dim] - width, None, axis=dim), axis, forward
        )
        high = lax.ppermute(lax.slice_in_dim(block, 0, width, axis=dim), axis, backward)
        block = jnp.concatenate([low, block, high], axis=dim)
    return block


def norm_scale(values_in, gain):
    wide = values_in.astype(jnp.float32)
    return wide * lax.rsqrt(jnp.mean(wide * wide, axis=-1, keepdims=True) + 1e-06) * gain


def body(
    skip_in,
    attn_gain,
    query_weight,
    kv_weight,
    pair_bias,
    out_weight,
    dec_gain,
    dec_weight,
    dec_bias,
):
    seq_count, local_rows, channels = skip_in.shape
    half_rows = local_rows // 2
    local_heads = query_weight.shape[1] // HEAD
    logit_scale = 1.0 / math.sqrt(HEAD)
    pooled = jnp.max(skip_in.reshape(seq_count, half_rows, 2, channels), axis=2)
    normed = norm_scale(pooled, attn_gain).astype(jnp.bfloat16)
    flattened = normed.reshape(seq_count * half_rows, channels)
    query_rows = jnp.dot(flattened, query_weight, preferred_element_type=jnp.float32).astype(
        jnp.bfloat16
    )
    query_rows = query_rows.reshape(seq_count, half_rows, local_heads, HEAD)
    row_bias = jnp.repeat(pair_bias, PAIR, axis=2)
    row_bias = jnp.pad(row_bias, ((0, 0), (0, 0), (0, 0), (0, 2)))
    quarter = half_rows // 2
    own_rows = lax.dynamic_slice_in_dim(normed, lax.axis_index("section") * quarter, quarter, 1)
    key_values = jnp.dot(
        own_rows.reshape(seq_count * quarter, channels),
        kv_weight,
        preferred_element_type=jnp.float32,
    )
    key_values = key_values.astype(jnp.bfloat16).reshape(seq_count, quarter, 2 * HEAD)
    piece = lax.all_gather(key_values, ("seq", "section"), axis=1, tiled=True)
    start = jnp.int32(0)
    running_max = jnp.full((seq_count, local_heads, half_rows), -1e30, jnp.float32)
    running_sum = jnp.zeros((seq_count, local_heads, half_rows), jnp.float32)
    weighted = jnp.zeros((seq_count, local_heads, half_rows, HEAD), jnp.float32)
    piece_rows = piece.shape[1]
    block_size = min(piece_rows, 2048)
    for offset in range(0, piece_rows, block_size):
        piece_len = min(block_size, piece_rows - offset)
        sub_piece = piece[:, offset : offset + piece_len]
        key_portion = sub_piece[:, :, :HEAD]
        value_part = sub_piece[:, :, HEAD:]
        first_row = start + offset
        blocks = lax.dynamic_slice_in_dim(row_bias, first_row // PAIR, piece_len // PAIR + 2, 3)
        spread = jnp.repeat(blocks, PAIR, axis=3)
        key_bias = lax.dynamic_slice_in_dim(spread, first_row % PAIR, piece_len, 3)
        scores = (
            jnp.einsum(
                "wtzj,wgj->wztg", query_rows, key_portion, preferred_element_type=jnp.float32
            )
            * logit_scale
            + key_bias
        )
        new_max = jnp.maximum(running_max, jnp.max(scores, axis=-1))
        rescale = jnp.exp(running_max - new_max)
        exponent_scores = jnp.exp(scores - new_max[..., None])
        running_sum = running_sum * rescale + jnp.sum(exponent_scores, axis=-1)
        weighted = weighted * rescale[..., None] + jnp.einsum(
            "umrl,ult->umrt",
            exponent_scores.astype(jnp.bfloat16),
            value_part,
            preferred_element_type=jnp.float32,
        )
        running_max = new_max
    folded = (running_max, running_sum, weighted)
    running_max, running_sum, weighted = folded
    context = (weighted / running_sum[..., None]).astype(jnp.bfloat16)
    context = jnp.transpose(context, (0, 2, 1, 3)).reshape(
        seq_count * half_rows, local_heads * HEAD
    )
    partial_value = jnp.dot(context, out_weight, preferred_element_type=jnp.float32).reshape(
        seq_count, half_rows, channels
    )
    summed = lax.psum(partial_value.astype(jnp.bfloat16), "section").astype(jnp.float32)
    attended = (pooled.astype(jnp.float32) + summed).astype(jnp.bfloat16)
    joined = (
        jnp.repeat(attended, 2, axis=1).astype(jnp.float32) + skip_in.astype(jnp.float32)
    ).astype(jnp.bfloat16)
    activated = jax.nn.gelu(norm_scale(joined, dec_gain)).astype(jnp.bfloat16)
    padded = extended(activated, (("seq", 1),), KW // 2)
    out_half = dec_weight.shape[2]
    piece = lax.all_gather(dec_weight, "seq", axis=1, tiled=True)
    piece_rows = piece.shape[1]
    stacked = jnp.concatenate(
        [padded[:, tap_index : tap_index + local_rows] for tap_index in range(KW)], axis=2
    )
    stacked = stacked.reshape(seq_count * local_rows, KW * piece_rows)
    convolved = jnp.dot(
        stacked, piece.reshape(KW * piece_rows, out_half), preferred_element_type=jnp.float32
    )
    residual = lax.dynamic_slice_in_dim(joined, lax.axis_index("section") * out_half, out_half, 2)
    decoded = (
        convolved.reshape(seq_count, local_rows, out_half) + dec_bias + residual.astype(jnp.float32)
    )
    return decoded.astype(jnp.bfloat16)


ROWS = 80
MSG = 48
LIMIT = 24 * 1024 * 1024


def exchange(values_in, axis, mask):
    count = lax.axis_size(axis)
    return lax.ppermute(values_in, axis, [(i, i ^ mask) for i in range(count)])


def call(kernel, outs, args, scratch=(), spaces=None, limit=LIMIT):
    vmem = pl.BlockSpec(memory_space=pltpu.VMEM)
    return pl.pallas_call(
        kernel,
        out_shape=[jax.ShapeDtypeStruct(shape, kind) for shape, kind in outs],
        in_specs=[vmem] * len(args) if spaces is None else spaces,
        out_specs=[vmem] * len(outs),
        scratch_shapes=list(scratch),
        compiler_params=pltpu.CompilerParams(vmem_limit_bytes=limit),
    )(*args)


def split_three(wide):
    high = wide.astype(jnp.bfloat16)
    rest = wide - high.astype(jnp.float32)
    middle = rest.astype(jnp.bfloat16)
    low = (rest - middle.astype(jnp.float32)).astype(jnp.bfloat16)
    return high, middle, low


def own_bias(bias_ref):
    return jnp.concatenate([bias_ref[0, h] for h in range(4)], axis=0)


def normalize(wide, gain):
    return wide * lax.rsqrt(jnp.mean(wide * wide, axis=-1, keepdims=True) + 1e-06) * gain


def gelu(wide):
    inner = math.sqrt(2.0 / math.pi) * (wide + 0.044715 * (wide * wide * wide))
    return 0.5 * wide * (1.0 + jnp.tanh(inner))


def spread_columns(wide, values_in):
    for k in range(wide.shape[0]):
        wide[k] = values_in[:, 128 * k : 128 * k + 128].astype(jnp.float32)


def take_rows(wide, start, size):
    return jnp.concatenate(
        [wide[k, pl.ds(start, size, stride=2), :] for k in range(wide.shape[0])], axis=1
    )


def put_rows(wide, start, values_in):
    for k in range(wide.shape[0]):
        wide[k, pl.ds(start, values_in.shape[0], stride=2), :] = values_in[:, 128 * k : 128 * k + 128]


def pool_kernel(
    skip_hbm,
    gain_hbm,
    weight_hbm,
    bias_hbm,
    dec_hbm,
    message_ref,
    normed_ref,
    piece_ref,
    skip_ref,
    gain_ref,
    weight_ref,
    bias_ref,
    wide,
    lines,
    semaphores,
):
    group = lax.axis_index("groups")
    pieces = dec_hbm.shape[0] // 2
    pairs = (
        (skip_hbm, skip_ref),
        (gain_hbm, gain_ref),
        (bias_hbm, bias_ref),
        (weight_hbm, weight_ref),
        (dec_hbm.at[pl.ds(group * pieces, pieces)], piece_ref),
    )
    copies = [
        pltpu.make_async_copy(source, target, semaphores.at[n])
        for n, (source, target) in enumerate(pairs)
    ]
    for copy in copies:
        copy.start()
    for copy in copies[:3]:
        copy.wait()
    section = lax.axis_index("section")
    half = skip_ref.shape[0] // 2
    quarter = half // 2
    spread_columns(wide, skip_ref)
    pooled = jnp.maximum(take_rows(wide, 0, half), take_rows(wide, 1, half))
    normed_ref[...] = normalize(pooled, gain_ref[...][None, :]).astype(jnp.bfloat16)
    copies[3].wait()
    own = normed_ref[pl.ds(pl.multiple_of(section * quarter, 16), quarter), :]
    lines[0:quarter, :] = jnp.dot(own, weight_ref[...], preferred_element_type=jnp.float32)
    for n in range(2):
        row = section * (skip_ref.shape[0] - 2) + n
        for k in range(12):
            at = quarter + 6 * n + k // 2
            lines[at : at + 1, 128 * (k % 2) : 128 * (k % 2) + 128] = wide[k, pl.ds(row, 1), :]
    terms = [term.astype(jnp.float32) for term in split_three(own_bias(bias_ref))]
    packed = [
        jnp.concatenate(
            [term[4 * h + cell : 4 * h + cell + 1, :] for cell in (0, 3) for h in range(4)], axis=1
        )
        for term in terms
    ]
    lines[MSG - 4 : MSG, :] = jnp.concatenate(packed + [jnp.zeros((1, 256), jnp.float32)], axis=0)
    message_ref[...] = lines[...].astype(jnp.bfloat16)
    copies[4].wait()


def join_kernel(first_ref, second_ref, out_ref):
    count = first_ref.shape[0]
    out_ref[0:count] = first_ref[...]
    out_ref[count:] = second_ref[...]


def slot_of(distance):
    return distance // 2 + 4 * (distance & 1)


def distance_of(slot):
    return 2 * (slot & 3) + slot // 4


def attention_kernel(
    query_ref,
    near_ref,
    near_other_ref,
    side_ref,
    side_other_ref,
    query_weight_ref,
    gain_ref,
    bias_ref,
    out_weight_ref,
    terms_ref,
    edge_ref,
):
    me = lax.axis_index("seq")
    section = lax.axis_index("section")
    count = lax.axis_size("seq")
    low_slot = slot_of(me ^ jnp.maximum(me - 1, 0))
    high_slot = slot_of(me ^ jnp.minimum(me + 1, count - 1))

    def block_of(slot, near, side):
        return jnp.where(
            slot < 4, near[slot & 3].astype(jnp.float32), side[slot & 3].astype(jnp.float32)
        )

    low, high = (block_of(slot, near_ref, side_ref) for slot in (low_slot, high_slot))
    low_edge = jnp.where(section == 1, low, block_of(low_slot, near_other_ref, side_other_ref))
    high_edge = jnp.where(section == 0, high, block_of(high_slot, near_other_ref, side_other_ref))

    def line(block, row):
        start = 32 + 6 * row
        return jnp.concatenate([block[start + k : start + k + 1, :] for k in range(6)], axis=1)

    edges = jnp.concatenate(
        [line(low_edge, 0), line(low_edge, 1), line(high_edge, 0), line(high_edge, 1)], axis=0
    )
    edge_ref[0:4, :] = edges
    edge_ref[4:8, :] = jnp.zeros_like(edges)
    pooled = jnp.concatenate(
        [
            jnp.maximum(edges[0:1], edges[1:2]),
            jnp.maximum(edges[2:3], edges[3:4]),
            jnp.zeros((14, edges.shape[1]), jnp.float32),
        ],
        axis=0,
    )
    normed = normalize(pooled, gain_ref[...][None, :]).astype(jnp.bfloat16)
    halo_query = jnp.dot(normed, query_weight_ref[...], preferred_element_type=jnp.float32)
    queries = jnp.concatenate([query_ref[...], halo_query.astype(jnp.bfloat16)], axis=0)
    pieces = []
    for mine, others in ((near_ref, near_other_ref), (side_ref, side_other_ref)):
        for k in range(4):
            pieces += [mine[k, 0:32, :], others[k, 0:32, :]]
    keys = jnp.concatenate([piece[:, 0:HEAD] for piece in pieces], axis=0)
    values = jnp.concatenate([piece[:, HEAD : 2 * HEAD] for piece in pieces], axis=0)
    cell = lax.broadcasted_iota(jnp.int32, (32, 512), 0)
    column = lax.broadcasted_iota(jnp.int32, (32, 512), 1)
    inner = 2 * (((column >> 5) & 1) ^ section) + ((column & 31) >> 4)
    wanted = 4 * (distance_of(column >> 6) ^ me) + inner
    spread = jnp.where(cell == wanted, 1.0, 0.0).astype(jnp.bfloat16)
    bias = jnp.zeros((24, 512), jnp.float32)
    for n, term in enumerate(split_three(own_bias(bias_ref))):
        at = MSG - 4 + n
        rows = [low[at : at + 1, 128 + 32 * h : 160 + 32 * h] for h in range(4)]
        rows += [high[at : at + 1, 32 * h : 32 * h + 32] for h in range(4)]
        table = jnp.concatenate([term.astype(jnp.float32)] + rows, axis=0).astype(jnp.bfloat16)
        bias = bias + jnp.dot(table, spread, preferred_element_type=jnp.float32)
    first = lax.broadcasted_iota(jnp.int32, (16, 512), 0) == 0
    parts = []
    for h in range(4):
        scores = lax.dot_general(
            queries[:, h * HEAD : (h + 1) * HEAD],
            keys,
            (((1,), (1,)), ((), ())),
            preferred_element_type=jnp.float32,
        )
        rows = [jnp.broadcast_to(bias[4 * h + r : 4 * h + r + 1, :], (16, 512)) for r in range(4)]
        rows.append(
            jnp.where(first, bias[16 + h : 17 + h, :], bias[20 + h : 21 + h, :])
        )
        scores = scores * (1.0 / math.sqrt(HEAD)) + jnp.concatenate(rows, axis=0)
        exps = jnp.exp(scores - jnp.max(scores, axis=-1, keepdims=True))
        totals = jnp.sum(exps, axis=-1, keepdims=True)
        mixed = jnp.dot(exps.astype(jnp.bfloat16), values, preferred_element_type=jnp.float32)
        parts.append((mixed / totals).astype(jnp.bfloat16))
    context = jnp.concatenate(parts, axis=1)
    terms_ref[...] = jnp.dot(
        context, out_weight_ref[...], preferred_element_type=jnp.float32
    ).astype(jnp.bfloat16)


def activate_kernel(
    skip_ref, edge_ref, own_ref, other_ref, gain_ref, dec_bias_ref, keep_ref, send_ref, base_ref, wide, active
):
    me = lax.axis_index("seq")
    section = lax.axis_index("section")
    upper = me >> 2
    gain = gain_ref[...][None, :]
    spread_columns(wide, skip_ref)
    even = take_rows(wide, 0, 64)
    odd = take_rows(wide, 1, 64)
    projected = own_ref[...].astype(jnp.float32) + other_ref[...].astype(jnp.float32)

    def rounded(values_in):
        return values_in.astype(jnp.bfloat16).astype(jnp.float32)

    attended = rounded(jnp.maximum(even, odd) + projected[0:64])
    even = rounded(attended + even)
    odd = rounded(attended + odd)
    put_rows(wide, 0, even)
    put_rows(wide, 1, odd)
    put_rows(active, 8, gelu(normalize(even, gain)))
    put_rows(active, 9, gelu(normalize(odd, gain)))
    edges = edge_ref[0:4, :]
    low = rounded(jnp.maximum(edges[0:1], edges[1:2]) + projected[64:65])
    high = rounded(jnp.maximum(edges[2:3], edges[3:4]) + projected[65:66])
    joined = rounded(edges + jnp.concatenate([low, low, high, high], axis=0))
    halo = gelu(normalize(joined, gain))
    above = jnp.where(me > 0, halo[0:2], 0.0)
    below = jnp.where(me < lax.axis_size("seq") - 1, halo[2:4], 0.0)
    zeros = jnp.zeros((6, 128), jnp.float32)
    for k in range(12):
        columns = slice(128 * k, 128 * k + 128)
        active[k, 0:8, :] = jnp.concatenate([zeros, above[:, columns]], axis=0)
        active[k, 136:144, :] = jnp.concatenate([below[:, columns], zeros], axis=0)
    for k in range(6):
        keep_ref[:, 128 * k : 128 * k + 128] = active[upper * 6 + k].astype(jnp.bfloat16)
    for k in range(3):
        columns = slice(128 * k, 128 * k + 128)
        send_ref[:, columns] = active[(1 - upper) * 6 + section * 3 + k].astype(jnp.bfloat16)
        base_ref[:, columns] = wide[section * 3 + k] + dec_bias_ref[columns][None, :]


def load_weight(own_ref, remote_refs, weight):
    slot = lax.axis_index("seq") & 3
    group = lax.axis_index("groups")
    for n in range(2 * KW):
        weight[(n // 2) * 8 + 2 * slot + n % 2] = own_ref[n]
    for n, ref in enumerate(remote_refs):
        block = slot ^ (n // 2 + 1)
        first = KW * (group if n % 2 == 0 else 1 - group)
        for k in range(KW):
            chunk = first + k
            weight[(chunk // 2) * 8 + 2 * block + chunk % 2] = ref[k]


def tap_weight(weight, tap, start, size):
    return weight[pl.ds(8 * tap + start, size)].reshape(size * weight.shape[1], weight.shape[2])


def shifted_sum(products):
    total = products[0][6:134]
    for tap in range(1, KW):
        total = total + products[tap][6 + tap : 134 + tap]
    return total


def own_kernel(active_ref, base_ref, w0, w1, w2, w3, w4, w5, w6, out_ref, weight):
    load_weight(w0, (w1, w2, w3, w4, w5, w6), weight)
    active = active_ref[...]
    out_ref[...] = base_ref[...] + shifted_sum(
        [
            jnp.dot(active, tap_weight(weight, t, 0, 8), preferred_element_type=jnp.float32)
            for t in range(KW)
        ]
    )


def partner_kernel(first_ref, second_ref, w0, w1, w2, w3, w4, w5, w6, out_ref, weight):
    load_weight(w0, (w1, w2, w3, w4, w5, w6), weight)
    section = lax.axis_index("section")
    first, second = first_ref[...], second_ref[...]
    near, far = 4 * section, 4 * (1 - section)
    out_ref[...] = shifted_sum(
        [
            jnp.dot(first, tap_weight(weight, t, near, 4), preferred_element_type=jnp.float32)
            + jnp.dot(second, tap_weight(weight, t, far, 4), preferred_element_type=jnp.float32)
            for t in range(KW)
        ]
    ).astype(jnp.bfloat16)


def split_body(
    skip_in, attn_gain, query_weight, kv_weight, pair_bias, out_weight, dec_gain, dec_weight, dec_bias
):
    bf16, f32 = jnp.bfloat16, jnp.float32
    skip = skip_in[0]
    rows, channels = skip.shape
    taps, depth, width = dec_weight.shape
    chunks = dec_weight.reshape(2 * taps, depth // 2, width)
    message, normed, piece = call(
        pool_kernel,
        [((MSG, 256), bf16), ((rows // 2, channels), bf16), ((taps, depth // 2, width), bf16)],
        [
            pltpu.with_memory_space_constraint(values_in, pltpu.HBM)
            for values_in in (skip, attn_gain, kv_weight, pair_bias, chunks)
        ],
        [
            pltpu.VMEM((rows, channels), bf16),
            pltpu.VMEM((channels,), f32),
            pltpu.VMEM(kv_weight.shape, bf16),
            pltpu.VMEM(pair_bias.shape, f32),
            pltpu.VMEM((channels // 128, rows, 128), f32),
            pltpu.VMEM((MSG, 256), f32),
            pltpu.SemaphoreType.DMA((5,)),
        ],
        [pl.BlockSpec(memory_space=pl.ANY)] * 5,
    )
    def joined(values_in, mask):
        count = values_in.shape[0]
        return call(
            join_kernel,
            [((2 * count,) + values_in.shape[1:], bf16)],
            [values_in, exchange(values_in, "seq", mask)],
        )[0]

    def behind(values_in, gate):
        return lax.optimization_barrier((values_in, gate))[0]

    near = joined(message[None], 2)
    side = exchange(piece, "seq", 1)
    after = exchange(behind(piece, near), "seq", 2)
    received, side = lax.optimization_barrier((exchange(near, "seq", 4), side))
    near = call(join_kernel, [((4, MSG, 256), bf16)], [near, received])[0]
    across = exchange(near, "seq", 1)
    near_other = exchange(near, "section", 1)
    side_rest = exchange(side, "groups", 1)
    across_other = exchange(across, "section", 1)
    queries = jnp.dot(normed, query_weight, preferred_element_type=f32).astype(bf16)
    terms, edges = call(
        attention_kernel,
        [((ROWS, channels), bf16), ((8, channels), f32)],
        [queries, near, near_other, across, across_other, query_weight, attn_gain, pair_bias, out_weight],
    )
    terms, after = lax.optimization_barrier((terms, after))
    other = exchange(terms, "section", 1)
    after_rest = exchange(after, "groups", 1)
    far = exchange(after, "seq", 1)
    far_rest = exchange(behind(side_rest, terms), "seq", 2)
    keep, send, base = call(
        activate_kernel,
        [((rows + 16, channels // 2), bf16), ((rows + 16, channels // 4), bf16), ((rows, width), f32)],
        [skip, edges, terms, other, dec_gain, dec_bias],
        [pltpu.VMEM((channels // 128, rows + extra, 128), f32) for extra in (0, 16)],
    )
    first = exchange(send, "seq", 4)
    first, far_rest = lax.optimization_barrier((first, far_rest))
    second = exchange(first, "section", 1)
    weights = [chunks, side, side_rest, after, after_rest, far, far_rest]
    scratch = [pltpu.VMEM((8 * taps, depth // 2, width), bf16)]
    (own,) = call(own_kernel, [((rows, width), f32)], [keep, base] + weights, scratch)
    (partial,) = call(
        partner_kernel, [((rows, width), bf16)], [first, second] + weights, scratch
    )
    decoded = own + exchange(partial, "seq", 4).astype(f32)
    return decoded.astype(bf16)[None]


def solution(mesh):
    return jax.shard_map(
        split_body if mesh.shape["seq"] == 8 else body,
        mesh=mesh,
        in_specs=(
            P("groups", "seq", None),
            P(),
            P(None, "section"),
            P(),
            P("groups", "section", "seq", None),
            P("section", None),
            P(),
            P(None, "seq", "section"),
            P("section"),
        ),
        out_specs=P("groups", "seq", "section"),
        check_vma=False,
    )
```

```python
import math

import jax
import jax.numpy as jnp
from jax import lax
from jax.experimental import pallas as pl
from jax.experimental.pallas import tpu as pltpu
from jax.sharding import PartitionSpec as P

HEAD = 128
KW = 5
PAIR = 16


def extended(block, sides, width):
    for axis, dim in sides:
        count = lax.axis_size(axis)
        forward = [(i, i + 1) for i in range(count - 1)]
        backward = [(target, source) for source, target in forward]
        low = lax.ppermute(
            lax.slice_in_dim(block, block.shape[dim] - width, None, axis=dim), axis, forward
        )
        high = lax.ppermute(lax.slice_in_dim(block, 0, width, axis=dim), axis, backward)
        block = jnp.concatenate([low, block, high], axis=dim)
    return block


def norm_scale(values_in, gain):
    wide = values_in.astype(jnp.float32)
    return wide * lax.rsqrt(jnp.mean(wide * wide, axis=-1, keepdims=True) + 1e-06) * gain


def body(
    skip_in,
    attn_gain,
    query_weight,
    kv_weight,
    pair_bias,
    out_weight,
    dec_gain,
    dec_weight,
    dec_bias,
):
    seq_count, local_rows, channels = skip_in.shape
    half_rows = local_rows // 2
    local_heads = query_weight.shape[1] // HEAD
    logit_scale = 1.0 / math.sqrt(HEAD)
    pooled = jnp.max(skip_in.reshape(seq_count, half_rows, 2, channels), axis=2)
    normed = norm_scale(pooled, attn_gain).astype(jnp.bfloat16)
    flattened = normed.reshape(seq_count * half_rows, channels)
    query_rows = jnp.dot(flattened, query_weight, preferred_element_type=jnp.float32).astype(
        jnp.bfloat16
    )
    query_rows = query_rows.reshape(seq_count, half_rows, local_heads, HEAD)
    row_bias = jnp.repeat(pair_bias, PAIR, axis=2)
    row_bias = jnp.pad(row_bias, ((0, 0), (0, 0), (0, 0), (0, 2)))
    quarter = half_rows // 2
    own_rows = lax.dynamic_slice_in_dim(normed, lax.axis_index("section") * quarter, quarter, 1)
    key_values = jnp.dot(
        own_rows.reshape(seq_count * quarter, channels),
        kv_weight,
        preferred_element_type=jnp.float32,
    )
    key_values = key_values.astype(jnp.bfloat16).reshape(seq_count, quarter, 2 * HEAD)
    piece = lax.all_gather(key_values, ("seq", "section"), axis=1, tiled=True)
    start = jnp.int32(0)
    running_max = jnp.full((seq_count, local_heads, half_rows), -1e30, jnp.float32)
    running_sum = jnp.zeros((seq_count, local_heads, half_rows), jnp.float32)
    weighted = jnp.zeros((seq_count, local_heads, half_rows, HEAD), jnp.float32)
    piece_rows = piece.shape[1]
    block_size = min(piece_rows, 2048)
    for offset in range(0, piece_rows, block_size):
        piece_len = min(block_size, piece_rows - offset)
        sub_piece = piece[:, offset : offset + piece_len]
        key_portion = sub_piece[:, :, :HEAD]
        value_part = sub_piece[:, :, HEAD:]
        first_row = start + offset
        blocks = lax.dynamic_slice_in_dim(row_bias, first_row // PAIR, piece_len // PAIR + 2, 3)
        spread = jnp.repeat(blocks, PAIR, axis=3)
        key_bias = lax.dynamic_slice_in_dim(spread, first_row % PAIR, piece_len, 3)
        scores = (
            jnp.einsum(
                "wtzj,wgj->wztg", query_rows, key_portion, preferred_element_type=jnp.float32
            )
            * logit_scale
            + key_bias
        )
        new_max = jnp.maximum(running_max, jnp.max(scores, axis=-1))
        rescale = jnp.exp(running_max - new_max)
        exponent_scores = jnp.exp(scores - new_max[..., None])
        running_sum = running_sum * rescale + jnp.sum(exponent_scores, axis=-1)
        weighted = weighted * rescale[..., None] + jnp.einsum(
            "umrl,ult->umrt",
            exponent_scores.astype(jnp.bfloat16),
            value_part,
            preferred_element_type=jnp.float32,
        )
        running_max = new_max
    folded = (running_max, running_sum, weighted)
    running_max, running_sum, weighted = folded
    context = (weighted / running_sum[..., None]).astype(jnp.bfloat16)
    context = jnp.transpose(context, (0, 2, 1, 3)).reshape(
        seq_count * half_rows, local_heads * HEAD
    )
    partial_value = jnp.dot(context, out_weight, preferred_element_type=jnp.float32).reshape(
        seq_count, half_rows, channels
    )
    summed = lax.psum(partial_value.astype(jnp.bfloat16), "section").astype(jnp.float32)
    attended = (pooled.astype(jnp.float32) + summed).astype(jnp.bfloat16)
    joined = (
        jnp.repeat(attended, 2, axis=1).astype(jnp.float32) + skip_in.astype(jnp.float32)
    ).astype(jnp.bfloat16)
    activated = jax.nn.gelu(norm_scale(joined, dec_gain)).astype(jnp.bfloat16)
    padded = extended(activated, (("seq", 1),), KW // 2)
    out_half = dec_weight.shape[2]
    piece = lax.all_gather(dec_weight, "seq", axis=1, tiled=True)
    piece_rows = piece.shape[1]
    stacked = jnp.concatenate(
        [padded[:, tap_index : tap_index + local_rows] for tap_index in range(KW)], axis=2
    )
    stacked = stacked.reshape(seq_count * local_rows, KW * piece_rows)
    convolved = jnp.dot(
        stacked, piece.reshape(KW * piece_rows, out_half), preferred_element_type=jnp.float32
    )
    residual = lax.dynamic_slice_in_dim(joined, lax.axis_index("section") * out_half, out_half, 2)
    decoded = (
        convolved.reshape(seq_count, local_rows, out_half) + dec_bias + residual.astype(jnp.float32)
    )
    return decoded.astype(jnp.bfloat16)


ROWS = 80
MSG = 48
LIMIT = 24 * 1024 * 1024


def exchange(values_in, axis, mask):
    count = lax.axis_size(axis)
    return lax.ppermute(values_in, axis, [(i, i ^ mask) for i in range(count)])


def call(kernel, outs, args, scratch=(), spaces=None, limit=LIMIT):
    vmem = pl.BlockSpec(memory_space=pltpu.VMEM)
    return pl.pallas_call(
        kernel,
        out_shape=[jax.ShapeDtypeStruct(shape, kind) for shape, kind in outs],
        in_specs=[vmem] * len(args) if spaces is None else spaces,
        out_specs=[vmem] * len(outs),
        scratch_shapes=list(scratch),
        compiler_params=pltpu.CompilerParams(vmem_limit_bytes=limit),
    )(*args)


def split_three(wide):
    high = wide.astype(jnp.bfloat16)
    rest = wide - high.astype(jnp.float32)
    middle = rest.astype(jnp.bfloat16)
    low = (rest - middle.astype(jnp.float32)).astype(jnp.bfloat16)
    return high, middle, low


def own_bias(bias_ref):
    return jnp.concatenate([bias_ref[0, h] for h in range(4)], axis=0)


def normalize(wide, gain):
    return wide * lax.rsqrt(jnp.mean(wide * wide, axis=-1, keepdims=True) + 1e-06) * gain


def gelu(wide):
    inner = math.sqrt(2.0 / math.pi) * (wide + 0.044715 * (wide * wide * wide))
    return 0.5 * wide * (1.0 + jnp.tanh(inner))


def spread_columns(wide, values_in):
    for k in range(wide.shape[0]):
        wide[k] = values_in[:, 128 * k : 128 * k + 128].astype(jnp.float32)


def take_rows(wide, start, size):
    return jnp.concatenate(
        [wide[k, pl.ds(start, size, stride=2), :] for k in range(wide.shape[0])], axis=1
    )


def put_rows(wide, start, values_in):
    for k in range(wide.shape[0]):
        wide[k, pl.ds(start, values_in.shape[0], stride=2), :] = values_in[:, 128 * k : 128 * k + 128]


def pool_kernel(
    skip_hbm,
    gain_hbm,
    weight_hbm,
    bias_hbm,
    dec_hbm,
    message_ref,
    normed_ref,
    piece_ref,
    skip_ref,
    gain_ref,
    weight_ref,
    bias_ref,
    wide,
    lines,
    semaphores,
):
    group = lax.axis_index("groups")
    pieces = dec_hbm.shape[0] // 2
    pairs = (
        (skip_hbm, skip_ref),
        (gain_hbm, gain_ref),
        (bias_hbm, bias_ref),
        (weight_hbm, weight_ref),
        (dec_hbm.at[pl.ds(group * pieces, pieces)], piece_ref),
    )
    copies = [
        pltpu.make_async_copy(source, target, semaphores.at[n])
        for n, (source, target) in enumerate(pairs)
    ]
    for copy in copies:
        copy.start()
    for copy in copies[:3]:
        copy.wait()
    section = lax.axis_index("section")
    half = skip_ref.shape[0] // 2
    quarter = half // 2
    spread_columns(wide, skip_ref)
    pooled = jnp.maximum(take_rows(wide, 0, half), take_rows(wide, 1, half))
    normed_ref[...] = normalize(pooled, gain_ref[...][None, :]).astype(jnp.bfloat16)
    copies[3].wait()
    own = normed_ref[pl.ds(pl.multiple_of(section * quarter, 16), quarter), :]
    lines[0:quarter, :] = jnp.dot(own, weight_ref[...], preferred_element_type=jnp.float32)
    for n in range(2):
        row = section * (skip_ref.shape[0] - 2) + n
        for k in range(12):
            at = quarter + 6 * n + k // 2
            lines[at : at + 1, 128 * (k % 2) : 128 * (k % 2) + 128] = wide[k, pl.ds(row, 1), :]
    terms = [term.astype(jnp.float32) for term in split_three(own_bias(bias_ref))]
    packed = [
        jnp.concatenate(
            [term[4 * h + cell : 4 * h + cell + 1, :] for cell in (0, 3) for h in range(4)], axis=1
        )
        for term in terms
    ]
    lines[MSG - 4 : MSG, :] = jnp.concatenate(packed + [jnp.zeros((1, 256), jnp.float32)], axis=0)
    message_ref[...] = lines[...].astype(jnp.bfloat16)
    copies[4].wait()


def join_kernel(first_ref, second_ref, out_ref):
    count = first_ref.shape[0]
    out_ref[0:count] = first_ref[...]
    out_ref[count:] = second_ref[...]


def slot_of(distance):
    return distance // 2 + 4 * (distance & 1)


def distance_of(slot):
    return 2 * (slot & 3) + slot // 4


def attention_kernel(
    query_ref,
    near_ref,
    near_other_ref,
    side_ref,
    side_other_ref,
    query_weight_ref,
    gain_ref,
    bias_ref,
    out_weight_ref,
    terms_ref,
    edge_ref,
):
    me = lax.axis_index("seq")
    section = lax.axis_index("section")
    count = lax.axis_size("seq")
    low_slot = slot_of(me ^ jnp.maximum(me - 1, 0))
    high_slot = slot_of(me ^ jnp.minimum(me + 1, count - 1))

    def block_of(slot, near, side):
        return jnp.where(
            slot < 4, near[slot & 3].astype(jnp.float32), side[slot & 3].astype(jnp.float32)
        )

    low, high = (block_of(slot, near_ref, side_ref) for slot in (low_slot, high_slot))
    low_edge = jnp.where(section == 1, low, block_of(low_slot, near_other_ref, side_other_ref))
    high_edge = jnp.where(section == 0, high, block_of(high_slot, near_other_ref, side_other_ref))

    def line(block, row):
        start = 32 + 6 * row
        return jnp.concatenate([block[start + k : start + k + 1, :] for k in range(6)], axis=1)

    edges = jnp.concatenate(
        [line(low_edge, 0), line(low_edge, 1), line(high_edge, 0), line(high_edge, 1)], axis=0
    )
    edge_ref[0:4, :] = edges
    edge_ref[4:8, :] = jnp.zeros_like(edges)
    pooled = jnp.concatenate(
        [
            jnp.maximum(edges[0:1], edges[1:2]),
            jnp.maximum(edges[2:3], edges[3:4]),
            jnp.zeros((14, edges.shape[1]), jnp.float32),
        ],
        axis=0,
    )
    normed = normalize(pooled, gain_ref[...][None, :]).astype(jnp.bfloat16)
    halo_query = jnp.dot(normed, query_weight_ref[...], preferred_element_type=jnp.float32)
    queries = jnp.concatenate([query_ref[...], halo_query.astype(jnp.bfloat16)], axis=0)
    pieces = []
    for mine, others in ((near_ref, near_other_ref), (side_ref, side_other_ref)):
        for k in range(4):
            pieces += [mine[k, 0:32, :], others[k, 0:32, :]]
    keys = jnp.concatenate([piece[:, 0:HEAD] for piece in pieces], axis=0)
    values = jnp.concatenate([piece[:, HEAD : 2 * HEAD] for piece in pieces], axis=0)
    cell = lax.broadcasted_iota(jnp.int32, (32, 512), 0)
    column = lax.broadcasted_iota(jnp.int32, (32, 512), 1)
    inner = 2 * (((column >> 5) & 1) ^ section) + ((column & 31) >> 4)
    wanted = 4 * (distance_of(column >> 6) ^ me) + inner
    spread = jnp.where(cell == wanted, 1.0, 0.0).astype(jnp.bfloat16)
    bias = jnp.zeros((24, 512), jnp.float32)
    for n, term in enumerate(split_three(own_bias(bias_ref))):
        at = MSG - 4 + n
        rows = [low[at : at + 1, 128 + 32 * h : 160 + 32 * h] for h in range(4)]
        rows += [high[at : at + 1, 32 * h : 32 * h + 32] for h in range(4)]
        table = jnp.concatenate([term.astype(jnp.float32)] + rows, axis=0).astype(jnp.bfloat16)
        bias = bias + jnp.dot(table, spread, preferred_element_type=jnp.float32)
    first = lax.broadcasted_iota(jnp.int32, (16, 512), 0) == 0
    parts = []
    for h in range(4):
        scores = lax.dot_general(
            queries[:, h * HEAD : (h + 1) * HEAD],
            keys,
            (((1,), (1,)), ((), ())),
            preferred_element_type=jnp.float32,
        )
        rows = [jnp.broadcast_to(bias[4 * h + r : 4 * h + r + 1, :], (16, 512)) for r in range(4)]
        rows.append(
            jnp.where(first, bias[16 + h : 17 + h, :], bias[20 + h : 21 + h, :])
        )
        scores = scores * (1.0 / math.sqrt(HEAD)) + jnp.concatenate(rows, axis=0)
        exps = jnp.exp(scores - jnp.max(scores, axis=-1, keepdims=True))
        totals = jnp.sum(exps, axis=-1, keepdims=True)
        mixed = jnp.dot(exps.astype(jnp.bfloat16), values, preferred_element_type=jnp.float32)
        parts.append((mixed / totals).astype(jnp.bfloat16))
    context = jnp.concatenate(parts, axis=1)
    terms_ref[...] = jnp.dot(
        context, out_weight_ref[...], preferred_element_type=jnp.float32
    ).astype(jnp.bfloat16)


def activate_kernel(
    skip_ref, edge_ref, own_ref, other_ref, gain_ref, dec_bias_ref, keep_ref, send_ref, base_ref, wide, active
):
    me = lax.axis_index("seq")
    section = lax.axis_index("section")
    upper = me >> 2
    gain = gain_ref[...][None, :]
    spread_columns(wide, skip_ref)
    even = take_rows(wide, 0, 64)
    odd = take_rows(wide, 1, 64)
    projected = own_ref[...].astype(jnp.float32) + other_ref[...].astype(jnp.float32)

    def rounded(values_in):
        return values_in.astype(jnp.bfloat16).astype(jnp.float32)

    attended = rounded(jnp.maximum(even, odd) + projected[0:64])
    even = rounded(attended + even)
    odd = rounded(attended + odd)
    put_rows(wide, 0, even)
    put_rows(wide, 1, odd)
    put_rows(active, 8, gelu(normalize(even, gain)))
    put_rows(active, 9, gelu(normalize(odd, gain)))
    edges = edge_ref[0:4, :]
    low = rounded(jnp.maximum(edges[0:1], edges[1:2]) + projected[64:65])
    high = rounded(jnp.maximum(edges[2:3], edges[3:4]) + projected[65:66])
    joined = rounded(edges + jnp.concatenate([low, low, high, high], axis=0))
    halo = gelu(normalize(joined, gain))
    above = jnp.where(me > 0, halo[0:2], 0.0)
    below = jnp.where(me < lax.axis_size("seq") - 1, halo[2:4], 0.0)
    zeros = jnp.zeros((6, 128), jnp.float32)
    for k in range(12):
        columns = slice(128 * k, 128 * k + 128)
        active[k, 0:8, :] = jnp.concatenate([zeros, above[:, columns]], axis=0)
        active[k, 136:144, :] = jnp.concatenate([below[:, columns], zeros], axis=0)
    for k in range(6):
        keep_ref[:, 128 * k : 128 * k + 128] = active[upper * 6 + k].astype(jnp.bfloat16)
    for k in range(3):
        columns = slice(128 * k, 128 * k + 128)
        send_ref[:, columns] = active[(1 - upper) * 6 + section * 3 + k].astype(jnp.bfloat16)
        base_ref[:, columns] = wide[section * 3 + k] + dec_bias_ref[columns][None, :]


def load_weight(own_ref, remote_refs, weight):
    slot = lax.axis_index("seq") & 3
    group = lax.axis_index("groups")
    for n in range(2 * KW):
        weight[(n // 2) * 8 + 2 * slot + n % 2] = own_ref[n]
    for n, ref in enumerate(remote_refs):
        block = slot ^ (n // 2 + 1)
        first = KW * (group if n % 2 == 0 else 1 - group)
        for k in range(KW):
            chunk = first + k
            weight[(chunk // 2) * 8 + 2 * block + chunk % 2] = ref[k]


def tap_weight(weight, tap, start, size):
    return weight[pl.ds(8 * tap + start, size)].reshape(size * weight.shape[1], weight.shape[2])


def shifted_sum(products):
    total = products[0][6:134]
    for tap in range(1, KW):
        total = total + products[tap][6 + tap : 134 + tap]
    return total


def own_kernel(active_ref, base_ref, w0, w1, w2, w3, w4, w5, w6, out_ref, weight):
    load_weight(w0, (w1, w2, w3, w4, w5, w6), weight)
    active = active_ref[...]
    out_ref[...] = base_ref[...] + shifted_sum(
        [
            jnp.dot(active, tap_weight(weight, t, 0, 8), preferred_element_type=jnp.float32)
            for t in range(KW)
        ]
    )


def partner_kernel(first_ref, second_ref, w0, w1, w2, w3, w4, w5, w6, out_ref, weight):
    load_weight(w0, (w1, w2, w3, w4, w5, w6), weight)
    section = lax.axis_index("section")
    first, second = first_ref[...], second_ref[...]
    near, far = 4 * section, 4 * (1 - section)
    out_ref[...] = shifted_sum(
        [
            jnp.dot(first, tap_weight(weight, t, near, 4), preferred_element_type=jnp.float32)
            + jnp.dot(second, tap_weight(weight, t, far, 4), preferred_element_type=jnp.float32)
            for t in range(KW)
        ]
    ).astype(jnp.bfloat16)


def split_body(
    skip_in, attn_gain, query_weight, kv_weight, pair_bias, out_weight, dec_gain, dec_weight, dec_bias
):
    bf16, f32 = jnp.bfloat16, jnp.float32
    skip = skip_in[0]
    rows, channels = skip.shape
    taps, depth, width = dec_weight.shape
    chunks = dec_weight.reshape(2 * taps, depth // 2, width)
    message, normed, piece = call(
        pool_kernel,
        [((MSG, 256), bf16), ((rows // 2, channels), bf16), ((taps, depth // 2, width), bf16)],
        [
            pltpu.with_memory_space_constraint(values_in, pltpu.HBM)
            for values_in in (skip, attn_gain, kv_weight, pair_bias, chunks)
        ],
        [
            pltpu.VMEM((rows, channels), bf16),
            pltpu.VMEM((channels,), f32),
            pltpu.VMEM(kv_weight.shape, bf16),
            pltpu.VMEM(pair_bias.shape, f32),
            pltpu.VMEM((channels // 128, rows, 128), f32),
            pltpu.VMEM((MSG, 256), f32),
            pltpu.SemaphoreType.DMA((5,)),
        ],
        [pl.BlockSpec(memory_space=pl.ANY)] * 5,
    )
    def joined(values_in, mask):
        count = values_in.shape[0]
        return call(
            join_kernel,
            [((2 * count,) + values_in.shape[1:], bf16)],
            [values_in, exchange(values_in, "seq", mask)],
        )[0]

    def behind(values_in, gate):
        return lax.optimization_barrier((values_in, gate))[0]

    near = joined(message[None], 2)
    side = exchange(piece, "seq", 1)
    after = exchange(behind(piece, near), "seq", 2)
    near = joined(near, 4)
    across = exchange(near, "seq", 1)
    held, side = lax.optimization_barrier((near, side))
    near_other = exchange(held, "section", 1)
    side_rest = exchange(side, "groups", 1)
    across_other = exchange(across, "section", 1)
    queries = jnp.dot(normed, query_weight, preferred_element_type=f32).astype(bf16)
    terms, edges = call(
        attention_kernel,
        [((ROWS, channels), bf16), ((8, channels), f32)],
        [queries, near, near_other, across, across_other, query_weight, attn_gain, pair_bias, out_weight],
    )
    terms, after = lax.optimization_barrier((terms, after))
    other = exchange(terms, "section", 1)
    after_rest = exchange(after, "groups", 1)
    far = exchange(after, "seq", 1)
    far_rest = exchange(behind(side_rest, terms), "seq", 2)
    keep, send, base = call(
        activate_kernel,
        [((rows + 16, channels // 2), bf16), ((rows + 16, channels // 4), bf16), ((rows, width), f32)],
        [skip, edges, terms, other, dec_gain, dec_bias],
        [pltpu.VMEM((channels // 128, rows + extra, 128), f32) for extra in (0, 16)],
    )
    first = exchange(send, "seq", 4)
    first, far, far_rest = lax.optimization_barrier((first, far, far_rest))
    second = exchange(first, "section", 1)
    weights = [chunks, side, side_rest, after, after_rest, far, far_rest]
    scratch = [pltpu.VMEM((8 * taps, depth // 2, width), bf16)]
    (own,) = call(own_kernel, [((rows, width), f32)], [keep, base] + weights, scratch)
    (partial,) = call(
        partner_kernel, [((rows, width), bf16)], [first, second] + weights, scratch
    )
    decoded = own + exchange(partial, "seq", 4).astype(f32)
    return decoded.astype(bf16)[None]


def solution(mesh):
    return jax.shard_map(
        split_body if mesh.shape["seq"] == 8 else body,
        mesh=mesh,
        in_specs=(
            P("groups", "seq", None),
            P(),
            P(None, "section"),
            P(),
            P("groups", "section", "seq", None),
            P("section", None),
            P(),
            P(None, "seq", "section"),
            P("section"),
        ),
        out_specs=P("groups", "seq", "section"),
        check_vma=False,
    )
```

```python
import math

import jax
import jax.numpy as jnp
from jax import lax
from jax.experimental import pallas as pl
from jax.experimental.pallas import tpu as pltpu
from jax.sharding import PartitionSpec as P

HEAD = 128
KW = 5
PAIR = 16


def extended(block, sides, width):
    for axis, dim in sides:
        count = lax.axis_size(axis)
        forward = [(i, i + 1) for i in range(count - 1)]
        backward = [(target, source) for source, target in forward]
        low = lax.ppermute(
            lax.slice_in_dim(block, block.shape[dim] - width, None, axis=dim), axis, forward
        )
        high = lax.ppermute(lax.slice_in_dim(block, 0, width, axis=dim), axis, backward)
        block = jnp.concatenate([low, block, high], axis=dim)
    return block


def norm_scale(values_in, gain):
    wide = values_in.astype(jnp.float32)
    return wide * lax.rsqrt(jnp.mean(wide * wide, axis=-1, keepdims=True) + 1e-06) * gain


def body(
    skip_in,
    attn_gain,
    query_weight,
    kv_weight,
    pair_bias,
    out_weight,
    dec_gain,
    dec_weight,
    dec_bias,
):
    seq_count, local_rows, channels = skip_in.shape
    half_rows = local_rows // 2
    local_heads = query_weight.shape[1] // HEAD
    logit_scale = 1.0 / math.sqrt(HEAD)
    pooled = jnp.max(skip_in.reshape(seq_count, half_rows, 2, channels), axis=2)
    normed = norm_scale(pooled, attn_gain).astype(jnp.bfloat16)
    flattened = normed.reshape(seq_count * half_rows, channels)
    query_rows = jnp.dot(flattened, query_weight, preferred_element_type=jnp.float32).astype(
        jnp.bfloat16
    )
    query_rows = query_rows.reshape(seq_count, half_rows, local_heads, HEAD)
    row_bias = jnp.repeat(pair_bias, PAIR, axis=2)
    row_bias = jnp.pad(row_bias, ((0, 0), (0, 0), (0, 0), (0, 2)))
    quarter = half_rows // 2
    own_rows = lax.dynamic_slice_in_dim(normed, lax.axis_index("section") * quarter, quarter, 1)
    key_values = jnp.dot(
        own_rows.reshape(seq_count * quarter, channels),
        kv_weight,
        preferred_element_type=jnp.float32,
    )
    key_values = key_values.astype(jnp.bfloat16).reshape(seq_count, quarter, 2 * HEAD)
    piece = lax.all_gather(key_values, ("seq", "section"), axis=1, tiled=True)
    start = jnp.int32(0)
    running_max = jnp.full((seq_count, local_heads, half_rows), -1e30, jnp.float32)
    running_sum = jnp.zeros((seq_count, local_heads, half_rows), jnp.float32)
    weighted = jnp.zeros((seq_count, local_heads, half_rows, HEAD), jnp.float32)
    piece_rows = piece.shape[1]
    block_size = min(piece_rows, 2048)
    for offset in range(0, piece_rows, block_size):
        piece_len = min(block_size, piece_rows - offset)
        sub_piece = piece[:, offset : offset + piece_len]
        key_portion = sub_piece[:, :, :HEAD]
        value_part = sub_piece[:, :, HEAD:]
        first_row = start + offset
        blocks = lax.dynamic_slice_in_dim(row_bias, first_row // PAIR, piece_len // PAIR + 2, 3)
        spread = jnp.repeat(blocks, PAIR, axis=3)
        key_bias = lax.dynamic_slice_in_dim(spread, first_row % PAIR, piece_len, 3)
        scores = (
            jnp.einsum(
                "wtzj,wgj->wztg", query_rows, key_portion, preferred_element_type=jnp.float32
            )
            * logit_scale
            + key_bias
        )
        new_max = jnp.maximum(running_max, jnp.max(scores, axis=-1))
        rescale = jnp.exp(running_max - new_max)
        exponent_scores = jnp.exp(scores - new_max[..., None])
        running_sum = running_sum * rescale + jnp.sum(exponent_scores, axis=-1)
        weighted = weighted * rescale[..., None] + jnp.einsum(
            "umrl,ult->umrt",
            exponent_scores.astype(jnp.bfloat16),
            value_part,
            preferred_element_type=jnp.float32,
        )
        running_max = new_max
    folded = (running_max, running_sum, weighted)
    running_max, running_sum, weighted = folded
    context = (weighted / running_sum[..., None]).astype(jnp.bfloat16)
    context = jnp.transpose(context, (0, 2, 1, 3)).reshape(
        seq_count * half_rows, local_heads * HEAD
    )
    partial_value = jnp.dot(context, out_weight, preferred_element_type=jnp.float32).reshape(
        seq_count, half_rows, channels
    )
    summed = lax.psum(partial_value.astype(jnp.bfloat16), "section").astype(jnp.float32)
    attended = (pooled.astype(jnp.float32) + summed).astype(jnp.bfloat16)
    joined = (
        jnp.repeat(attended, 2, axis=1).astype(jnp.float32) + skip_in.astype(jnp.float32)
    ).astype(jnp.bfloat16)
    activated = jax.nn.gelu(norm_scale(joined, dec_gain)).astype(jnp.bfloat16)
    padded = extended(activated, (("seq", 1),), KW // 2)
    out_half = dec_weight.shape[2]
    piece = lax.all_gather(dec_weight, "seq", axis=1, tiled=True)
    piece_rows = piece.shape[1]
    stacked = jnp.concatenate(
        [padded[:, tap_index : tap_index + local_rows] for tap_index in range(KW)], axis=2
    )
    stacked = stacked.reshape(seq_count * local_rows, KW * piece_rows)
    convolved = jnp.dot(
        stacked, piece.reshape(KW * piece_rows, out_half), preferred_element_type=jnp.float32
    )
    residual = lax.dynamic_slice_in_dim(joined, lax.axis_index("section") * out_half, out_half, 2)
    decoded = (
        convolved.reshape(seq_count, local_rows, out_half) + dec_bias + residual.astype(jnp.float32)
    )
    return decoded.astype(jnp.bfloat16)


ROWS = 80
MSG = 48
LIMIT = 24 * 1024 * 1024


def exchange(values_in, axis, mask):
    count = lax.axis_size(axis)
    return lax.ppermute(values_in, axis, [(i, i ^ mask) for i in range(count)])


def call(kernel, outs, args, scratch=(), spaces=None, limit=LIMIT):
    vmem = pl.BlockSpec(memory_space=pltpu.VMEM)
    return pl.pallas_call(
        kernel,
        out_shape=[jax.ShapeDtypeStruct(shape, kind) for shape, kind in outs],
        in_specs=[vmem] * len(args) if spaces is None else spaces,
        out_specs=[vmem] * len(outs),
        scratch_shapes=list(scratch),
        compiler_params=pltpu.CompilerParams(vmem_limit_bytes=limit),
    )(*args)


def split_three(wide):
    high = wide.astype(jnp.bfloat16)
    rest = wide - high.astype(jnp.float32)
    middle = rest.astype(jnp.bfloat16)
    low = (rest - middle.astype(jnp.float32)).astype(jnp.bfloat16)
    return high, middle, low


def own_bias(bias_ref):
    return jnp.concatenate([bias_ref[0, h] for h in range(4)], axis=0)


def normalize(wide, gain):
    return wide * lax.rsqrt(jnp.mean(wide * wide, axis=-1, keepdims=True) + 1e-06) * gain


def gelu(wide):
    inner = math.sqrt(2.0 / math.pi) * (wide + 0.044715 * (wide * wide * wide))
    return 0.5 * wide * (1.0 + jnp.tanh(inner))


def spread_columns(wide, values_in):
    for k in range(wide.shape[0]):
        wide[k] = values_in[:, 128 * k : 128 * k + 128].astype(jnp.float32)


def take_rows(wide, start, size):
    return jnp.concatenate(
        [wide[k, pl.ds(start, size, stride=2), :] for k in range(wide.shape[0])], axis=1
    )


def put_rows(wide, start, values_in):
    for k in range(wide.shape[0]):
        wide[k, pl.ds(start, values_in.shape[0], stride=2), :] = values_in[:, 128 * k : 128 * k + 128]


def pool_kernel(
    skip_hbm,
    gain_hbm,
    weight_hbm,
    bias_hbm,
    dec_hbm,
    message_ref,
    normed_ref,
    piece_ref,
    skip_ref,
    gain_ref,
    weight_ref,
    bias_ref,
    wide,
    lines,
    semaphores,
):
    group = lax.axis_index("groups")
    pieces = dec_hbm.shape[0] // 2
    pairs = (
        (skip_hbm, skip_ref),
        (gain_hbm, gain_ref),
        (bias_hbm, bias_ref),
        (weight_hbm, weight_ref),
        (dec_hbm.at[pl.ds(group * pieces, pieces)], piece_ref),
    )
    copies = [
        pltpu.make_async_copy(source, target, semaphores.at[n])
        for n, (source, target) in enumerate(pairs)
    ]
    for copy in copies:
        copy.start()
    for copy in copies[:3]:
        copy.wait()
    section = lax.axis_index("section")
    half = skip_ref.shape[0] // 2
    quarter = half // 2
    spread_columns(wide, skip_ref)
    pooled = jnp.maximum(take_rows(wide, 0, half), take_rows(wide, 1, half))
    normed_ref[...] = normalize(pooled, gain_ref[...][None, :]).astype(jnp.bfloat16)
    copies[3].wait()
    own = normed_ref[pl.ds(pl.multiple_of(section * quarter, 16), quarter), :]
    lines[0:quarter, :] = jnp.dot(own, weight_ref[...], preferred_element_type=jnp.float32)
    for n in range(2):
        row = section * (skip_ref.shape[0] - 2) + n
        for k in range(12):
            at = quarter + 6 * n + k // 2
            lines[at : at + 1, 128 * (k % 2) : 128 * (k % 2) + 128] = wide[k, pl.ds(row, 1), :]
    terms = [term.astype(jnp.float32) for term in split_three(own_bias(bias_ref))]
    packed = [
        jnp.concatenate(
            [term[4 * h + cell : 4 * h + cell + 1, :] for cell in (0, 3) for h in range(4)], axis=1
        )
        for term in terms
    ]
    lines[MSG - 4 : MSG, :] = jnp.concatenate(packed + [jnp.zeros((1, 256), jnp.float32)], axis=0)
    message_ref[...] = lines[...].astype(jnp.bfloat16)
    copies[4].wait()


def join_kernel(first_ref, second_ref, out_ref):
    count = first_ref.shape[0]
    out_ref[0:count] = first_ref[...]
    out_ref[count:] = second_ref[...]


def slot_of(distance):
    return distance // 2 + 4 * (distance & 1)


def distance_of(slot):
    return 2 * (slot & 3) + slot // 4


def attention_kernel(
    query_ref,
    near_ref,
    near_other_ref,
    side_ref,
    side_other_ref,
    query_weight_ref,
    gain_ref,
    bias_ref,
    out_weight_ref,
    terms_ref,
    edge_ref,
):
    me = lax.axis_index("seq")
    section = lax.axis_index("section")
    count = lax.axis_size("seq")
    low_slot = slot_of(me ^ jnp.maximum(me - 1, 0))
    high_slot = slot_of(me ^ jnp.minimum(me + 1, count - 1))

    def block_of(slot, near, side):
        return jnp.where(
            slot < 4, near[slot & 3].astype(jnp.float32), side[slot & 3].astype(jnp.float32)
        )

    low, high = (block_of(slot, near_ref, side_ref) for slot in (low_slot, high_slot))
    low_edge = jnp.where(section == 1, low, block_of(low_slot, near_other_ref, side_other_ref))
    high_edge = jnp.where(section == 0, high, block_of(high_slot, near_other_ref, side_other_ref))

    def line(block, row):
        start = 32 + 6 * row
        return jnp.concatenate([block[start + k : start + k + 1, :] for k in range(6)], axis=1)

    edges = jnp.concatenate(
        [line(low_edge, 0), line(low_edge, 1), line(high_edge, 0), line(high_edge, 1)], axis=0
    )
    edge_ref[0:4, :] = edges
    edge_ref[4:8, :] = jnp.zeros_like(edges)
    pooled = jnp.concatenate(
        [
            jnp.maximum(edges[0:1], edges[1:2]),
            jnp.maximum(edges[2:3], edges[3:4]),
            jnp.zeros((14, edges.shape[1]), jnp.float32),
        ],
        axis=0,
    )
    normed = normalize(pooled, gain_ref[...][None, :]).astype(jnp.bfloat16)
    halo_query = jnp.dot(normed, query_weight_ref[...], preferred_element_type=jnp.float32)
    queries = jnp.concatenate([query_ref[...], halo_query.astype(jnp.bfloat16)], axis=0)
    pieces = []
    for mine, others in ((near_ref, near_other_ref), (side_ref, side_other_ref)):
        for k in range(4):
            pieces += [mine[k, 0:32, :], others[k, 0:32, :]]
    keys = jnp.concatenate([piece[:, 0:HEAD] for piece in pieces], axis=0)
    values = jnp.concatenate([piece[:, HEAD : 2 * HEAD] for piece in pieces], axis=0)
    cell = lax.broadcasted_iota(jnp.int32, (32, 512), 0)
    column = lax.broadcasted_iota(jnp.int32, (32, 512), 1)
    inner = 2 * (((column >> 5) & 1) ^ section) + ((column & 31) >> 4)
    wanted = 4 * (distance_of(column >> 6) ^ me) + inner
    spread = jnp.where(cell == wanted, 1.0, 0.0).astype(jnp.bfloat16)
    bias = jnp.zeros((24, 512), jnp.float32)
    for n, term in enumerate(split_three(own_bias(bias_ref))):
        at = MSG - 4 + n
        rows = [low[at : at + 1, 128 + 32 * h : 160 + 32 * h] for h in range(4)]
        rows += [high[at : at + 1, 32 * h : 32 * h + 32] for h in range(4)]
        table = jnp.concatenate([term.astype(jnp.float32)] + rows, axis=0).astype(jnp.bfloat16)
        bias = bias + jnp.dot(table, spread, preferred_element_type=jnp.float32)
    first = lax.broadcasted_iota(jnp.int32, (16, 512), 0) == 0
    parts = []
    for h in range(4):
        scores = lax.dot_general(
            queries[:, h * HEAD : (h + 1) * HEAD],
            keys,
            (((1,), (1,)), ((), ())),
            preferred_element_type=jnp.float32,
        )
        rows = [jnp.broadcast_to(bias[4 * h + r : 4 * h + r + 1, :], (16, 512)) for r in range(4)]
        rows.append(
            jnp.where(first, bias[16 + h : 17 + h, :], bias[20 + h : 21 + h, :])
        )
        scores = scores * (1.0 / math.sqrt(HEAD)) + jnp.concatenate(rows, axis=0)
        exps = jnp.exp(scores - jnp.max(scores, axis=-1, keepdims=True))
        totals = jnp.sum(exps, axis=-1, keepdims=True)
        mixed = jnp.dot(exps.astype(jnp.bfloat16), values, preferred_element_type=jnp.float32)
        parts.append((mixed / totals).astype(jnp.bfloat16))
    context = jnp.concatenate(parts, axis=1)
    terms_ref[...] = jnp.dot(
        context, out_weight_ref[...], preferred_element_type=jnp.float32
    ).astype(jnp.bfloat16)


def activate_kernel(
    skip_ref, edge_ref, own_ref, other_ref, gain_ref, dec_bias_ref, keep_ref, send_ref, base_ref, wide, active
):
    me = lax.axis_index("seq")
    section = lax.axis_index("section")
    upper = me >> 2
    gain = gain_ref[...][None, :]
    spread_columns(wide, skip_ref)
    even = take_rows(wide, 0, 64)
    odd = take_rows(wide, 1, 64)
    projected = own_ref[...].astype(jnp.float32) + other_ref[...].astype(jnp.float32)

    def rounded(values_in):
        return values_in.astype(jnp.bfloat16).astype(jnp.float32)

    attended = rounded(jnp.maximum(even, odd) + projected[0:64])
    even = rounded(attended + even)
    odd = rounded(attended + odd)
    put_rows(wide, 0, even)
    put_rows(wide, 1, odd)
    put_rows(active, 8, gelu(normalize(even, gain)))
    put_rows(active, 9, gelu(normalize(odd, gain)))
    edges = edge_ref[0:4, :]
    low = rounded(jnp.maximum(edges[0:1], edges[1:2]) + projected[64:65])
    high = rounded(jnp.maximum(edges[2:3], edges[3:4]) + projected[65:66])
    joined = rounded(edges + jnp.concatenate([low, low, high, high], axis=0))
    halo = gelu(normalize(joined, gain))
    above = jnp.where(me > 0, halo[0:2], 0.0)
    below = jnp.where(me < lax.axis_size("seq") - 1, halo[2:4], 0.0)
    zeros = jnp.zeros((6, 128), jnp.float32)
    for k in range(12):
        columns = slice(128 * k, 128 * k + 128)
        active[k, 0:8, :] = jnp.concatenate([zeros, above[:, columns]], axis=0)
        active[k, 136:144, :] = jnp.concatenate([below[:, columns], zeros], axis=0)
    for k in range(6):
        keep_ref[:, 128 * k : 128 * k + 128] = active[upper * 6 + k].astype(jnp.bfloat16)
    for k in range(3):
        columns = slice(128 * k, 128 * k + 128)
        send_ref[:, columns] = active[(1 - upper) * 6 + section * 3 + k].astype(jnp.bfloat16)
        base_ref[:, columns] = wide[section * 3 + k] + dec_bias_ref[columns][None, :]


def load_weight(own_ref, remote_refs, weight):
    slot = lax.axis_index("seq") & 3
    group = lax.axis_index("groups")
    for n in range(2 * KW):
        weight[(n // 2) * 8 + 2 * slot + n % 2] = own_ref[n]
    for n, ref in enumerate(remote_refs):
        block = slot ^ (n // 2 + 1)
        first = KW * (group if n % 2 == 0 else 1 - group)
        for k in range(KW):
            chunk = first + k
            weight[(chunk // 2) * 8 + 2 * block + chunk % 2] = ref[k]


def tap_weight(weight, tap, start, size):
    return weight[pl.ds(8 * tap + start, size)].reshape(size * weight.shape[1], weight.shape[2])


def shifted_sum(products):
    total = products[0][6:134]
    for tap in range(1, KW):
        total = total + products[tap][6 + tap : 134 + tap]
    return total


def own_kernel(active_ref, base_ref, w0, w1, w2, w3, w4, w5, w6, out_ref, weight):
    load_weight(w0, (w1, w2, w3, w4, w5, w6), weight)
    active = active_ref[...]
    out_ref[...] = base_ref[...] + shifted_sum(
        [
            jnp.dot(active, tap_weight(weight, t, 0, 8), preferred_element_type=jnp.float32)
            for t in range(KW)
        ]
    )


def partner_kernel(first_ref, second_ref, w0, w1, w2, w3, w4, w5, w6, out_ref, weight):
    load_weight(w0, (w1, w2, w3, w4, w5, w6), weight)
    section = lax.axis_index("section")
    first, second = first_ref[...], second_ref[...]
    active = jnp.where(
        section == 0,
        jnp.concatenate([first, second], axis=1),
        jnp.concatenate([second, first], axis=1),
    )
    out_ref[...] = shifted_sum(
        [
            jnp.dot(active, tap_weight(weight, t, 0, 8), preferred_element_type=jnp.float32)
            for t in range(KW)
        ]
    ).astype(jnp.bfloat16)


def split_body(
    skip_in, attn_gain, query_weight, kv_weight, pair_bias, out_weight, dec_gain, dec_weight, dec_bias
):
    bf16, f32 = jnp.bfloat16, jnp.float32
    skip = skip_in[0]
    rows, channels = skip.shape
    taps, depth, width = dec_weight.shape
    chunks = dec_weight.reshape(2 * taps, depth // 2, width)
    message, normed, piece = call(
        pool_kernel,
        [((MSG, 256), bf16), ((rows // 2, channels), bf16), ((taps, depth // 2, width), bf16)],
        [
            pltpu.with_memory_space_constraint(values_in, pltpu.HBM)
            for values_in in (skip, attn_gain, kv_weight, pair_bias, chunks)
        ],
        [
            pltpu.VMEM((rows, channels), bf16),
            pltpu.VMEM((channels,), f32),
            pltpu.VMEM(kv_weight.shape, bf16),
            pltpu.VMEM(pair_bias.shape, f32),
            pltpu.VMEM((channels // 128, rows, 128), f32),
            pltpu.VMEM((MSG, 256), f32),
            pltpu.SemaphoreType.DMA((5,)),
        ],
        [pl.BlockSpec(memory_space=pl.ANY)] * 5,
    )
    def joined(values_in, mask):
        count = values_in.shape[0]
        return call(
            join_kernel,
            [((2 * count,) + values_in.shape[1:], bf16)],
            [values_in, exchange(values_in, "seq", mask)],
        )[0]

    def behind(values_in, gate):
        return lax.optimization_barrier((values_in, gate))[0]

    near = joined(message[None], 2)
    side = exchange(piece, "seq", 1)
    after = exchange(behind(piece, near), "seq", 2)
    near = joined(near, 4)
    across = exchange(near, "seq", 1)
    held, side = lax.optimization_barrier((near, side))
    near_other = exchange(held, "section", 1)
    side_rest = exchange(side, "groups", 1)
    across_other = exchange(across, "section", 1)
    queries = jnp.dot(normed, query_weight, preferred_element_type=f32).astype(bf16)
    terms, edges = call(
        attention_kernel,
        [((ROWS, channels), bf16), ((8, channels), f32)],
        [queries, near, near_other, across, across_other, query_weight, attn_gain, pair_bias, out_weight],
    )
    terms, after = lax.optimization_barrier((terms, after))
    other = exchange(terms, "section", 1)
    after_rest = exchange(after, "groups", 1)
    far = exchange(after, "seq", 1)
    far_rest = exchange(behind(side_rest, terms), "seq", 2)
    keep, send, base = call(
        activate_kernel,
        [((rows + 16, channels // 2), bf16), ((rows + 16, channels // 4), bf16), ((rows, width), f32)],
        [skip, edges, terms, other, dec_gain, dec_bias],
        [pltpu.VMEM((channels // 128, rows + extra, 128), f32) for extra in (0, 16)],
    )
    first = exchange(send, "seq", 4)
    first, far, far_rest = lax.optimization_barrier((first, far, far_rest))
    second = exchange(first, "section", 1)
    weights = [chunks, side, side_rest, after, after_rest, far, far_rest]
    scratch = [pltpu.VMEM((8 * taps, depth // 2, width), bf16)]
    (own,) = call(own_kernel, [((rows, width), f32)], [keep, base] + weights, scratch)
    (partial,) = call(
        partner_kernel, [((rows, width), bf16)], [first, second] + weights, scratch
    )
    decoded = own + exchange(partial, "seq", 4).astype(f32)
    return decoded.astype(bf16)[None]


def solution(mesh):
    return jax.shard_map(
        split_body if mesh.shape["seq"] == 8 else body,
        mesh=mesh,
        in_specs=(
            P("groups", "seq", None),
            P(),
            P(None, "section"),
            P(),
            P("groups", "section", "seq", None),
            P("section", None),
            P(),
            P(None, "seq", "section"),
            P("section"),
        ),
        out_specs=P("groups", "seq", "section"),
        check_vma=False,
    )
```

```python
import math

import jax
import jax.numpy as jnp
from jax import lax
from jax.experimental import pallas as pl
from jax.experimental.pallas import tpu as pltpu
from jax.sharding import PartitionSpec as P

HEAD = 128
KW = 5
PAIR = 16


def extended(block, sides, width):
    for axis, dim in sides:
        count = lax.axis_size(axis)
        forward = [(i, i + 1) for i in range(count - 1)]
        backward = [(target, source) for source, target in forward]
        low = lax.ppermute(
            lax.slice_in_dim(block, block.shape[dim] - width, None, axis=dim), axis, forward
        )
        high = lax.ppermute(lax.slice_in_dim(block, 0, width, axis=dim), axis, backward)
        block = jnp.concatenate([low, block, high], axis=dim)
    return block


def norm_scale(values_in, gain):
    wide = values_in.astype(jnp.float32)
    return wide * lax.rsqrt(jnp.mean(wide * wide, axis=-1, keepdims=True) + 1e-06) * gain


def body(
    skip_in,
    attn_gain,
    query_weight,
    kv_weight,
    pair_bias,
    out_weight,
    dec_gain,
    dec_weight,
    dec_bias,
):
    seq_count, local_rows, channels = skip_in.shape
    half_rows = local_rows // 2
    local_heads = query_weight.shape[1] // HEAD
    logit_scale = 1.0 / math.sqrt(HEAD)
    pooled = jnp.max(skip_in.reshape(seq_count, half_rows, 2, channels), axis=2)
    normed = norm_scale(pooled, attn_gain).astype(jnp.bfloat16)
    flattened = normed.reshape(seq_count * half_rows, channels)
    query_rows = jnp.dot(flattened, query_weight, preferred_element_type=jnp.float32).astype(
        jnp.bfloat16
    )
    query_rows = query_rows.reshape(seq_count, half_rows, local_heads, HEAD)
    row_bias = jnp.repeat(pair_bias, PAIR, axis=2)
    row_bias = jnp.pad(row_bias, ((0, 0), (0, 0), (0, 0), (0, 2)))
    quarter = half_rows // 2
    own_rows = lax.dynamic_slice_in_dim(normed, lax.axis_index("section") * quarter, quarter, 1)
    key_values = jnp.dot(
        own_rows.reshape(seq_count * quarter, channels),
        kv_weight,
        preferred_element_type=jnp.float32,
    )
    key_values = key_values.astype(jnp.bfloat16).reshape(seq_count, quarter, 2 * HEAD)
    piece = lax.all_gather(key_values, ("seq", "section"), axis=1, tiled=True)
    start = jnp.int32(0)
    running_max = jnp.full((seq_count, local_heads, half_rows), -1e30, jnp.float32)
    running_sum = jnp.zeros((seq_count, local_heads, half_rows), jnp.float32)
    weighted = jnp.zeros((seq_count, local_heads, half_rows, HEAD), jnp.float32)
    piece_rows = piece.shape[1]
    block_size = min(piece_rows, 2048)
    for offset in range(0, piece_rows, block_size):
        piece_len = min(block_size, piece_rows - offset)
        sub_piece = piece[:, offset : offset + piece_len]
        key_portion = sub_piece[:, :, :HEAD]
        value_part = sub_piece[:, :, HEAD:]
        first_row = start + offset
        blocks = lax.dynamic_slice_in_dim(row_bias, first_row // PAIR, piece_len // PAIR + 2, 3)
        spread = jnp.repeat(blocks, PAIR, axis=3)
        key_bias = lax.dynamic_slice_in_dim(spread, first_row % PAIR, piece_len, 3)
        scores = (
            jnp.einsum(
                "wtzj,wgj->wztg", query_rows, key_portion, preferred_element_type=jnp.float32
            )
            * logit_scale
            + key_bias
        )
        new_max = jnp.maximum(running_max, jnp.max(scores, axis=-1))
        rescale = jnp.exp(running_max - new_max)
        exponent_scores = jnp.exp(scores - new_max[..., None])
        running_sum = running_sum * rescale + jnp.sum(exponent_scores, axis=-1)
        weighted = weighted * rescale[..., None] + jnp.einsum(
            "umrl,ult->umrt",
            exponent_scores.astype(jnp.bfloat16),
            value_part,
            preferred_element_type=jnp.float32,
        )
        running_max = new_max
    folded = (running_max, running_sum, weighted)
    running_max, running_sum, weighted = folded
    context = (weighted / running_sum[..., None]).astype(jnp.bfloat16)
    context = jnp.transpose(context, (0, 2, 1, 3)).reshape(
        seq_count * half_rows, local_heads * HEAD
    )
    partial_value = jnp.dot(context, out_weight, preferred_element_type=jnp.float32).reshape(
        seq_count, half_rows, channels
    )
    summed = lax.psum(partial_value.astype(jnp.bfloat16), "section").astype(jnp.float32)
    attended = (pooled.astype(jnp.float32) + summed).astype(jnp.bfloat16)
    joined = (
        jnp.repeat(attended, 2, axis=1).astype(jnp.float32) + skip_in.astype(jnp.float32)
    ).astype(jnp.bfloat16)
    activated = jax.nn.gelu(norm_scale(joined, dec_gain)).astype(jnp.bfloat16)
    padded = extended(activated, (("seq", 1),), KW // 2)
    out_half = dec_weight.shape[2]
    piece = lax.all_gather(dec_weight, "seq", axis=1, tiled=True)
    piece_rows = piece.shape[1]
    stacked = jnp.concatenate(
        [padded[:, tap_index : tap_index + local_rows] for tap_index in range(KW)], axis=2
    )
    stacked = stacked.reshape(seq_count * local_rows, KW * piece_rows)
    convolved = jnp.dot(
        stacked, piece.reshape(KW * piece_rows, out_half), preferred_element_type=jnp.float32
    )
    residual = lax.dynamic_slice_in_dim(joined, lax.axis_index("section") * out_half, out_half, 2)
    decoded = (
        convolved.reshape(seq_count, local_rows, out_half) + dec_bias + residual.astype(jnp.float32)
    )
    return decoded.astype(jnp.bfloat16)


ROWS = 80
MSG = 48
LIMIT = 24 * 1024 * 1024


def exchange(values_in, axis, mask):
    count = lax.axis_size(axis)
    return lax.ppermute(values_in, axis, [(i, i ^ mask) for i in range(count)])


def call(kernel, outs, args, scratch=(), spaces=None, limit=LIMIT):
    vmem = pl.BlockSpec(memory_space=pltpu.VMEM)
    return pl.pallas_call(
        kernel,
        out_shape=[jax.ShapeDtypeStruct(shape, kind) for shape, kind in outs],
        in_specs=[vmem] * len(args) if spaces is None else spaces,
        out_specs=[vmem] * len(outs),
        scratch_shapes=list(scratch),
        compiler_params=pltpu.CompilerParams(vmem_limit_bytes=limit),
    )(*args)


def split_three(wide):
    high = wide.astype(jnp.bfloat16)
    rest = wide - high.astype(jnp.float32)
    middle = rest.astype(jnp.bfloat16)
    low = (rest - middle.astype(jnp.float32)).astype(jnp.bfloat16)
    return high, middle, low


def own_bias(bias_ref):
    return jnp.concatenate([bias_ref[0, h] for h in range(4)], axis=0)


def normalize(wide, gain):
    return wide * lax.rsqrt(jnp.mean(wide * wide, axis=-1, keepdims=True) + 1e-06) * gain


def gelu(wide):
    inner = math.sqrt(2.0 / math.pi) * (wide + 0.044715 * (wide * wide * wide))
    return 0.5 * wide * (1.0 + jnp.tanh(inner))


def spread_columns(wide, values_in):
    for k in range(wide.shape[0]):
        wide[k] = values_in[:, 128 * k : 128 * k + 128].astype(jnp.float32)


def take_rows(wide, start, size):
    return jnp.concatenate(
        [wide[k, pl.ds(start, size, stride=2), :] for k in range(wide.shape[0])], axis=1
    )


def put_rows(wide, start, values_in):
    for k in range(wide.shape[0]):
        wide[k, pl.ds(start, values_in.shape[0], stride=2), :] = values_in[:, 128 * k : 128 * k + 128]


def pool_kernel(
    skip_hbm,
    gain_hbm,
    weight_hbm,
    bias_hbm,
    dec_hbm,
    message_ref,
    normed_ref,
    piece_ref,
    skip_ref,
    gain_ref,
    weight_ref,
    bias_ref,
    wide,
    lines,
    semaphores,
):
    group = lax.axis_index("groups")
    pieces = dec_hbm.shape[0] // 2
    pairs = (
        (skip_hbm, skip_ref),
        (gain_hbm, gain_ref),
        (bias_hbm, bias_ref),
        (weight_hbm, weight_ref),
        (dec_hbm.at[pl.ds(group * pieces, pieces)], piece_ref),
    )
    copies = [
        pltpu.make_async_copy(source, target, semaphores.at[n])
        for n, (source, target) in enumerate(pairs)
    ]
    for copy in copies:
        copy.start()
    for copy in copies[:3]:
        copy.wait()
    section = lax.axis_index("section")
    half = skip_ref.shape[0] // 2
    quarter = half // 2
    spread_columns(wide, skip_ref)
    pooled = jnp.maximum(take_rows(wide, 0, half), take_rows(wide, 1, half))
    normed_ref[...] = normalize(pooled, gain_ref[...][None, :]).astype(jnp.bfloat16)
    copies[3].wait()
    own = normed_ref[pl.ds(pl.multiple_of(section * quarter, 16), quarter), :]
    lines[0:quarter, :] = jnp.dot(own, weight_ref[...], preferred_element_type=jnp.float32)
    for n in range(2):
        row = section * (skip_ref.shape[0] - 2) + n
        for k in range(12):
            at = quarter + 6 * n + k // 2
            lines[at : at + 1, 128 * (k % 2) : 128 * (k % 2) + 128] = wide[k, pl.ds(row, 1), :]
    terms = [term.astype(jnp.float32) for term in split_three(own_bias(bias_ref))]
    packed = [
        jnp.concatenate(
            [term[4 * h + cell : 4 * h + cell + 1, :] for cell in (0, 3) for h in range(4)], axis=1
        )
        for term in terms
    ]
    lines[MSG - 4 : MSG, :] = jnp.concatenate(packed + [jnp.zeros((1, 256), jnp.float32)], axis=0)
    message_ref[...] = lines[...].astype(jnp.bfloat16)
    copies[4].wait()


def join_kernel(first_ref, second_ref, out_ref):
    count = first_ref.shape[0]
    out_ref[0:count] = first_ref[...]
    out_ref[count:] = second_ref[...]


def slot_of(distance):
    return distance // 2 + 4 * (distance & 1)


def distance_of(slot):
    return 2 * (slot & 3) + slot // 4


def attention_kernel(
    query_ref,
    near_ref,
    near_other_ref,
    side_ref,
    side_other_ref,
    query_weight_ref,
    gain_ref,
    bias_ref,
    out_weight_ref,
    terms_ref,
    edge_ref,
):
    me = lax.axis_index("seq")
    section = lax.axis_index("section")
    count = lax.axis_size("seq")
    low_slot = slot_of(me ^ jnp.maximum(me - 1, 0))
    high_slot = slot_of(me ^ jnp.minimum(me + 1, count - 1))

    def block_of(slot, near, side):
        return jnp.where(
            slot < 4, near[slot & 3].astype(jnp.float32), side[slot & 3].astype(jnp.float32)
        )

    low, high = (block_of(slot, near_ref, side_ref) for slot in (low_slot, high_slot))
    low_edge = jnp.where(section == 1, low, block_of(low_slot, near_other_ref, side_other_ref))
    high_edge = jnp.where(section == 0, high, block_of(high_slot, near_other_ref, side_other_ref))

    def line(block, row):
        start = 32 + 6 * row
        return jnp.concatenate([block[start + k : start + k + 1, :] for k in range(6)], axis=1)

    edges = jnp.concatenate(
        [line(low_edge, 0), line(low_edge, 1), line(high_edge, 0), line(high_edge, 1)], axis=0
    )
    edge_ref[0:4, :] = edges
    edge_ref[4:8, :] = jnp.zeros_like(edges)
    pooled = jnp.concatenate(
        [
            jnp.maximum(edges[0:1], edges[1:2]),
            jnp.maximum(edges[2:3], edges[3:4]),
            jnp.zeros((14, edges.shape[1]), jnp.float32),
        ],
        axis=0,
    )
    normed = normalize(pooled, gain_ref[...][None, :]).astype(jnp.bfloat16)
    halo_query = jnp.dot(normed, query_weight_ref[...], preferred_element_type=jnp.float32)
    queries = jnp.concatenate([query_ref[...], halo_query.astype(jnp.bfloat16)], axis=0)
    pieces = []
    for mine, others in ((near_ref, near_other_ref), (side_ref, side_other_ref)):
        for k in range(4):
            pieces += [mine[k, 0:32, :], others[k, 0:32, :]]
    keys = jnp.concatenate([piece[:, 0:HEAD] for piece in pieces], axis=0)
    values = jnp.concatenate([piece[:, HEAD : 2 * HEAD] for piece in pieces], axis=0)
    cell = lax.broadcasted_iota(jnp.int32, (32, 512), 0)
    column = lax.broadcasted_iota(jnp.int32, (32, 512), 1)
    inner = 2 * (((column >> 5) & 1) ^ section) + ((column & 31) >> 4)
    wanted = 4 * (distance_of(column >> 6) ^ me) + inner
    spread = jnp.where(cell == wanted, 1.0, 0.0).astype(jnp.bfloat16)
    bias = jnp.zeros((24, 512), jnp.float32)
    for n, term in enumerate(split_three(own_bias(bias_ref))):
        at = MSG - 4 + n
        rows = [low[at : at + 1, 128 + 32 * h : 160 + 32 * h] for h in range(4)]
        rows += [high[at : at + 1, 32 * h : 32 * h + 32] for h in range(4)]
        table = jnp.concatenate([term.astype(jnp.float32)] + rows, axis=0).astype(jnp.bfloat16)
        bias = bias + jnp.dot(table, spread, preferred_element_type=jnp.float32)
    first = lax.broadcasted_iota(jnp.int32, (16, 512), 0) == 0
    parts = []
    for h in range(4):
        scores = lax.dot_general(
            queries[:, h * HEAD : (h + 1) * HEAD],
            keys,
            (((1,), (1,)), ((), ())),
            preferred_element_type=jnp.float32,
        )
        rows = [jnp.broadcast_to(bias[4 * h + r : 4 * h + r + 1, :], (16, 512)) for r in range(4)]
        rows.append(
            jnp.where(first, bias[16 + h : 17 + h, :], bias[20 + h : 21 + h, :])
        )
        scores = scores * (1.0 / math.sqrt(HEAD)) + jnp.concatenate(rows, axis=0)
        exps = jnp.exp(scores - jnp.max(scores, axis=-1, keepdims=True))
        totals = jnp.sum(exps, axis=-1, keepdims=True)
        mixed = jnp.dot(exps.astype(jnp.bfloat16), values, preferred_element_type=jnp.float32)
        parts.append((mixed / totals).astype(jnp.bfloat16))
    context = jnp.concatenate(parts, axis=1)
    terms_ref[...] = jnp.dot(
        context, out_weight_ref[...], preferred_element_type=jnp.float32
    ).astype(jnp.bfloat16)


def activate_kernel(
    skip_ref, edge_ref, own_ref, other_ref, gain_ref, dec_bias_ref, keep_ref, send_ref, base_ref, wide, active
):
    me = lax.axis_index("seq")
    section = lax.axis_index("section")
    upper = me >> 2
    gain = gain_ref[...][None, :]
    spread_columns(wide, skip_ref)
    even = take_rows(wide, 0, 64)
    odd = take_rows(wide, 1, 64)
    projected = own_ref[...].astype(jnp.float32) + other_ref[...].astype(jnp.float32)

    def rounded(values_in):
        return values_in.astype(jnp.bfloat16).astype(jnp.float32)

    attended = rounded(jnp.maximum(even, odd) + projected[0:64])
    even = rounded(attended + even)
    odd = rounded(attended + odd)
    put_rows(wide, 0, even)
    put_rows(wide, 1, odd)
    put_rows(active, 2, gelu(normalize(even, gain)))
    put_rows(active, 3, gelu(normalize(odd, gain)))
    edges = edge_ref[0:4, :]
    low = rounded(jnp.maximum(edges[0:1], edges[1:2]) + projected[64:65])
    high = rounded(jnp.maximum(edges[2:3], edges[3:4]) + projected[65:66])
    joined = rounded(edges + jnp.concatenate([low, low, high, high], axis=0))
    halo = gelu(normalize(joined, gain))
    above = jnp.where(me > 0, halo[0:2], 0.0)
    below = jnp.where(me < lax.axis_size("seq") - 1, halo[2:4], 0.0)
    zeros = jnp.zeros((4, 128), jnp.float32)
    for k in range(12):
        columns = slice(128 * k, 128 * k + 128)
        active[k, 0:2, :] = above[:, columns]
        active[k, 130:136, :] = jnp.concatenate([below[:, columns], zeros], axis=0)
    for k in range(6):
        keep_ref[:, 128 * k : 128 * k + 128] = active[upper * 6 + k].astype(jnp.bfloat16)
    for k in range(3):
        columns = slice(128 * k, 128 * k + 128)
        send_ref[:, columns] = active[(1 - upper) * 6 + section * 3 + k].astype(jnp.bfloat16)
        base_ref[:, columns] = wide[section * 3 + k] + dec_bias_ref[columns][None, :]


def load_weight(own_ref, remote_refs, weight):
    slot = lax.axis_index("seq") & 3
    group = lax.axis_index("groups")
    for n in range(2 * KW):
        weight[(n // 2) * 8 + 2 * slot + n % 2] = own_ref[n]
    for n, ref in enumerate(remote_refs):
        block = slot ^ (n // 2 + 1)
        first = KW * (group if n % 2 == 0 else 1 - group)
        for k in range(KW):
            chunk = first + k
            weight[(chunk // 2) * 8 + 2 * block + chunk % 2] = ref[k]


def tap_weight(weight, tap, start, size):
    return weight[pl.ds(8 * tap + start, size)].reshape(size * weight.shape[1], weight.shape[2])


def shifted_sum(products):
    total = products[0][0:128]
    for tap in range(1, KW):
        total = total + products[tap][tap : 128 + tap]
    return total


def own_kernel(active_ref, base_ref, w0, w1, w2, w3, w4, w5, w6, out_ref, weight):
    load_weight(w0, (w1, w2, w3, w4, w5, w6), weight)
    active = active_ref[...]
    out_ref[...] = base_ref[...] + shifted_sum(
        [
            jnp.dot(active, tap_weight(weight, t, 0, 8), preferred_element_type=jnp.float32)
            for t in range(KW)
        ]
    )


def partner_kernel(first_ref, second_ref, w0, w1, w2, w3, w4, w5, w6, out_ref, weight):
    load_weight(w0, (w1, w2, w3, w4, w5, w6), weight)
    section = lax.axis_index("section")
    first, second = first_ref[...], second_ref[...]
    active = jnp.where(
        section == 0,
        jnp.concatenate([first, second], axis=1),
        jnp.concatenate([second, first], axis=1),
    )
    out_ref[...] = shifted_sum(
        [
            jnp.dot(active, tap_weight(weight, t, 0, 8), preferred_element_type=jnp.float32)
            for t in range(KW)
        ]
    ).astype(jnp.bfloat16)


def split_body(
    skip_in, attn_gain, query_weight, kv_weight, pair_bias, out_weight, dec_gain, dec_weight, dec_bias
):
    bf16, f32 = jnp.bfloat16, jnp.float32
    skip = skip_in[0]
    rows, channels = skip.shape
    taps, depth, width = dec_weight.shape
    chunks = dec_weight.reshape(2 * taps, depth // 2, width)
    message, normed, piece = call(
        pool_kernel,
        [((MSG, 256), bf16), ((rows // 2, channels), bf16), ((taps, depth // 2, width), bf16)],
        [
            pltpu.with_memory_space_constraint(values_in, pltpu.HBM)
            for values_in in (skip, attn_gain, kv_weight, pair_bias, chunks)
        ],
        [
            pltpu.VMEM((rows, channels), bf16),
            pltpu.VMEM((channels,), f32),
            pltpu.VMEM(kv_weight.shape, bf16),
            pltpu.VMEM(pair_bias.shape, f32),
            pltpu.VMEM((channels // 128, rows, 128), f32),
            pltpu.VMEM((MSG, 256), f32),
            pltpu.SemaphoreType.DMA((5,)),
        ],
        [pl.BlockSpec(memory_space=pl.ANY)] * 5,
    )
    def joined(values_in, mask):
        count = values_in.shape[0]
        return call(
            join_kernel,
            [((2 * count,) + values_in.shape[1:], bf16)],
            [values_in, exchange(values_in, "seq", mask)],
        )[0]

    def behind(values_in, gate):
        return lax.optimization_barrier((values_in, gate))[0]

    near = joined(message[None], 2)
    side = exchange(piece, "seq", 1)
    after = exchange(behind(piece, near), "seq", 2)
    near = joined(near, 4)
    across = exchange(near, "seq", 1)
    held, side = lax.optimization_barrier((near, side))
    near_other = exchange(held, "section", 1)
    side_rest = exchange(side, "groups", 1)
    across_other = exchange(across, "section", 1)
    queries = jnp.dot(normed, query_weight, preferred_element_type=f32).astype(bf16)
    terms, edges = call(
        attention_kernel,
        [((ROWS, channels), bf16), ((8, channels), f32)],
        [queries, near, near_other, across, across_other, query_weight, attn_gain, pair_bias, out_weight],
    )
    terms, after = lax.optimization_barrier((terms, after))
    other = exchange(terms, "section", 1)
    after_rest = exchange(after, "groups", 1)
    far = exchange(after, "seq", 1)
    far_rest = exchange(behind(side_rest, terms), "seq", 2)
    keep, send, base = call(
        activate_kernel,
        [((rows + 8, channels // 2), bf16), ((rows + 8, channels // 4), bf16), ((rows, width), f32)],
        [skip, edges, terms, other, dec_gain, dec_bias],
        [pltpu.VMEM((channels // 128, rows + extra, 128), f32) for extra in (0, 8)],
    )
    first = exchange(send, "seq", 4)
    first, far, far_rest = lax.optimization_barrier((first, far, far_rest))
    second = exchange(first, "section", 1)
    weights = [chunks, side, side_rest, after, after_rest, far, far_rest]
    scratch = [pltpu.VMEM((8 * taps, depth // 2, width), bf16)]
    (own,) = call(own_kernel, [((rows, width), f32)], [keep, base] + weights, scratch)
    (partial,) = call(
        partner_kernel, [((rows, width), bf16)], [first, second] + weights, scratch
    )
    decoded = own + exchange(partial, "seq", 4).astype(f32)
    return decoded.astype(bf16)[None]


def solution(mesh):
    return jax.shard_map(
        split_body if mesh.shape["seq"] == 8 else body,
        mesh=mesh,
        in_specs=(
            P("groups", "seq", None),
            P(),
            P(None, "section"),
            P(),
            P("groups", "section", "seq", None),
            P("section", None),
            P(),
            P(None, "seq", "section"),
            P("section"),
        ),
        out_specs=P("groups", "seq", "section"),
        check_vma=False,
    )
```

```python
import math

import jax
import jax.numpy as jnp
from jax import lax
from jax.experimental import pallas as pl
from jax.experimental.pallas import tpu as pltpu
from jax.sharding import PartitionSpec as P

HEAD = 128
KW = 5
PAIR = 16


def extended(block, sides, width):
    for axis, dim in sides:
        count = lax.axis_size(axis)
        forward = [(i, i + 1) for i in range(count - 1)]
        backward = [(target, source) for source, target in forward]
        low = lax.ppermute(
            lax.slice_in_dim(block, block.shape[dim] - width, None, axis=dim), axis, forward
        )
        high = lax.ppermute(lax.slice_in_dim(block, 0, width, axis=dim), axis, backward)
        block = jnp.concatenate([low, block, high], axis=dim)
    return block


def norm_scale(values_in, gain):
    wide = values_in.astype(jnp.float32)
    return wide * lax.rsqrt(jnp.mean(wide * wide, axis=-1, keepdims=True) + 1e-06) * gain


def body(
    skip_in,
    attn_gain,
    query_weight,
    kv_weight,
    pair_bias,
    out_weight,
    dec_gain,
    dec_weight,
    dec_bias,
):
    seq_count, local_rows, channels = skip_in.shape
    half_rows = local_rows // 2
    local_heads = query_weight.shape[1] // HEAD
    logit_scale = 1.0 / math.sqrt(HEAD)
    pooled = jnp.max(skip_in.reshape(seq_count, half_rows, 2, channels), axis=2)
    normed = norm_scale(pooled, attn_gain).astype(jnp.bfloat16)
    flattened = normed.reshape(seq_count * half_rows, channels)
    query_rows = jnp.dot(flattened, query_weight, preferred_element_type=jnp.float32).astype(
        jnp.bfloat16
    )
    query_rows = query_rows.reshape(seq_count, half_rows, local_heads, HEAD)
    row_bias = jnp.repeat(pair_bias, PAIR, axis=2)
    row_bias = jnp.pad(row_bias, ((0, 0), (0, 0), (0, 0), (0, 2)))
    quarter = half_rows // 2
    own_rows = lax.dynamic_slice_in_dim(normed, lax.axis_index("section") * quarter, quarter, 1)
    key_values = jnp.dot(
        own_rows.reshape(seq_count * quarter, channels),
        kv_weight,
        preferred_element_type=jnp.float32,
    )
    key_values = key_values.astype(jnp.bfloat16).reshape(seq_count, quarter, 2 * HEAD)
    piece = lax.all_gather(key_values, ("seq", "section"), axis=1, tiled=True)
    start = jnp.int32(0)
    running_max = jnp.full((seq_count, local_heads, half_rows), -1e30, jnp.float32)
    running_sum = jnp.zeros((seq_count, local_heads, half_rows), jnp.float32)
    weighted = jnp.zeros((seq_count, local_heads, half_rows, HEAD), jnp.float32)
    piece_rows = piece.shape[1]
    block_size = min(piece_rows, 2048)
    for offset in range(0, piece_rows, block_size):
        piece_len = min(block_size, piece_rows - offset)
        sub_piece = piece[:, offset : offset + piece_len]
        key_portion = sub_piece[:, :, :HEAD]
        value_part = sub_piece[:, :, HEAD:]
        first_row = start + offset
        blocks = lax.dynamic_slice_in_dim(row_bias, first_row // PAIR, piece_len // PAIR + 2, 3)
        spread = jnp.repeat(blocks, PAIR, axis=3)
        key_bias = lax.dynamic_slice_in_dim(spread, first_row % PAIR, piece_len, 3)
        scores = (
            jnp.einsum(
                "wtzj,wgj->wztg", query_rows, key_portion, preferred_element_type=jnp.float32
            )
            * logit_scale
            + key_bias
        )
        new_max = jnp.maximum(running_max, jnp.max(scores, axis=-1))
        rescale = jnp.exp(running_max - new_max)
        exponent_scores = jnp.exp(scores - new_max[..., None])
        running_sum = running_sum * rescale + jnp.sum(exponent_scores, axis=-1)
        weighted = weighted * rescale[..., None] + jnp.einsum(
            "umrl,ult->umrt",
            exponent_scores.astype(jnp.bfloat16),
            value_part,
            preferred_element_type=jnp.float32,
        )
        running_max = new_max
    folded = (running_max, running_sum, weighted)
    running_max, running_sum, weighted = folded
    context = (weighted / running_sum[..., None]).astype(jnp.bfloat16)
    context = jnp.transpose(context, (0, 2, 1, 3)).reshape(
        seq_count * half_rows, local_heads * HEAD
    )
    partial_value = jnp.dot(context, out_weight, preferred_element_type=jnp.float32).reshape(
        seq_count, half_rows, channels
    )
    summed = lax.psum(partial_value.astype(jnp.bfloat16), "section").astype(jnp.float32)
    attended = (pooled.astype(jnp.float32) + summed).astype(jnp.bfloat16)
    joined = (
        jnp.repeat(attended, 2, axis=1).astype(jnp.float32) + skip_in.astype(jnp.float32)
    ).astype(jnp.bfloat16)
    activated = jax.nn.gelu(norm_scale(joined, dec_gain)).astype(jnp.bfloat16)
    padded = extended(activated, (("seq", 1),), KW // 2)
    out_half = dec_weight.shape[2]
    piece = lax.all_gather(dec_weight, "seq", axis=1, tiled=True)
    piece_rows = piece.shape[1]
    stacked = jnp.concatenate(
        [padded[:, tap_index : tap_index + local_rows] for tap_index in range(KW)], axis=2
    )
    stacked = stacked.reshape(seq_count * local_rows, KW * piece_rows)
    convolved = jnp.dot(
        stacked, piece.reshape(KW * piece_rows, out_half), preferred_element_type=jnp.float32
    )
    residual = lax.dynamic_slice_in_dim(joined, lax.axis_index("section") * out_half, out_half, 2)
    decoded = (
        convolved.reshape(seq_count, local_rows, out_half) + dec_bias + residual.astype(jnp.float32)
    )
    return decoded.astype(jnp.bfloat16)


ROWS = 80
MSG = 48
LIMIT = 24 * 1024 * 1024


def exchange(values_in, axis, mask):
    count = lax.axis_size(axis)
    return lax.ppermute(values_in, axis, [(i, i ^ mask) for i in range(count)])


def call(kernel, outs, args, scratch=(), spaces=None, limit=LIMIT):
    vmem = pl.BlockSpec(memory_space=pltpu.VMEM)
    return pl.pallas_call(
        kernel,
        out_shape=[jax.ShapeDtypeStruct(shape, kind) for shape, kind in outs],
        in_specs=[vmem] * len(args) if spaces is None else spaces,
        out_specs=[vmem] * len(outs),
        scratch_shapes=list(scratch),
        compiler_params=pltpu.CompilerParams(vmem_limit_bytes=limit),
    )(*args)


def split_three(wide):
    high = wide.astype(jnp.bfloat16)
    rest = wide - high.astype(jnp.float32)
    middle = rest.astype(jnp.bfloat16)
    low = (rest - middle.astype(jnp.float32)).astype(jnp.bfloat16)
    return high, middle, low


def own_bias(bias_ref):
    return jnp.concatenate([bias_ref[0, h] for h in range(4)], axis=0)


def normalize(wide, gain):
    return wide * lax.rsqrt(jnp.mean(wide * wide, axis=-1, keepdims=True) + 1e-06) * gain


def gelu(wide):
    inner = math.sqrt(2.0 / math.pi) * (wide + 0.044715 * (wide * wide * wide))
    return 0.5 * wide * (1.0 + jnp.tanh(inner))


def spread_columns(wide, values_in):
    for k in range(wide.shape[0]):
        wide[k] = values_in[:, 128 * k : 128 * k + 128].astype(jnp.float32)


def take_rows(wide, start, size):
    return jnp.concatenate(
        [wide[k, pl.ds(start, size, stride=2), :] for k in range(wide.shape[0])], axis=1
    )


def put_rows(wide, start, values_in):
    for k in range(wide.shape[0]):
        wide[k, pl.ds(start, values_in.shape[0], stride=2), :] = values_in[:, 128 * k : 128 * k + 128]


def pool_kernel(
    skip_hbm,
    gain_hbm,
    weight_hbm,
    bias_hbm,
    dec_hbm,
    message_ref,
    normed_ref,
    piece_ref,
    skip_ref,
    gain_ref,
    weight_ref,
    bias_ref,
    wide,
    lines,
    semaphores,
):
    group = lax.axis_index("groups")
    pieces = dec_hbm.shape[0] // 2
    pairs = (
        (skip_hbm, skip_ref),
        (gain_hbm, gain_ref),
        (bias_hbm, bias_ref),
        (weight_hbm, weight_ref),
        (dec_hbm.at[pl.ds(group * pieces, pieces)], piece_ref),
    )
    copies = [
        pltpu.make_async_copy(source, target, semaphores.at[n])
        for n, (source, target) in enumerate(pairs)
    ]
    for copy in copies:
        copy.start()
    for copy in copies[:3]:
        copy.wait()
    section = lax.axis_index("section")
    half = skip_ref.shape[0] // 2
    quarter = half // 2
    spread_columns(wide, skip_ref)
    pooled = jnp.maximum(take_rows(wide, 0, half), take_rows(wide, 1, half))
    normed_ref[...] = normalize(pooled, gain_ref[...][None, :]).astype(jnp.bfloat16)
    copies[3].wait()
    own = normed_ref[pl.ds(pl.multiple_of(section * quarter, 16), quarter), :]
    lines[0:quarter, :] = jnp.dot(own, weight_ref[...], preferred_element_type=jnp.float32)
    for n in range(2):
        row = section * (skip_ref.shape[0] - 2) + n
        for k in range(12):
            at = quarter + 6 * n + k // 2
            lines[at : at + 1, 128 * (k % 2) : 128 * (k % 2) + 128] = wide[k, pl.ds(row, 1), :]
    terms = [term.astype(jnp.float32) for term in split_three(own_bias(bias_ref))]
    packed = [
        jnp.concatenate(
            [term[4 * h + cell : 4 * h + cell + 1, :] for cell in (0, 3) for h in range(4)], axis=1
        )
        for term in terms
    ]
    lines[MSG - 4 : MSG, :] = jnp.concatenate(packed + [jnp.zeros((1, 256), jnp.float32)], axis=0)
    message_ref[...] = lines[...].astype(jnp.bfloat16)
    copies[4].wait()


def join_kernel(first_ref, second_ref, out_ref):
    count = first_ref.shape[0]
    out_ref[0:count] = first_ref[...]
    out_ref[count:] = second_ref[...]


def add_kernel(own_ref, partial_ref, out_ref):
    out_ref[...] = (own_ref[...] + partial_ref[...].astype(jnp.float32)).astype(jnp.bfloat16)


def slot_of(distance):
    return distance // 2 + 4 * (distance & 1)


def distance_of(slot):
    return 2 * (slot & 3) + slot // 4


def attention_kernel(
    query_ref,
    near_ref,
    near_other_ref,
    side_ref,
    side_other_ref,
    query_weight_ref,
    gain_ref,
    bias_ref,
    out_weight_ref,
    terms_ref,
    edge_ref,
):
    me = lax.axis_index("seq")
    section = lax.axis_index("section")
    count = lax.axis_size("seq")
    low_slot = slot_of(me ^ jnp.maximum(me - 1, 0))
    high_slot = slot_of(me ^ jnp.minimum(me + 1, count - 1))

    def block_of(slot, near, side):
        return jnp.where(
            slot < 4, near[slot & 3].astype(jnp.float32), side[slot & 3].astype(jnp.float32)
        )

    low, high = (block_of(slot, near_ref, side_ref) for slot in (low_slot, high_slot))
    low_edge = jnp.where(section == 1, low, block_of(low_slot, near_other_ref, side_other_ref))
    high_edge = jnp.where(section == 0, high, block_of(high_slot, near_other_ref, side_other_ref))

    def line(block, row):
        start = 32 + 6 * row
        return jnp.concatenate([block[start + k : start + k + 1, :] for k in range(6)], axis=1)

    edges = jnp.concatenate(
        [line(low_edge, 0), line(low_edge, 1), line(high_edge, 0), line(high_edge, 1)], axis=0
    )
    edge_ref[0:4, :] = edges
    edge_ref[4:8, :] = jnp.zeros_like(edges)
    pooled = jnp.concatenate(
        [
            jnp.maximum(edges[0:1], edges[1:2]),
            jnp.maximum(edges[2:3], edges[3:4]),
            jnp.zeros((14, edges.shape[1]), jnp.float32),
        ],
        axis=0,
    )
    normed = normalize(pooled, gain_ref[...][None, :]).astype(jnp.bfloat16)
    halo_query = jnp.dot(normed, query_weight_ref[...], preferred_element_type=jnp.float32)
    queries = jnp.concatenate([query_ref[...], halo_query.astype(jnp.bfloat16)], axis=0)
    pieces = []
    for mine, others in ((near_ref, near_other_ref), (side_ref, side_other_ref)):
        for k in range(4):
            pieces += [mine[k, 0:32, :], others[k, 0:32, :]]
    keys = jnp.concatenate([piece[:, 0:HEAD] for piece in pieces], axis=0)
    values = jnp.concatenate([piece[:, HEAD : 2 * HEAD] for piece in pieces], axis=0)
    cell = lax.broadcasted_iota(jnp.int32, (32, 512), 0)
    column = lax.broadcasted_iota(jnp.int32, (32, 512), 1)
    inner = 2 * (((column >> 5) & 1) ^ section) + ((column & 31) >> 4)
    wanted = 4 * (distance_of(column >> 6) ^ me) + inner
    spread = jnp.where(cell == wanted, 1.0, 0.0).astype(jnp.bfloat16)
    bias = jnp.zeros((24, 512), jnp.float32)
    for n, term in enumerate(split_three(own_bias(bias_ref))):
        at = MSG - 4 + n
        rows = [low[at : at + 1, 128 + 32 * h : 160 + 32 * h] for h in range(4)]
        rows += [high[at : at + 1, 32 * h : 32 * h + 32] for h in range(4)]
        table = jnp.concatenate([term.astype(jnp.float32)] + rows, axis=0).astype(jnp.bfloat16)
        bias = bias + jnp.dot(table, spread, preferred_element_type=jnp.float32)
    first = lax.broadcasted_iota(jnp.int32, (16, 512), 0) == 0
    parts = []
    for h in range(4):
        scores = lax.dot_general(
            queries[:, h * HEAD : (h + 1) * HEAD],
            keys,
            (((1,), (1,)), ((), ())),
            preferred_element_type=jnp.float32,
        )
        rows = [jnp.broadcast_to(bias[4 * h + r : 4 * h + r + 1, :], (16, 512)) for r in range(4)]
        rows.append(
            jnp.where(first, bias[16 + h : 17 + h, :], bias[20 + h : 21 + h, :])
        )
        scores = scores * (1.0 / math.sqrt(HEAD)) + jnp.concatenate(rows, axis=0)
        exps = jnp.exp(scores - jnp.max(scores, axis=-1, keepdims=True))
        totals = jnp.sum(exps, axis=-1, keepdims=True)
        mixed = jnp.dot(exps.astype(jnp.bfloat16), values, preferred_element_type=jnp.float32)
        parts.append((mixed / totals).astype(jnp.bfloat16))
    context = jnp.concatenate(parts, axis=1)
    terms_ref[...] = jnp.dot(
        context, out_weight_ref[...], preferred_element_type=jnp.float32
    ).astype(jnp.bfloat16)


def activate_kernel(
    skip_ref, edge_ref, own_ref, other_ref, gain_ref, dec_bias_ref, keep_ref, send_ref, base_ref, wide, active
):
    me = lax.axis_index("seq")
    section = lax.axis_index("section")
    upper = me >> 2
    gain = gain_ref[...][None, :]
    spread_columns(wide, skip_ref)
    even = take_rows(wide, 0, 64)
    odd = take_rows(wide, 1, 64)
    projected = own_ref[...].astype(jnp.float32) + other_ref[...].astype(jnp.float32)

    def rounded(values_in):
        return values_in.astype(jnp.bfloat16).astype(jnp.float32)

    attended = rounded(jnp.maximum(even, odd) + projected[0:64])
    even = rounded(attended + even)
    odd = rounded(attended + odd)
    put_rows(wide, 0, even)
    put_rows(wide, 1, odd)
    put_rows(active, 8, gelu(normalize(even, gain)))
    put_rows(active, 9, gelu(normalize(odd, gain)))
    edges = edge_ref[0:4, :]
    low = rounded(jnp.maximum(edges[0:1], edges[1:2]) + projected[64:65])
    high = rounded(jnp.maximum(edges[2:3], edges[3:4]) + projected[65:66])
    joined = rounded(edges + jnp.concatenate([low, low, high, high], axis=0))
    halo = gelu(normalize(joined, gain))
    above = jnp.where(me > 0, halo[0:2], 0.0)
    below = jnp.where(me < lax.axis_size("seq") - 1, halo[2:4], 0.0)
    zeros = jnp.zeros((6, 128), jnp.float32)
    for k in range(12):
        columns = slice(128 * k, 128 * k + 128)
        active[k, 0:8, :] = jnp.concatenate([zeros, above[:, columns]], axis=0)
        active[k, 136:144, :] = jnp.concatenate([below[:, columns], zeros], axis=0)
    for k in range(6):
        keep_ref[:, 128 * k : 128 * k + 128] = active[upper * 6 + k].astype(jnp.bfloat16)
    for k in range(3):
        columns = slice(128 * k, 128 * k + 128)
        send_ref[:, columns] = active[(1 - upper) * 6 + section * 3 + k].astype(jnp.bfloat16)
        base_ref[:, columns] = wide[section * 3 + k] + dec_bias_ref[columns][None, :]


def load_weight(own_ref, remote_refs, weight):
    slot = lax.axis_index("seq") & 3
    group = lax.axis_index("groups")
    for n in range(2 * KW):
        weight[(n // 2) * 8 + 2 * slot + n % 2] = own_ref[n]
    for n, ref in enumerate(remote_refs):
        block = slot ^ (n // 2 + 1)
        first = KW * (group if n % 2 == 0 else 1 - group)
        for k in range(KW):
            chunk = first + k
            weight[(chunk // 2) * 8 + 2 * block + chunk % 2] = ref[k]


def tap_weight(weight, tap, start, size):
    return weight[pl.ds(8 * tap + start, size)].reshape(size * weight.shape[1], weight.shape[2])


def shifted_sum(products):
    total = products[0][6:134]
    for tap in range(1, KW):
        total = total + products[tap][6 + tap : 134 + tap]
    return total


def own_kernel(active_ref, base_ref, w0, w1, w2, w3, w4, w5, w6, out_ref, weight):
    load_weight(w0, (w1, w2, w3, w4, w5, w6), weight)
    active = active_ref[...]
    out_ref[...] = base_ref[...] + shifted_sum(
        [
            jnp.dot(active, tap_weight(weight, t, 0, 8), preferred_element_type=jnp.float32)
            for t in range(KW)
        ]
    )


def partner_kernel(first_ref, second_ref, w0, w1, w2, w3, w4, w5, w6, out_ref, weight):
    load_weight(w0, (w1, w2, w3, w4, w5, w6), weight)
    section = lax.axis_index("section")
    first, second = first_ref[...], second_ref[...]
    active = jnp.where(
        section == 0,
        jnp.concatenate([first, second], axis=1),
        jnp.concatenate([second, first], axis=1),
    )
    out_ref[...] = shifted_sum(
        [
            jnp.dot(active, tap_weight(weight, t, 0, 8), preferred_element_type=jnp.float32)
            for t in range(KW)
        ]
    ).astype(jnp.bfloat16)


def split_body(
    skip_in, attn_gain, query_weight, kv_weight, pair_bias, out_weight, dec_gain, dec_weight, dec_bias
):
    bf16, f32 = jnp.bfloat16, jnp.float32
    skip = skip_in[0]
    rows, channels = skip.shape
    taps, depth, width = dec_weight.shape
    chunks = dec_weight.reshape(2 * taps, depth // 2, width)
    message, normed, piece = call(
        pool_kernel,
        [((MSG, 256), bf16), ((rows // 2, channels), bf16), ((taps, depth // 2, width), bf16)],
        [
            pltpu.with_memory_space_constraint(values_in, pltpu.HBM)
            for values_in in (skip, attn_gain, kv_weight, pair_bias, chunks)
        ],
        [
            pltpu.VMEM((rows, channels), bf16),
            pltpu.VMEM((channels,), f32),
            pltpu.VMEM(kv_weight.shape, bf16),
            pltpu.VMEM(pair_bias.shape, f32),
            pltpu.VMEM((channels // 128, rows, 128), f32),
            pltpu.VMEM((MSG, 256), f32),
            pltpu.SemaphoreType.DMA((5,)),
        ],
        [pl.BlockSpec(memory_space=pl.ANY)] * 5,
    )
    def joined(values_in, mask):
        count = values_in.shape[0]
        return call(
            join_kernel,
            [((2 * count,) + values_in.shape[1:], bf16)],
            [values_in, exchange(values_in, "seq", mask)],
        )[0]

    def behind(values_in, gate):
        return lax.optimization_barrier((values_in, gate))[0]

    near = joined(message[None], 2)
    side = exchange(piece, "seq", 1)
    after = exchange(behind(piece, near), "seq", 2)
    near = joined(near, 4)
    across = exchange(near, "seq", 1)
    held, side = lax.optimization_barrier((near, side))
    near_other = exchange(held, "section", 1)
    side_rest = exchange(side, "groups", 1)
    across_other = exchange(across, "section", 1)
    queries = jnp.dot(normed, query_weight, preferred_element_type=f32).astype(bf16)
    terms, edges = call(
        attention_kernel,
        [((ROWS, channels), bf16), ((8, channels), f32)],
        [queries, near, near_other, across, across_other, query_weight, attn_gain, pair_bias, out_weight],
    )
    terms, after = lax.optimization_barrier((terms, after))
    other = exchange(terms, "section", 1)
    after_rest = exchange(after, "groups", 1)
    far = exchange(after, "seq", 1)
    far_rest = exchange(behind(side_rest, terms), "seq", 2)
    keep, send, base = call(
        activate_kernel,
        [((rows + 16, channels // 2), bf16), ((rows + 16, channels // 4), bf16), ((rows, width), f32)],
        [skip, edges, terms, other, dec_gain, dec_bias],
        [pltpu.VMEM((channels // 128, rows + extra, 128), f32) for extra in (0, 16)],
    )
    first = exchange(send, "seq", 4)
    first, far, far_rest = lax.optimization_barrier((first, far, far_rest))
    second = exchange(first, "section", 1)
    weights = [chunks, side, side_rest, after, after_rest, far, far_rest]
    scratch = [pltpu.VMEM((8 * taps, depth // 2, width), bf16)]
    (own,) = call(own_kernel, [((rows, width), f32)], [keep, base] + weights, scratch)
    (partial,) = call(
        partner_kernel, [((rows, width), bf16)], [first, second] + weights, scratch
    )
    (decoded,) = call(add_kernel, [((rows, width), bf16)], [own, exchange(partial, "seq", 4)])
    return decoded[None]


def solution(mesh):
    return jax.shard_map(
        split_body if mesh.shape["seq"] == 8 else body,
        mesh=mesh,
        in_specs=(
            P("groups", "seq", None),
            P(),
            P(None, "section"),
            P(),
            P("groups", "section", "seq", None),
            P("section", None),
            P(),
            P(None, "seq", "section"),
            P("section"),
        ),
        out_specs=P("groups", "seq", "section"),
        check_vma=False,
    )
```
